256 devices in a mesh: lat: 8 (over y, x_hi), lon: 32 (over z, x_lo, core).
Axes of the slice: x: 4 (x_hi: 2, x_lo: 2; x = x_hi * 2 + x_lo), y: 4, z: 8, core: 2. Of those that a mesh axis runs over, the one named last changes fastest.
Arguments:
- hi_res: bfloat16 [384, 768, 256], P('lat', 'lon'), may hold values from -6 to 6
- low_res: bfloat16 [128, 256, 256], P('lat', 'lon'), may hold values from -6 to 6
- kernel_high: bfloat16 [3, 3, 256, 256], replicated, may hold values from -0.125 to 0.125
- kernel_low: bfloat16 [3, 3, 256, 256], replicated, may hold values from -0.125 to 0.125
- kernel_join: bfloat16 [3, 3, 256, 256], replicated, may hold values from -0.125 to 0.125
- target: bfloat16 [384, 768, 256], P('lat', 'lon'), may hold values from -6 to 6
- land_count: int32 [8, 32], P('lat', 'lon'), may hold values from 144 to 1152
Outputs:
- grad_high: float32 [2304, 256], P('lon', 'lat')
- grad_low: float32 [2304, 256], P('lon', 'lat')
- grad_join: float32 [2304, 256], P('lon', 'lat')
The draws below stay inside these ranges and needn't reach their ends.
All inputs are finite; a program needn't handle non-finite values.
Results may differ from the reference program's by a relative error of at most 0.003.
Values may be sent and summed in bfloat16 or wider, within the bound.
No kernel may reach another device: no remote copies, remote signals or barrier semaphores. Data moves between devices by JAX's collectives and lax.ppermute only.
A program may use at most 64 MiB of HBM per device.

```python
import jax
import jax.numpy as jnp
from jax import lax

CHANNELS = 256
TILE_H = 48
TILE_W = 24
LAT_TILES = 8
LON_TILES = 32
ROWS = 384
COLS = 768
LOW_ROWS = 128
LOW_COLS = 256


def touch_ends(result, stream_key, smallest, high):
    longest = result.shape.index(max(result.shape))
    spots = []
    for shift in (0, 1):
        where = [jax.random.randint(jax.random.fold_in(stream_key, axis), (), 0, length) for axis, length in enumerate(result.shape)]
        where[longest] = (where[longest] + shift) % result.shape[longest]
        spots.append(tuple(where))
    return result.at[spots[0]].set(smallest).at[spots[1]].set(high)


def block_scale(rng, shape, shards, least, high):
    def one(axis_at, shards_of):
        steps = jax.random.uniform(jax.random.fold_in(jax.random.fold_in(rng, 6), axis_at), (shards_of,), jnp.float32, least / len(shards), high / len(shards))
        return jnp.repeat(jnp.exp(steps), shape[axis_at] // shards_of).reshape((-1,) + (1,) * (len(shape) - axis_at - 1))

    factor_of = one(*shards[0])
    for cut in shards[1:]:
        factor_of = factor_of * one(*cut)
    return factor_of


def centred(key, dims, width, bound, shards=(), kind=jnp.bfloat16):
    entries = jax.random.normal(key, dims, jnp.float32) * width
    if len(shards) > 0:
        entries = block_scale(key, dims, shards, -0.22, 0.18) * entries
    return jnp.clip(entries, min=-bound, max=bound).astype(kind)


def setup_inputs(seed: int = 0) -> dict:
    key_list = jax.random.split(jax.random.key(seed), 8)
    return {
        "hi_res": centred(key_list[0], (ROWS, COLS, CHANNELS), 1.0, 6.0, ((0, 8), (1, 32))),
        "low_res": centred(key_list[1], (LOW_ROWS, LOW_COLS, CHANNELS), 1.0, 6.0, ((0, 8), (1, 32))),
        "kernel_high": centred(key_list[2], (3, 3, CHANNELS, CHANNELS), (9 * CHANNELS) ** -0.5, 0.125),
        "kernel_low": centred(key_list[3], (3, 3, CHANNELS, CHANNELS), (9 * CHANNELS) ** -0.5, 0.125),
        "kernel_join": centred(key_list[4], (3, 3, CHANNELS, CHANNELS), (9 * CHANNELS) ** -0.5, 0.125),
        "target": centred(key_list[5], (ROWS, COLS, CHANNELS), 1.0, 6.0, ((0, 8), (1, 32))),
        "land_count": touch_ends(jax.random.randint(key_list[6], (LAT_TILES, LON_TILES), TILE_H * TILE_W // 8, TILE_H * TILE_W + 1), jax.random.fold_in(key_list[6], 1), TILE_H * TILE_W // 8, TILE_H * TILE_W).astype(jnp.int32),
    }


ONE_THIRD = 1.0 / 3.0
TWO_THIRDS = 2.0 / 3.0

def pad_cycle(values, margin):
    wrapped = jnp.concatenate([values[:, -margin:], values, values[:, :margin]], axis=1)
    return jnp.pad(wrapped, ((margin, margin), (0, 0), (0, 0)))

def conv_valid(padded, kernel):
    row_count = padded.shape[0] - 2
    col_count = padded.shape[1] - 2
    channels = padded.shape[2]
    running = jnp.zeros((row_count * col_count, kernel.shape[3]), jnp.float32)
    for offset_row in range(3):
        for offset_col in range(3):
            window = padded[offset_row:offset_row + row_count, offset_col:offset_col + col_count].reshape(row_count * col_count, channels)
            running = running + jnp.dot(window, kernel[offset_row, offset_col], preferred_element_type=jnp.float32)
    return running.reshape(row_count, col_count, kernel.shape[3])

def conv_back(padded, kernel):
    row_count = padded.shape[0] - 2
    col_count = padded.shape[1] - 2
    channels = padded.shape[2]
    running = jnp.zeros((row_count * col_count, kernel.shape[2]), jnp.float32)
    for offset_row in range(3):
        for offset_col in range(3):
            window = padded[2 - offset_row:2 - offset_row + row_count, 2 - offset_col:2 - offset_col + col_count].reshape(row_count * col_count, channels)
            running = running + lax.dot_general(window, kernel[offset_row, offset_col], (((1,), (1,)), ((), ())), preferred_element_type=jnp.float32)
    return running.reshape(row_count, col_count, kernel.shape[2])

def kernel_grad(padded, gradient):
    row_count, col_count, out_count = gradient.shape
    flat_grad = gradient.reshape(row_count * col_count, out_count)
    pieces = []
    for offset_row in range(3):
        for offset_col in range(3):
            window = padded[offset_row:offset_row + row_count, offset_col:offset_col + col_count].reshape(row_count * col_count, padded.shape[2])
            pieces.append(lax.dot_general(window, flat_grad, (((0,), (0,)), ((), ())), preferred_element_type=jnp.float32))
    return jnp.concatenate(pieces, axis=0)

def up_rows(values):
    before = values[:-2]
    centre = values[1:-1]
    latter = values[2:]
    leading = ONE_THIRD * before + TWO_THIRDS * centre
    trailing = TWO_THIRDS * centre + ONE_THIRD * latter
    return jnp.stack([leading, centre, trailing], axis=1).reshape(3 * centre.shape[0], values.shape[1], values.shape[2])

def up_cols(values):
    before = values[:, :-2]
    centre = values[:, 1:-1]
    latter = values[:, 2:]
    leading = ONE_THIRD * before + TWO_THIRDS * centre
    trailing = TWO_THIRDS * centre + ONE_THIRD * latter
    return jnp.stack([leading, centre, trailing], axis=2).reshape(values.shape[0], 3 * centre.shape[1], values.shape[2])

def down_rows(values):
    cell_count = (values.shape[0] - 2) // 3
    triple = values[1:-1].reshape(cell_count, 3, values.shape[1], values.shape[2])
    middle = TWO_THIRDS * triple[:, 0] + triple[:, 1] + TWO_THIRDS * triple[:, 2]
    return middle + ONE_THIRD * (values[0:3 * cell_count:3] + values[4:3 * cell_count + 4:3])

def down_cols(values):
    cell_count = (values.shape[1] - 2) // 3
    triple = values[:, 1:-1].reshape(values.shape[0], cell_count, 3, values.shape[2])
    middle = TWO_THIRDS * triple[:, :, 0] + triple[:, :, 1] + TWO_THIRDS * triple[:, :, 2]
    return middle + ONE_THIRD * (values[:, 0:3 * cell_count:3] + values[:, 4:3 * cell_count + 4:3])

def reference(hi_res, low_res, kernel_high, kernel_low, kernel_join, target, land_count):
    high_pad = pad_cycle(hi_res, 1)
    high_act = jnp.maximum(conv_valid(high_pad, kernel_high), 0.0).astype(jnp.bfloat16)
    low_pad = pad_cycle(low_res, 1)
    low_act = jnp.maximum(conv_valid(low_pad, kernel_low), 0.0).astype(jnp.bfloat16)
    lifted = up_cols(up_rows(pad_cycle(low_act, 1).astype(jnp.float32)))
    joined = (high_act.astype(jnp.float32) + lifted).astype(jnp.bfloat16)
    joined_pad = pad_cycle(joined, 1)
    output = conv_valid(joined_pad, kernel_join)
    scale = 2.0 / (TILE_H * TILE_W * TILE_H * TILE_W)
    weight_map = jnp.repeat(jnp.repeat(land_count.astype(jnp.float32), TILE_H, 0), TILE_W, 1)[:, :, None] * scale
    out_grad = (weight_map * (output - target.astype(jnp.float32))).astype(jnp.bfloat16)
    grad_join = kernel_grad(joined_pad, out_grad)
    joined_grad = conv_back(pad_cycle(out_grad, 1), kernel_join).astype(jnp.bfloat16)
    high_grad = jnp.where(high_act > 0, joined_grad, jnp.zeros_like(joined_grad))
    grad_high = kernel_grad(high_pad, high_grad)
    lifted_grad = down_cols(down_rows(pad_cycle(joined_grad, 1).astype(jnp.float32)))
    low_grad = jnp.where(low_act > 0, lifted_grad, jnp.zeros_like(lifted_grad)).astype(jnp.bfloat16)
    grad_low = kernel_grad(low_pad, low_grad)
    return (grad_high, grad_low, grad_join)
```

```python
import jax
import jax.numpy as jnp
import numpy as np
from jax import lax
from jax.experimental import pallas as pl
from jax.experimental.pallas import tpu as pltpu
from jax.sharding import Mesh, PartitionSpec as P

F32 = jnp.float32
BF16 = jnp.bfloat16
C = 256
H, W = 48, 24
LH, LW = 16, 8
WW = 32
LWW = 16
LAT = ("yh", "yl", "xh")
LON = ("zh", "zm", "zl", "xl", "core")
SCALE = 2.0 / (H * W * H * W)
NINTH = 1.0 / 9.0
PK = 304
PAD = 8
VMEM = pl.BlockSpec(memory_space=pltpu.VMEM)
SMEM = pl.BlockSpec(memory_space=pltpu.SMEM)


def up_matrix():
    def line(pixel, cell_of):
        m, r = pixel // 3, pixel % 3
        return {0: {m - 1: 1, m: 2}, 1: {m: 3}, 2: {m: 2, m + 1: 1}}[r].get(cell_of, 0)

    rows = np.array([[line(i - 3, e - 2) for e in range(8)] for i in range(18)])
    cols = np.array([[line(j - 4, f - 3) for f in range(LWW)] for j in range(WW)])
    return np.einsum("ie,jf->ijef", rows, cols).reshape(18 * WW, 8 * LWW)


def down_matrix():
    taps = [1, 2, 3, 2, 1]
    rows = np.zeros((8, 26))
    for m in range(8):
        rows[m, 3 * m : 3 * m + 5] = taps
    cols = np.zeros((LWW, WW))
    for m in range(LW):
        cols[m + 3, 3 * m + 3 : 3 * m + 8] = taps
    return np.einsum("md,fj->mfdj", rows, cols).reshape(8 * LWW, 26 * WW)


def pack_lon(land_ref, hi_ref, tgt_ref, low_ref, west_ref, east_ref):
    land = land_ref[0, 0]
    sub = lax.broadcasted_iota(jnp.int32, (H, 8, C), 1)
    land_a = (land // 32).astype(F32)
    land_b = (land % 32).astype(F32)
    lands = jnp.where(sub == 6, land_a, land_b)
    hi = hi_ref[...].astype(F32)
    tgt = tgt_ref[...].astype(F32)
    west = jnp.where(sub < 4, hi[:, 0:8], jnp.where(sub < 6, pltpu.roll(tgt[:, 0:8], 4, 1), lands))
    east = jnp.where(
        sub < 4,
        pltpu.roll(hi[:, 16:24], 4, 1),
        jnp.where(sub < 6, pltpu.roll(tgt[:, 16:24], 6, 1), lands),
    )
    west_ref[0:H] = west.astype(BF16)
    east_ref[0:H] = east.astype(BF16)
    west_ref[H:] = low_ref[...]
    east_ref[H:] = low_ref[...]


def widen(land_ref, hi_ref, tgt_ref, low_ref, w_ref, e_ref, hiw_ref, tgw_ref, loww_ref, landw_ref, north_ref, south_ref):
    sub = lax.broadcasted_iota(jnp.int32, (H, 8, C), 1)
    low_half = sub < 4
    wpk = w_ref[0:H].astype(F32)
    epk = e_ref[0:H].astype(F32)

    def joined_groups(own, left, right):
        turned = [pltpu.roll(own[:, 8 * g : 8 * g + 8], 4, 1) for g in range(3)]
        parts = [left] + turned + [right]
        return jnp.concatenate(
            [jnp.where(low_half, parts[g], parts[g + 1]) for g in range(4)], axis=1
        ).reshape(H * WW, C)

    hi = joined_groups(hi_ref[...].astype(F32), wpk, pltpu.roll(epk, 4, 1)).astype(BF16)
    hiw_ref[...] = hi
    tgt = joined_groups(tgt_ref[...].astype(F32), pltpu.roll(wpk, 6, 1), epk).astype(BF16)
    tgw_ref[...] = tgt
    sub_low = lax.broadcasted_iota(jnp.int32, (LH, 8, C), 1)
    own_low = pltpu.roll(low_ref[...].astype(F32), 3, 1)
    w_low = pltpu.roll(w_ref[H:].astype(F32), 3, 1)
    e_low = pltpu.roll(e_ref[H:].astype(F32), 3, 1)
    low = jnp.concatenate(
        [jnp.where(sub_low < 3, w_low, own_low), jnp.where(sub_low < 3, own_low, e_low)], axis=1
    ).reshape(LH * LWW, C).astype(BF16)
    loww_ref[...] = low
    land = land_ref[0, 0]
    col = lax.broadcasted_iota(jnp.int32, (WW, C), 0)

    def land_rows(part, own):
        left = wpk[0, part : part + 1, :]
        right = epk[0, part : part + 1, :]
        return jnp.where(col < 4, left, jnp.where(col < 4 + W, own, right))

    lands = jnp.concatenate(
        [land_rows(6, (land // 32).astype(F32)), land_rows(7, (land % 32).astype(F32))], axis=0
    ).astype(BF16)
    landw_ref[...] = lands
    north_ref[0:128] = hi[0:128]
    north_ref[128:192] = tgt[0:64]
    north_ref[192:240] = low[0:48]
    north_ref[240:304] = lands
    south_ref[0:128] = hi[44 * WW :]
    south_ref[128:192] = tgt[46 * WW :]
    south_ref[192:240] = low[13 * LWW :]
    south_ref[240:304] = lands


def main(
    pos_ref, hiw_ref, tgw_ref, loww_ref, landw_ref, n_ref, s_ref, kh_ref, kl_ref, kj_ref, up_ref, down_ref,
    keep_ref, send_ref,
    x3_ref, j3_ref, o3_ref, l3_ref, f_ref, ha_ref, la_ref, jg_ref, og_ref, lg_ref, tg_ref, kt_ref, g_ref,
):
    lat = pos_ref[0]
    core = pos_ref[1]
    first = lat == 0
    last = lat == 7

    def spread(dst, count, step):
        def one(t, _):
            s = pl.multiple_of(t * step, 16)
            v = f_ref[pl.ds(s, step + 2 * PAD), :]
            dst[pl.ds(s, step), 0:C] = v[PAD - 1 : PAD - 1 + step].astype(BF16)
            dst[pl.ds(s, step), C : 2 * C] = v[PAD : PAD + step].astype(BF16)
            dst[pl.ds(s, step), 2 * C : 3 * C] = v[PAD + 1 : PAD + 1 + step].astype(BF16)
            return 0

        lax.fori_loop(0, count // step, one, 0)

    def window(src, start, rows, stride):
        return jnp.concatenate(
            [src[pl.ds(pl.multiple_of(start + d * stride, 16), rows), :] for d in range(3)], axis=1
        )

    def zero_rows(start, rows):
        f_ref[PAD + start : PAD + start + rows, :] = jnp.zeros((rows, C), F32)

    f_ref[0:PAD, :] = jnp.zeros((PAD, C), F32)
    f_ref[PAD + 56 * WW :, :] = jnp.zeros((PAD, C), F32)
    for tap in range(9):
        kt_ref[(8 - tap) * C : (9 - tap) * C, :] = kj_ref[tap * C : (tap + 1) * C, :].T

    f_ref[PAD : PAD + 48, :] = n_ref[192:240, :].astype(F32)
    f_ref[PAD + 48 : PAD + 304, :] = loww_ref[...].astype(F32)
    f_ref[PAD + 304 : PAD + 352, :] = s_ref[192:240, :].astype(F32)
    f_ref[PAD + 352 : PAD + 368, :] = jnp.zeros((16, C), F32)

    @pl.when(first)
    def _():
        zero_rows(0, 48)

    @pl.when(last)
    def _():
        zero_rows(304, 48)

    spread(l3_ref, 352, 176)
    low_act = jnp.maximum(
        jnp.dot(window(l3_ref, 0, 320, LWW), kl_ref[...], preferred_element_type=F32), 0.0
    ).astype(BF16)
    la_ref[...] = low_act

    @pl.when(first)
    def _():
        la_ref[0:32, :] = jnp.zeros((32, C), BF16)

    @pl.when(last)
    def _():
        la_ref[288:320, :] = jnp.zeros((32, C), BF16)

    f_ref[PAD : PAD + 128, :] = n_ref[0:128, :].astype(F32)
    f_ref[PAD + 128 : PAD + 1664, :] = hiw_ref[...].astype(F32)
    f_ref[PAD + 1664 : PAD + 1792, :] = s_ref[0:128, :].astype(F32)
    tg_ref[0:64, :] = n_ref[128:192, :]
    tg_ref[64:1600, :] = tgw_ref[...]
    tg_ref[1600:1664, :] = s_ref[128:192, :]

    @pl.when(first)
    def _():
        zero_rows(0, 128)

    @pl.when(last)
    def _():
        zero_rows(1664, 128)

    spread(x3_ref, 1792, 256)

    def high(b, _):
        s = pl.multiple_of(b * 576, 64)
        act = jnp.maximum(
            jnp.dot(window(x3_ref, s, 576, WW), kh_ref[...], preferred_element_type=F32), 0.0
        ).astype(BF16)
        ha_ref[pl.ds(s, 576), :] = act
        cells = la_ref[pl.ds(pl.multiple_of(b * 96, 32), 128), :]
        lift = jnp.dot(up_ref[...], cells, preferred_element_type=F32) * NINTH
        f_ref[pl.ds(PAD + s, 576), :] = act.astype(F32) + lift
        return 0

    lax.fori_loop(0, 3, high, 0)

    @pl.when(first)
    def _():
        zero_rows(0, 96)

    @pl.when(last)
    def _():
        zero_rows(51 * WW, 96)

    spread(j3_ref, 1728, 288)

    def weight_of(ref, base):
        return (ref[base : base + 32, :].astype(F32) * 32.0 + ref[base + 32 : base + 64, :].astype(F32)) * SCALE

    top = weight_of(n_ref, 240)[None]
    mid = weight_of(landw_ref, 0)[None]
    bot = weight_of(s_ref, 240)[None]

    def join(b, _):
        s = pl.multiple_of(b * 416, 32)
        y = jnp.dot(window(j3_ref, s, 416, WW), kj_ref[...], preferred_element_type=F32)
        diff = (y - tg_ref[pl.ds(s, 416), :].astype(F32)).reshape(13, WW, C)
        row = lax.broadcasted_iota(jnp.int32, (13, WW, C), 0) + b * 13
        weight = jnp.where(row < 2, top, jnp.where(row >= 50, bot, mid))
        f_ref[pl.ds(PAD + s, 416), :] = (weight * diff).reshape(416, C)
        return 0

    lax.fori_loop(0, 4, join, 0)

    @pl.when(first)
    def _():
        zero_rows(0, 64)

    @pl.when(last)
    def _():
        zero_rows(50 * WW, 64)

    spread(o3_ref, 1664, 416)

    def own_columns(rows):
        col = lax.broadcasted_iota(jnp.int32, (rows // WW, WW, C), 1).reshape(rows, C)
        return (col >= 4) & (col < 4 + W)

    def contract(x_ref, g_val, base, stride, rows, slot):
        for d in range(3):
            g_ref[slot, d * 768 : (d + 1) * 768, :] = lax.dot_general(
                x_ref[base + d * stride : base + d * stride + rows, :],
                g_val,
                (((0,), (0,)), ((), ())),
                preferred_element_type=F32,
            )

    def own_grad(t, _):
        s = pl.multiple_of(t * 256, 64)
        v = f_ref[pl.ds(PAD + 64 + s, 256), :]
        og_ref[pl.ds(s, 256), :] = jnp.where(own_columns(256), v, 0.0).astype(BF16)
        return 0

    lax.fori_loop(0, 6, own_grad, 0)
    contract(j3_ref, og_ref[...], 64, WW, 1536, 2)

    def back(b, _):
        s = pl.multiple_of(b * 320, 32)
        y = jnp.dot(window(o3_ref, s, 320, WW), kt_ref[...], preferred_element_type=F32)
        jg_ref[pl.ds(s, 320), :] = y.astype(BF16)
        return 0

    lax.fori_loop(0, 5, back, 0)

    @pl.when(first)
    def _():
        jg_ref[0:32, :] = jnp.zeros((32, C), BF16)

    @pl.when(last)
    def _():
        jg_ref[49 * WW :, :] = jnp.zeros((32, C), BF16)

    def high_grad(t, _):
        s = pl.multiple_of(t * 256, 64)
        v = jg_ref[pl.ds(s + 32, 256), :].astype(F32)
        on = ha_ref[pl.ds(s + 96, 256), :].astype(F32) > 0
        og_ref[pl.ds(s, 256), :] = jnp.where(own_columns(256) & on, v, 0.0).astype(BF16)
        return 0

    lax.fori_loop(0, 6, high_grad, 0)
    contract(x3_ref, og_ref[...], 96, WW, 1536, 0)

    for b in range(2):
        lifted = jnp.dot(down_ref[...], jg_ref[b * 768 : b * 768 + 832, :], preferred_element_type=F32) * NINTH
        on = la_ref[32 + b * 128 : 160 + b * 128, :].astype(F32) > 0
        lg_ref[b * 128 : (b + 1) * 128, :] = jnp.where(on, lifted, 0.0).astype(BF16)
    contract(l3_ref, lg_ref[...], 32, LWW, 256, 1)

    def split(t, _):
        pair = t // 4
        k = t % 4
        dst = pl.multiple_of(t * 224, 32)
        for half, ref in ((core, keep_ref), (1 - core, send_ref)):
            src = pl.multiple_of((k * 8 + pair * 2 + half) * 72, 8)
            block = jnp.concatenate(
                [g_ref[g, pl.ds(src, 72), :] for g in range(3)] + [jnp.zeros((8, C), F32)], axis=0
            )
            ref[pl.ds(dst, 224), :] = block.astype(ref.dtype)
        return 0

    lax.fori_loop(0, 16, split, 0)


def merge(keep_ref, recv_ref, out_ref):
    lane = lax.broadcasted_iota(jnp.int32, (224, 128), 1) < 64

    def one(t, _):
        s = pl.multiple_of(t * 224, 32)
        v = keep_ref[pl.ds(s, 224), :] + recv_ref[pl.ds(s, 224), :].astype(F32)
        a, b = v[:, :128], v[:, 128:]
        out_ref[0, pl.ds(s, 224), :] = jnp.where(lane, a, pltpu.roll(b, 64, 1)).astype(BF16)
        out_ref[1, pl.ds(s, 224), :] = jnp.where(lane, pltpu.roll(a, 64, 1), b).astype(BF16)
        return 0

    lax.fori_loop(0, 16, one, 0)


def regroup(in_ref, out_ref):
    quarter = lax.broadcasted_iota(jnp.int32, (56, 128), 1) // 32
    for k in range(4):
        total = in_ref[0, k * 224 : (k + 1) * 224, :].astype(F32)
        for i in range(1, 8):
            total = total + in_ref[i, k * 224 : (k + 1) * 224, :].astype(F32)
        parts = [total[s * 56 : (s + 1) * 56] for s in range(4)]
        for q in range(4):
            out = jnp.zeros((56, 128), F32)
            for s in range(4):
                shift = ((s - q) * 32) % 128
                turned = pltpu.roll(parts[s], shift, 1) if shift else parts[s]
                out = jnp.where(quarter == s, turned, out)
            out_ref[q * 4 + k] = out.astype(out_ref.dtype)


def finish(in_ref, a_ref, b_ref, c_ref):
    total = in_ref[0].astype(F32)
    for i in range(1, 16):
        total = total + in_ref[i].astype(F32)
    rows = jnp.concatenate(
        [total if s == 0 else pltpu.roll(total, 128 - 32 * s, 1) for s in range(4)], axis=0
    )
    for g, ref in enumerate((a_ref, b_ref, c_ref)):
        ref[...] = rows[g * 72 : (g + 1) * 72, 0:32]


def call(kernel, out, specs, scratch=(), name=None, vmem=None):
    return pl.pallas_call(
        kernel,
        out_shape=tuple(jax.ShapeDtypeStruct(s, d) for s, d in out),
        in_specs=list(specs),
        out_specs=tuple(VMEM for _ in out),
        scratch_shapes=list(scratch),
        name=name,
        compiler_params=pltpu.CompilerParams(vmem_limit_bytes=vmem) if vmem else None,
    )


def ring(count, step):
    return [(i, (i + step) % count) for i in range(count)]


def body(hi, low, kh, kl, kj, tgt, land):
    west, east = call(
        pack_lon, [((H + LH, 8, C), BF16)] * 2, [SMEM] + [VMEM] * 3, name="pack_lon"
    )(land, hi, tgt, low)
    from_e = lax.ppermute(west, LON, ring(32, -1))
    from_w = lax.ppermute(east, LON, ring(32, 1))
    hiw, tgw, loww, landw, north, south = call(
        widen,
        [((H * WW, C), BF16), ((H * WW, C), BF16), ((LH * LWW, C), BF16), ((64, C), BF16), ((PK, C), BF16), ((PK, C), BF16)],
        [SMEM] + [VMEM] * 5,
        name="widen",
    )(land, hi, tgt, low, from_w, from_e)
    from_s = lax.ppermute(north, LAT, ring(8, -1))
    from_n = lax.ppermute(south, LAT, ring(8, 1))
    pos = jnp.stack([lax.axis_index(LAT), lax.axis_index("core")]).astype(jnp.int32)
    keep, send = call(
        main,
        [((3584, C), F32), ((3584, C), BF16)],
        [SMEM] + [VMEM] * 11,
        [
            pltpu.VMEM((1792, 768), BF16),
            pltpu.VMEM((1728, 768), BF16),
            pltpu.VMEM((1664, 768), BF16),
            pltpu.VMEM((352, 768), BF16),
            pltpu.VMEM((1792 + 2 * PAD, C), F32),
            pltpu.VMEM((1728, C), BF16),
            pltpu.VMEM((320, C), BF16),
            pltpu.VMEM((1600, C), BF16),
            pltpu.VMEM((1536, C), BF16),
            pltpu.VMEM((256, C), BF16),
            pltpu.VMEM((1664, C), BF16),
            pltpu.VMEM((2304, C), BF16),
            pltpu.VMEM((3, 2304, C), F32),
        ],
        name="main",
        vmem=60 * 1024 * 1024,
    )(
        pos, hiw, tgw, loww, landw, from_n, from_s,
        kh.reshape(9 * C, C), kl.reshape(9 * C, C), kj.reshape(9 * C, C),
        jnp.asarray(up_matrix(), BF16), jnp.asarray(down_matrix(), BF16),
    )
    recv = lax.ppermute(send, "core", ring(2, 1))
    (parts,) = call(merge, [((2, 3584, 128), BF16)], [VMEM] * 2, name="merge")(keep, recv)
    parts = lax.all_to_all(parts.reshape(8, 896, 128), ("yl", "zl", "xl"), 0, 0, tiled=True)
    (parts,) = call(regroup, [((16, 56, 128), F32)], [VMEM], name="regroup")(parts)
    parts = lax.all_to_all(parts, ("yh", "xh", "zh", "zm"), 0, 0, tiled=True)
    return call(finish, [((72, 32), F32)] * 3, [VMEM], name="finish")(parts)


def solution(mesh):
    fine = Mesh(mesh.devices.reshape((2,) * 8), LAT + LON)
    tile = P(LAT, LON, None)
    return jax.shard_map(
        body,
        mesh=fine,
        in_specs=(tile, tile, P(), P(), P(), tile, P(LAT, LON)),
        out_specs=(P(LON, LAT),) * 3,
        check_vma=False,
    )
```

```python
import jax
import jax.numpy as jnp
import numpy as np
from jax import lax
from jax.experimental import pallas as pl
from jax.experimental.pallas import tpu as pltpu
from jax.sharding import Mesh, PartitionSpec as P

F32 = jnp.float32
BF16 = jnp.bfloat16
C = 256
H, W = 48, 24
LH, LW = 16, 8
WW = 32
LWW = 16
LAT = ("yh", "yl", "xh")
LON = ("zh", "zm", "zl", "xl", "core")
SCALE = 2.0 / (H * W * H * W)
NINTH = 1.0 / 9.0
PK = 304
PAD = 8
MIB = 1024 * 1024
VMEM = pl.BlockSpec(memory_space=pltpu.VMEM)
SMEM = pl.BlockSpec(memory_space=pltpu.SMEM)


def up_matrix():
    def line(pixel, cell_of):
        m, r = pixel // 3, pixel % 3
        return {0: {m - 1: 1, m: 2}, 1: {m: 3}, 2: {m: 2, m + 1: 1}}[r].get(cell_of, 0)

    rows = np.array([[line(i - 3, e - 2) for e in range(8)] for i in range(18)])
    cols = np.array([[line(j - 4, f - 3) for f in range(LWW)] for j in range(WW)])
    return np.einsum("ie,jf->ijef", rows, cols).reshape(18 * WW, 8 * LWW)


def down_matrix():
    taps = [1, 2, 3, 2, 1]
    rows = np.zeros((8, 26))
    for m in range(8):
        rows[m, 3 * m : 3 * m + 5] = taps
    cols = np.zeros((LWW, WW))
    for m in range(LW):
        cols[m + 3, 3 * m + 3 : 3 * m + 8] = taps
    return np.einsum("md,fj->mfdj", rows, cols).reshape(8 * LWW, 26 * WW)


def pack_lon(land_ref, hi_ref, tgt_ref, low_ref, west_ref, east_ref):
    land = land_ref[0, 0]
    sub = lax.broadcasted_iota(jnp.int32, (H, 8, C), 1)
    land_a = (land // 32).astype(F32)
    land_b = (land % 32).astype(F32)
    lands = jnp.where(sub == 6, land_a, land_b)
    hi = hi_ref[...].astype(F32)
    tgt = tgt_ref[...].astype(F32)
    west = jnp.where(sub < 4, hi[:, 0:8], jnp.where(sub < 6, pltpu.roll(tgt[:, 0:8], 4, 1), lands))
    east = jnp.where(
        sub < 4,
        pltpu.roll(hi[:, 16:24], 4, 1),
        jnp.where(sub < 6, pltpu.roll(tgt[:, 16:24], 6, 1), lands),
    )
    west_ref[0:H] = west.astype(BF16)
    east_ref[0:H] = east.astype(BF16)
    west_ref[H:] = low_ref[...]
    east_ref[H:] = low_ref[...]


def widen(land_ref, hi_ref, tgt_ref, low_ref, w_ref, e_ref, hiw_ref, tgw_ref, loww_ref, landw_ref, north_ref, south_ref):
    sub = lax.broadcasted_iota(jnp.int32, (H, 8, C), 1)
    low_half = sub < 4
    wpk = w_ref[0:H].astype(F32)
    epk = e_ref[0:H].astype(F32)

    def joined_groups(own, left, right):
        turned = [pltpu.roll(own[:, 8 * g : 8 * g + 8], 4, 1) for g in range(3)]
        parts = [left] + turned + [right]
        return jnp.concatenate(
            [jnp.where(low_half, parts[g], parts[g + 1]) for g in range(4)], axis=1
        ).reshape(H * WW, C)

    hi = joined_groups(hi_ref[...].astype(F32), wpk, pltpu.roll(epk, 4, 1)).astype(BF16)
    hiw_ref[...] = hi
    tgt = joined_groups(tgt_ref[...].astype(F32), pltpu.roll(wpk, 6, 1), epk).astype(BF16)
    tgw_ref[...] = tgt
    sub_low = lax.broadcasted_iota(jnp.int32, (LH, 8, C), 1)
    own_low = pltpu.roll(low_ref[...].astype(F32), 3, 1)
    w_low = pltpu.roll(w_ref[H:].astype(F32), 3, 1)
    e_low = pltpu.roll(e_ref[H:].astype(F32), 3, 1)
    low = jnp.concatenate(
        [jnp.where(sub_low < 3, w_low, own_low), jnp.where(sub_low < 3, own_low, e_low)], axis=1
    ).reshape(LH * LWW, C).astype(BF16)
    loww_ref[...] = low
    land = land_ref[0, 0]
    col = lax.broadcasted_iota(jnp.int32, (WW, C), 0)

    def land_rows(part, own):
        left = wpk[0, part : part + 1, :]
        right = epk[0, part : part + 1, :]
        return jnp.where(col < 4, left, jnp.where(col < 4 + W, own, right))

    lands = jnp.concatenate(
        [land_rows(6, (land // 32).astype(F32)), land_rows(7, (land % 32).astype(F32))], axis=0
    ).astype(BF16)
    landw_ref[...] = lands
    north_ref[0:128] = hi[0:128]
    north_ref[128:192] = tgt[0:64]
    north_ref[192:240] = low[0:48]
    north_ref[240:304] = lands
    south_ref[0:128] = hi[44 * WW :]
    south_ref[128:192] = tgt[46 * WW :]
    south_ref[192:240] = low[13 * LWW :]
    south_ref[240:304] = lands


def main(
    pos_ref, hiw_ref, tgw_ref, loww_ref, landw_ref, n_ref, s_ref, kh_ref, kl_ref, kj_ref, up_ref, down_ref,
    keep_ref, send_ref,
    x3_ref, j3_ref, o3_ref, l3_ref, f_ref, ha_ref, la_ref, jg_ref, og_ref, lg_ref, tg_ref, kt_ref, g_ref,
):
    lat = pos_ref[0]
    core = pos_ref[1]
    first = lat == 0
    last = lat == 7

    def spread(dst, count, step):
        def one(t, _):
            s = pl.multiple_of(t * step, 16)
            v = f_ref[pl.ds(s, step + 2 * PAD), :]
            dst[pl.ds(s, step), 0:C] = v[PAD - 1 : PAD - 1 + step].astype(BF16)
            dst[pl.ds(s, step), C : 2 * C] = v[PAD : PAD + step].astype(BF16)
            dst[pl.ds(s, step), 2 * C : 3 * C] = v[PAD + 1 : PAD + 1 + step].astype(BF16)
            return 0

        lax.fori_loop(0, count // step, one, 0)

    def window(src, start, rows, stride):
        return jnp.concatenate(
            [src[pl.ds(pl.multiple_of(start + d * stride, 16), rows), :] for d in range(3)], axis=1
        )

    def zero_rows(start, rows):
        f_ref[PAD + start : PAD + start + rows, :] = jnp.zeros((rows, C), F32)

    f_ref[0:PAD, :] = jnp.zeros((PAD, C), F32)
    f_ref[PAD + 56 * WW :, :] = jnp.zeros((PAD, C), F32)
    for tap in range(9):
        kt_ref[(8 - tap) * C : (9 - tap) * C, :] = kj_ref[tap * C : (tap + 1) * C, :].T

    f_ref[PAD : PAD + 48, :] = n_ref[192:240, :].astype(F32)
    f_ref[PAD + 48 : PAD + 304, :] = loww_ref[...].astype(F32)
    f_ref[PAD + 304 : PAD + 352, :] = s_ref[192:240, :].astype(F32)
    f_ref[PAD + 352 : PAD + 368, :] = jnp.zeros((16, C), F32)

    @pl.when(first)
    def _():
        zero_rows(0, 48)

    @pl.when(last)
    def _():
        zero_rows(304, 48)

    spread(l3_ref, 352, 176)
    low_act = jnp.maximum(
        jnp.dot(window(l3_ref, 0, 320, LWW), kl_ref[...], preferred_element_type=F32), 0.0
    ).astype(BF16)
    la_ref[...] = low_act

    @pl.when(first)
    def _():
        la_ref[0:32, :] = jnp.zeros((32, C), BF16)

    @pl.when(last)
    def _():
        la_ref[288:320, :] = jnp.zeros((32, C), BF16)

    f_ref[PAD : PAD + 128, :] = n_ref[0:128, :].astype(F32)
    f_ref[PAD + 128 : PAD + 1664, :] = hiw_ref[...].astype(F32)
    f_ref[PAD + 1664 : PAD + 1792, :] = s_ref[0:128, :].astype(F32)
    tg_ref[0:64, :] = n_ref[128:192, :]
    tg_ref[64:1600, :] = tgw_ref[...]
    tg_ref[1600:1664, :] = s_ref[128:192, :]

    @pl.when(first)
    def _():
        zero_rows(0, 128)

    @pl.when(last)
    def _():
        zero_rows(1664, 128)

    spread(x3_ref, 1792, 256)

    def high(b, _):
        s = pl.multiple_of(b * 576, 64)
        act = jnp.maximum(
            jnp.dot(window(x3_ref, s, 576, WW), kh_ref[...], preferred_element_type=F32), 0.0
        ).astype(BF16)
        ha_ref[pl.ds(s, 576), :] = act
        cells = la_ref[pl.ds(pl.multiple_of(b * 96, 32), 128), :]
        lift = jnp.dot(up_ref[...], cells, preferred_element_type=F32) * NINTH
        f_ref[pl.ds(PAD + s, 576), :] = act.astype(F32) + lift
        return 0

    lax.fori_loop(0, 3, high, 0)

    @pl.when(first)
    def _():
        zero_rows(0, 96)

    @pl.when(last)
    def _():
        zero_rows(51 * WW, 96)

    spread(j3_ref, 1728, 288)

    def weight_of(ref, base):
        return (ref[base : base + 32, :].astype(F32) * 32.0 + ref[base + 32 : base + 64, :].astype(F32)) * SCALE

    top = weight_of(n_ref, 240)[None]
    mid = weight_of(landw_ref, 0)[None]
    bot = weight_of(s_ref, 240)[None]

    def join(b, _):
        s = pl.multiple_of(b * 416, 32)
        y = jnp.dot(window(j3_ref, s, 416, WW), kj_ref[...], preferred_element_type=F32)
        diff = (y - tg_ref[pl.ds(s, 416), :].astype(F32)).reshape(13, WW, C)
        row = lax.broadcasted_iota(jnp.int32, (13, WW, C), 0) + b * 13
        weight = jnp.where(row < 2, top, jnp.where(row >= 50, bot, mid))
        f_ref[pl.ds(PAD + s, 416), :] = (weight * diff).reshape(416, C)
        return 0

    lax.fori_loop(0, 4, join, 0)

    @pl.when(first)
    def _():
        zero_rows(0, 64)

    @pl.when(last)
    def _():
        zero_rows(50 * WW, 64)

    spread(o3_ref, 1664, 416)

    def own_columns(rows):
        col = lax.broadcasted_iota(jnp.int32, (rows // WW, WW, C), 1).reshape(rows, C)
        return (col >= 4) & (col < 4 + W)

    def contract(x_ref, g_val, base, stride, rows, slot):
        for d in range(3):
            g_ref[slot, d * 768 : (d + 1) * 768, :] = lax.dot_general(
                x_ref[base + d * stride : base + d * stride + rows, :],
                g_val,
                (((0,), (0,)), ((), ())),
                preferred_element_type=F32,
            )

    def own_grad(t, _):
        s = pl.multiple_of(t * 256, 64)
        v = f_ref[pl.ds(PAD + 64 + s, 256), :]
        og_ref[pl.ds(s, 256), :] = jnp.where(own_columns(256), v, 0.0).astype(BF16)
        return 0

    lax.fori_loop(0, 6, own_grad, 0)
    contract(j3_ref, og_ref[...], 64, WW, 1536, 2)

    def back(b, _):
        s = pl.multiple_of(b * 320, 32)
        y = jnp.dot(window(o3_ref, s, 320, WW), kt_ref[...], preferred_element_type=F32)
        jg_ref[pl.ds(s, 320), :] = y.astype(BF16)
        return 0

    lax.fori_loop(0, 5, back, 0)

    @pl.when(first)
    def _():
        jg_ref[0:32, :] = jnp.zeros((32, C), BF16)

    @pl.when(last)
    def _():
        jg_ref[49 * WW :, :] = jnp.zeros((32, C), BF16)

    def high_grad(t, _):
        s = pl.multiple_of(t * 256, 64)
        v = jg_ref[pl.ds(s + 32, 256), :].astype(F32)
        on = ha_ref[pl.ds(s + 96, 256), :].astype(F32) > 0
        og_ref[pl.ds(s, 256), :] = jnp.where(own_columns(256) & on, v, 0.0).astype(BF16)
        return 0

    lax.fori_loop(0, 6, high_grad, 0)
    contract(x3_ref, og_ref[...], 96, WW, 1536, 0)

    for b in range(2):
        lifted = jnp.dot(down_ref[...], jg_ref[b * 768 : b * 768 + 832, :], preferred_element_type=F32) * NINTH
        on = la_ref[32 + b * 128 : 160 + b * 128, :].astype(F32) > 0
        lg_ref[b * 128 : (b + 1) * 128, :] = jnp.where(on, lifted, 0.0).astype(BF16)
    contract(l3_ref, lg_ref[...], 32, LWW, 256, 1)

    def split(t, _):
        xl = t // 8
        z = t % 8
        dst = pl.multiple_of(t * 224, 32)
        for half, ref in ((core, keep_ref), (1 - core, send_ref)):
            src = pl.multiple_of((z * 4 + xl * 2 + half) * 72, 8)
            block = jnp.concatenate(
                [g_ref[g, pl.ds(src, 72), :] for g in range(3)] + [jnp.zeros((8, C), F32)], axis=0
            )
            ref[pl.ds(dst, 224), :] = block.astype(ref.dtype)
        return 0

    lax.fori_loop(0, 16, split, 0)


def merge(keep_ref, recv_ref, out_ref):
    quarter = lax.broadcasted_iota(jnp.int32, (56, 128), 1) // 32

    def one(t, _):
        xl = t // 8
        z = t % 8
        s = pl.multiple_of(t * 224, 32)
        v = keep_ref[pl.ds(s, 224), :] + recv_ref[pl.ds(s, 224), :].astype(F32)
        for h in range(2):
            parts = [v[g * 56 : (g + 1) * 56, h * 128 : (h + 1) * 128] for g in range(4)]
            for q in range(4):
                out = None
                for g in range(4):
                    shift = ((g - q) * 32) % 128
                    turned = pltpu.roll(parts[g], shift, 1) if shift else parts[g]
                    out = turned if out is None else jnp.where(quarter == g, turned, out)
                out_ref[(h * 4 + q) * 2 + xl, z] = out.astype(BF16)
        return 0

    lax.fori_loop(0, 16, one, 0)


def total(in_ref, out_ref):
    def one(z, _):
        acc = in_ref[0, z].astype(F32)
        for i in range(1, 16):
            acc = acc + in_ref[i, z].astype(F32)
        out_ref[z] = acc.astype(out_ref.dtype)
        return 0

    lax.fori_loop(0, 8, one, 0)


def finish(in_ref, a_ref, b_ref, c_ref):
    acc = in_ref[0].astype(F32)
    for i in range(1, 8):
        acc = acc + in_ref[i].astype(F32)
    rows = jnp.concatenate(
        [acc if s == 0 else pltpu.roll(acc, 128 - 32 * s, 1) for s in range(4)], axis=0
    )
    for g, ref in enumerate((a_ref, b_ref, c_ref)):
        ref[...] = rows[g * 72 : (g + 1) * 72].T[0:32]


def call(kernel, out, specs, scratch=(), name=None, vmem=None):
    return pl.pallas_call(
        kernel,
        out_shape=tuple(jax.ShapeDtypeStruct(s, d) for s, d in out),
        in_specs=list(specs),
        out_specs=tuple(VMEM for _ in out),
        scratch_shapes=list(scratch),
        name=name,
        compiler_params=pltpu.CompilerParams(vmem_limit_bytes=vmem) if vmem else None,
    )


def ring(count, step):
    return [(i, (i + step) % count) for i in range(count)]


def body(hi, low, kh, kl, kj, tgt, land):
    west, east = call(
        pack_lon, [((H + LH, 8, C), BF16)] * 2, [SMEM] + [VMEM] * 3, name="pack_lon", vmem=8 * MIB
    )(land, hi, tgt, low)
    from_e = lax.ppermute(west, LON, ring(32, -1))
    from_w = lax.ppermute(east, LON, ring(32, 1))
    hiw, tgw, loww, landw, north, south = call(
        widen,
        [((H * WW, C), BF16), ((H * WW, C), BF16), ((LH * LWW, C), BF16), ((64, C), BF16), ((PK, C), BF16), ((PK, C), BF16)],
        [SMEM] + [VMEM] * 5,
        name="widen",
        vmem=14 * MIB,
    )(land, hi, tgt, low, from_w, from_e)
    from_s = lax.ppermute(north, LAT, ring(8, -1))
    from_n = lax.ppermute(south, LAT, ring(8, 1))
    pos = jnp.stack([lax.axis_index(LAT), lax.axis_index("core")]).astype(jnp.int32)
    keep, send = call(
        main,
        [((3584, C), F32), ((3584, C), BF16)],
        [SMEM] + [VMEM] * 11,
        [
            pltpu.VMEM((1792, 768), BF16),
            pltpu.VMEM((1728, 768), BF16),
            pltpu.VMEM((1664, 768), BF16),
            pltpu.VMEM((352, 768), BF16),
            pltpu.VMEM((1792 + 2 * PAD, C), F32),
            pltpu.VMEM((1728, C), BF16),
            pltpu.VMEM((320, C), BF16),
            pltpu.VMEM((1600, C), BF16),
            pltpu.VMEM((1536, C), BF16),
            pltpu.VMEM((256, C), BF16),
            pltpu.VMEM((1664, C), BF16),
            pltpu.VMEM((2304, C), BF16),
            pltpu.VMEM((3, 2304, C), F32),
        ],
        name="main",
        vmem=38 * MIB,
    )(
        pos, hiw, tgw, loww, landw, from_n, from_s,
        kh.reshape(9 * C, C), kl.reshape(9 * C, C), kj.reshape(9 * C, C),
        jnp.asarray(up_matrix(), BF16), jnp.asarray(down_matrix(), BF16),
    )
    recv = lax.ppermute(send, "core", ring(2, 1))
    (parts,) = call(merge, [((16, 8, 56, 128), BF16)], [VMEM] * 2, name="merge", vmem=12 * MIB)(keep, recv)
    parts = lax.all_to_all(parts, ("yh", "yl", "xh", "xl"), 0, 0, tiled=True)
    (parts,) = call(total, [((8, 56, 128), F32)], [VMEM], name="total", vmem=6 * MIB)(parts)
    parts = lax.all_to_all(parts, ("zh", "zm", "zl"), 0, 0, tiled=True)
    grads = call(finish, [((32, 72), F32)] * 3, [VMEM], name="finish", vmem=2 * MIB)(parts)
    return tuple(g.T for g in grads)


def solution(mesh):
    fine = Mesh(mesh.devices.reshape((2,) * 8), LAT + LON)
    tile = P(LAT, LON, None)
    return jax.shard_map(
        body,
        mesh=fine,
        in_specs=(tile, tile, P(), P(), P(), tile, P(LAT, LON)),
        out_specs=(P(LON, LAT),) * 3,
        check_vma=False,
    )
```

```python
import jax
import jax.numpy as jnp
from jax import lax
from jax.experimental import pallas as pl
from jax.experimental.pallas import tpu as pltpu
from jax.sharding import Mesh, PartitionSpec as P

F32 = jnp.float32
BF16 = jnp.bfloat16
C = 256
H, W = 48, 24
LH, LW = 16, 8
WW = 32
LWW = 16
LAT = ("yh", "yl", "xh")
LON = ("zh", "zm", "zl", "xl", "core")
SCALE = 2.0 / (H * W * H * W)
NINTH = 1.0 / 9.0
PK = 304
PAD = 8
MIB = 1024 * 1024
FULL = 60 * 1024 * 1024
MAIN_LIMIT = 64 * MIB - 12_000_000
VMEM = pl.BlockSpec(memory_space=pltpu.VMEM)
SMEM = pl.BlockSpec(memory_space=pltpu.SMEM)
HBM = pl.BlockSpec(memory_space=pltpu.HBM)


def up_matrix():
    def weight(m, r, cell):
        return jnp.where(
            r == 1,
            jnp.where(cell == m, 3.0, 0.0),
            jnp.where(cell == m, 2.0, jnp.where(cell == m + r - 1, 1.0, 0.0)),
        )

    p = lax.broadcasted_iota(jnp.int32, (18 * WW, 8 * LWW), 0)
    q = lax.broadcasted_iota(jnp.int32, (18 * WW, 8 * LWW), 1)
    i, j = p // WW, p % WW + 2
    e, f = q // LWW, q % LWW
    return (weight(i // 3 + 1, i % 3, e) * weight(j // 3 + 1, j % 3, f)).astype(BF16)


def down_matrix():
    def weight(tap):
        return jnp.maximum(3 - jnp.abs(tap - 2), 0).astype(F32)

    p = lax.broadcasted_iota(jnp.int32, (8 * LWW, 26 * WW), 0)
    q = lax.broadcasted_iota(jnp.int32, (8 * LWW, 26 * WW), 1)
    m, f = p // LWW, p % LWW - 3
    d, j = q // WW, q % WW - 3
    return jnp.where((f >= 0) & (f < LW), weight(d - 3 * m) * weight(j - 3 * f), 0.0).astype(BF16)


def pack_lon(land_ref, hi_ref, tgt_ref, low_ref, west_ref, east_ref, edge_ref, hi_v, tgt_v, low_v, sem):
    copies = [
        pltpu.make_async_copy(src.at[:, pl.ds(start, 8), :], dst.at[side], sem.at[2 * n + side])
        for n, (src, dst) in enumerate(((hi_ref, hi_v), (tgt_ref, tgt_v)))
        for side, start in enumerate((0, 16))
    ]
    copies.append(pltpu.make_async_copy(low_ref, low_v, sem.at[4]))
    for side in range(2):
        copies.append(pltpu.make_async_copy(hi_ref.at[pl.ds(44 * side, 4)], edge_ref.at[side, 0:4], sem.at[5 + side]))
        copies.append(pltpu.make_async_copy(tgt_ref.at[pl.ds(46 * side, 2)], edge_ref.at[side, 4:6], sem.at[7 + side]))
    for copy in copies:
        copy.start()
    land = land_ref[0, 0]
    sub = lax.broadcasted_iota(jnp.int32, (H, 8, C), 1)
    land_a = (land // 32).astype(F32)
    land_b = (land % 32).astype(F32)
    lands = jnp.where(sub == 6, land_a, land_b)
    for copy in copies:
        copy.wait()
    west = jnp.where(
        sub < 4, hi_v[0].astype(F32), jnp.where(sub < 6, pltpu.roll(tgt_v[0].astype(F32), 4, 1), lands)
    )
    east = jnp.where(
        sub < 4,
        pltpu.roll(hi_v[1].astype(F32), 4, 1),
        jnp.where(sub < 6, pltpu.roll(tgt_v[1].astype(F32), 6, 1), lands),
    )
    west_ref[0:H] = west.astype(BF16)
    east_ref[0:H] = east.astype(BF16)
    west_ref[H:] = low_v[...]
    east_ref[H:] = low_v[...]
    for side in range(2):
        edge_ref[side, 6] = low_v[13 * side : 13 * side + 3].astype(F32).reshape(24, C).astype(BF16)


def widen_pixels(own, left, right):
    turned = [pltpu.roll(own[:, 8 * g : 8 * g + 8], 4, 1) for g in range(3)]
    parts = [left] + turned + [right]
    low_half = lax.broadcasted_iota(jnp.int32, left.shape, 1) < 4
    return jnp.concatenate([jnp.where(low_half, parts[g], parts[g + 1]) for g in range(4)], axis=1)


def widen_hi(own, wpk, epk):
    return widen_pixels(own, wpk, pltpu.roll(epk, 4, 1))


def widen_tgt(own, wpk, epk):
    return widen_pixels(own, pltpu.roll(wpk, 6, 1), epk)


def widen_low(own, w_low, e_low):
    own, w_low, e_low = (pltpu.roll(v, 3, 1) for v in (own, w_low, e_low))
    head = lax.broadcasted_iota(jnp.int32, own.shape, 1) < 3
    return jnp.concatenate([jnp.where(head, w_low, own), jnp.where(head, own, e_low)], axis=1)


def land_row(part, own, wpk, epk):
    col = lax.broadcasted_iota(jnp.int32, (WW, C), 0)
    left = wpk[0, part : part + 1, :]
    right = epk[0, part : part + 1, :]
    return jnp.where(col < 4, left, jnp.where(col < 4 + W, own, right))


def pack_lat(land_ref, own_ref, w_ref, e_ref, north_ref, south_ref):
    land = land_ref[0, 0]
    wpk = w_ref[0:1].astype(F32)
    epk = e_ref[0:1].astype(F32)
    lands = jnp.concatenate(
        [
            land_row(6, (land // 32).astype(F32), wpk, epk),
            land_row(7, (land % 32).astype(F32), wpk, epk),
        ],
        axis=0,
    ).astype(BF16)
    for side, out_ref in enumerate((north_ref, south_ref)):
        def edge(ref, depth, size, base=0):
            start = base + (size - depth) * side
            return ref[start : start + depth].astype(F32)

        own = own_ref[side].astype(F32)
        hi = widen_hi(own[0:4], edge(w_ref, 4, H), edge(e_ref, 4, H))
        tgt = widen_tgt(own[4:6], edge(w_ref, 2, H), edge(e_ref, 2, H))
        low = widen_low(own[6].reshape(3, 8, C), edge(w_ref, 3, LH, H), edge(e_ref, 3, LH, H))
        out_ref[0:128] = hi.reshape(128, C).astype(BF16)
        out_ref[128:192] = tgt.reshape(64, C).astype(BF16)
        out_ref[192:240] = low.reshape(48, C).astype(BF16)
        out_ref[240:304] = lands


def main(
    pos_ref, land_ref, hi_hbm, tgt_hbm, low_hbm, w_ref, e_ref, n_ref, s_ref, kh_hbm, kl_hbm, kj_hbm,
    keep_ref, send_ref,
    x3_ref, j3_ref, o3_ref, l3_ref, f_ref, ha_ref, la_ref, jg_ref, og_ref, lg_ref, tg_ref, kt_ref, g_ref, up_ref,
    hi_v, tgt_v, low_v, kh_ref, kl_ref, kj_ref, sem, keep_sem,
):
    fetch = [
        pltpu.make_async_copy(src, dst, sem.at[n])
        for n, (src, dst) in enumerate(
            (
                (low_hbm, low_v),
                (kl_hbm, kl_ref),
                (hi_hbm, hi_v),
                (kh_hbm, kh_ref),
                (tgt_hbm, tgt_v),
                (kj_hbm, kj_ref),
            )
        )
    ]
    for copy in fetch:
        copy.start()
    fetch_low, fetch_kl, fetch_hi, fetch_kh, fetch_tgt, fetch_kj = fetch
    lat = pos_ref[0]
    core = pos_ref[1]
    first = lat == 0
    last = lat == 7

    def spread(dst, count, step):
        def one(t, _):
            s = pl.multiple_of(t * step, 16)
            v = f_ref[pl.ds(s, step + 2 * PAD), :]
            dst[pl.ds(s, step), 0:C] = v[PAD - 1 : PAD - 1 + step].astype(BF16)
            dst[pl.ds(s, step), C : 2 * C] = v[PAD : PAD + step].astype(BF16)
            dst[pl.ds(s, step), 2 * C : 3 * C] = v[PAD + 1 : PAD + 1 + step].astype(BF16)
            return 0

        lax.fori_loop(0, count // step, one, 0)

    def window(src, start, rows, stride):
        return jnp.concatenate(
            [src[pl.ds(pl.multiple_of(start + d * stride, 16), rows), :] for d in range(3)], axis=1
        )

    def zero_rows(start, rows):
        f_ref[PAD + start : PAD + start + rows, :] = jnp.zeros((rows, C), F32)

    f_ref[0:PAD, :] = jnp.zeros((PAD, C), F32)
    f_ref[PAD + 56 * WW :, :] = jnp.zeros((PAD, C), F32)
    f_ref[PAD : PAD + 48, :] = n_ref[192:240, :].astype(F32)
    fetch_low.wait()
    f_ref[PAD + 48 : PAD + 304, :] = widen_low(
        low_v[...].astype(F32), w_ref[H:].astype(F32), e_ref[H:].astype(F32)
    ).reshape(256, C)
    f_ref[PAD + 304 : PAD + 352, :] = s_ref[192:240, :].astype(F32)
    f_ref[PAD + 352 : PAD + 368, :] = jnp.zeros((16, C), F32)

    @pl.when(first)
    def _():
        zero_rows(0, 48)

    @pl.when(last)
    def _():
        zero_rows(304, 48)

    spread(l3_ref, 352, 176)
    fetch_kl.wait()
    low_act = jnp.maximum(
        jnp.dot(window(l3_ref, 0, 320, LWW), kl_ref[...], preferred_element_type=F32), 0.0
    ).astype(BF16)
    la_ref[...] = low_act

    @pl.when(first)
    def _():
        la_ref[0:32, :] = jnp.zeros((32, C), BF16)

    @pl.when(last)
    def _():
        la_ref[288:320, :] = jnp.zeros((32, C), BF16)

    f_ref[PAD : PAD + 128, :] = n_ref[0:128, :].astype(F32)
    f_ref[PAD + 1664 : PAD + 1792, :] = s_ref[0:128, :].astype(F32)

    fetch_hi.wait()

    def widen_rows(t, _):
        rows = pl.ds(pl.multiple_of(t * 8, 8), 8)
        wide = widen_hi(hi_v[rows].astype(F32), w_ref[rows].astype(F32), e_ref[rows].astype(F32))
        f_ref[pl.ds(pl.multiple_of(PAD + 128 + t * 256, 8), 256), :] = wide.reshape(256, C)
        return 0

    lax.fori_loop(0, 6, widen_rows, 0)

    @pl.when(first)
    def _():
        zero_rows(0, 128)

    @pl.when(last)
    def _():
        zero_rows(1664, 128)

    spread(x3_ref, 1792, 256)
    up_ref[...] = up_matrix()
    fetch_kh.wait()

    def high(b, _):
        s = pl.multiple_of(b * 576, 64)
        act = jnp.maximum(
            jnp.dot(window(x3_ref, s, 576, WW), kh_ref[...], preferred_element_type=F32), 0.0
        ).astype(BF16)
        ha_ref[pl.ds(s, 576), :] = act
        cells = la_ref[pl.ds(pl.multiple_of(b * 96, 32), 128), :]
        lift = jnp.dot(up_ref[...], cells, preferred_element_type=F32) * NINTH
        f_ref[pl.ds(PAD + s, 576), :] = act.astype(F32) + lift
        return 0

    lax.fori_loop(0, 3, high, 0)

    @pl.when(first)
    def _():
        zero_rows(0, 96)

    @pl.when(last)
    def _():
        zero_rows(51 * WW, 96)

    spread(j3_ref, 1728, 288)
    tg_ref[0:64, :] = n_ref[128:192, :]
    tg_ref[1600:1664, :] = s_ref[128:192, :]

    fetch_tgt.wait()

    def widen_targets(t, _):
        rows = pl.ds(pl.multiple_of(t * 8, 8), 8)
        wide = widen_tgt(tgt_v[rows].astype(F32), w_ref[rows].astype(F32), e_ref[rows].astype(F32))
        tg_ref[pl.ds(pl.multiple_of(64 + t * 256, 64), 256), :] = wide.reshape(256, C).astype(BF16)
        return 0

    lax.fori_loop(0, 6, widen_targets, 0)
    fetch_kj.wait()
    for tap in range(9):
        kt_ref[(8 - tap) * C : (9 - tap) * C, :] = kj_ref[tap * C : (tap + 1) * C, :].T

    def weight_of(ref, base):
        return (ref[base : base + 32, :].astype(F32) * 32.0 + ref[base + 32 : base + 64, :].astype(F32)) * SCALE

    top = weight_of(n_ref, 240)[None]
    own = land_ref[0, 0]
    wland = w_ref[0:1].astype(F32)
    eland = e_ref[0:1].astype(F32)
    mid_a = land_row(6, (own // 32).astype(F32), wland, eland)
    mid_b = land_row(7, (own % 32).astype(F32), wland, eland)
    mid = ((mid_a * 32.0 + mid_b) * SCALE)[None]
    bot = weight_of(s_ref, 240)[None]

    def join(b, _):
        s = pl.multiple_of(b * 416, 32)
        y = jnp.dot(window(j3_ref, s, 416, WW), kj_ref[...], preferred_element_type=F32)
        diff = (y - tg_ref[pl.ds(s, 416), :].astype(F32)).reshape(13, WW, C)
        row = lax.broadcasted_iota(jnp.int32, (13, WW, C), 0) + b * 13
        weight = jnp.where(row < 2, top, jnp.where(row >= 50, bot, mid))
        f_ref[pl.ds(PAD + s, 416), :] = (weight * diff).reshape(416, C)
        return 0

    lax.fori_loop(0, 4, join, 0)

    @pl.when(first)
    def _():
        zero_rows(0, 64)

    @pl.when(last)
    def _():
        zero_rows(50 * WW, 64)

    spread(o3_ref, 1664, 416)

    def own_columns(rows):
        col = lax.broadcasted_iota(jnp.int32, (rows // WW, WW, C), 1).reshape(rows, C)
        return (col >= 4) & (col < 4 + W)

    def contract(x_ref, g_val, base, stride, rows, slot):
        for d in range(3):
            g_ref[slot, d * 768 : (d + 1) * 768, :] = lax.dot_general(
                x_ref[base + d * stride : base + d * stride + rows, :],
                g_val,
                (((0,), (0,)), ((), ())),
                preferred_element_type=F32,
            )

        def one(t, _):
            pltpu.make_async_copy(
                g_ref.at[slot, pl.ds(block_start(t, core), 72)],
                keep_ref.at[pl.ds(pl.multiple_of(t * 224 + slot * 72, 8), 72)],
                keep_sem.at[slot],
            ).start()
            return 0

        lax.fori_loop(0, 16, one, 0)

    def block_start(t, half):
        return pl.multiple_of((t % 8 * 4 + t // 8 * 2 + half) * 72, 8)

    def own_grad(t, _):
        s = pl.multiple_of(t * 256, 64)
        v = f_ref[pl.ds(PAD + 64 + s, 256), :]
        og_ref[pl.ds(s, 256), :] = jnp.where(own_columns(256), v, 0.0).astype(BF16)
        return 0

    lax.fori_loop(0, 6, own_grad, 0)
    contract(j3_ref, og_ref[...], 64, WW, 1536, 2)

    def back(b, _):
        s = pl.multiple_of(b * 320, 32)
        y = jnp.dot(window(o3_ref, s, 320, WW), kt_ref[...], preferred_element_type=F32)
        jg_ref[pl.ds(s, 320), :] = y.astype(BF16)
        return 0

    lax.fori_loop(0, 5, back, 0)

    @pl.when(first)
    def _():
        jg_ref[0:32, :] = jnp.zeros((32, C), BF16)

    @pl.when(last)
    def _():
        jg_ref[49 * WW :, :] = jnp.zeros((32, C), BF16)

    def high_grad(t, _):
        s = pl.multiple_of(t * 256, 64)
        v = jg_ref[pl.ds(s + 32, 256), :].astype(F32)
        on = ha_ref[pl.ds(s + 96, 256), :].astype(F32) > 0
        og_ref[pl.ds(s, 256), :] = jnp.where(own_columns(256) & on, v, 0.0).astype(BF16)
        return 0

    lax.fori_loop(0, 6, high_grad, 0)
    contract(x3_ref, og_ref[...], 96, WW, 1536, 0)

    down = down_matrix()
    for b in range(2):
        lifted = jnp.dot(down, jg_ref[b * 768 : b * 768 + 832, :], preferred_element_type=F32) * NINTH
        on = la_ref[32 + b * 128 : 160 + b * 128, :].astype(F32) > 0
        lg_ref[b * 128 : (b + 1) * 128, :] = jnp.where(on, lifted, 0.0).astype(BF16)
    contract(l3_ref, lg_ref[...], 32, LWW, 256, 1)

    def split(t, _):
        src = block_start(t, 1 - core)
        block = jnp.concatenate(
            [g_ref[g, pl.ds(src, 72), :] for g in range(3)] + [jnp.zeros((8, C), F32)], axis=0
        )
        send_ref[pl.ds(pl.multiple_of(t * 224, 32), 224), :] = block.astype(BF16)
        return 0

    lax.fori_loop(0, 16, split, 0)
    for g in range(3):
        pltpu.make_async_copy(g_ref.at[g, 0:1152], keep_ref.at[0:1152], keep_sem.at[g]).wait()


def regroup_lanes(parts, rows):
    quarter = lax.broadcasted_iota(jnp.int32, (rows, 128), 1) // 32
    for q in range(4):
        out = None
        for g in range(4):
            shift = ((g - q) * 32) % 128
            turned = pltpu.roll(parts[g], shift, 1) if shift else parts[g]
            out = turned if out is None else jnp.where(quarter == g, turned, out)
        yield q, out


def merge(keep_ref, recv_ref, out_ref):
    def one(t, _):
        xl = t // 8
        z = t % 8
        s = pl.multiple_of(t * 224, 32)
        v = keep_ref[pl.ds(s, 224), :] + recv_ref[pl.ds(s, 224), :].astype(F32)
        for h in range(2):
            parts = [v[g * 56 : (g + 1) * 56, h * 128 : (h + 1) * 128] for g in range(4)]
            for q, out in regroup_lanes(parts, 56):
                out_ref[(h * 4 + q) * 2 + xl, z] = out.astype(BF16)
        return 0

    lax.fori_loop(0, 16, one, 0)


def total(in_ref, out_ref):
    def one(z, _):
        acc = in_ref[0, z].astype(F32)
        for i in range(1, 16):
            acc = acc + in_ref[i, z].astype(F32)
        out_ref[z] = acc.astype(out_ref.dtype)
        return 0

    lax.fori_loop(0, 8, one, 0)


def finish(in_ref, a_ref, b_ref, c_ref):
    acc = in_ref[0].astype(F32)
    for i in range(1, 8):
        acc = acc + in_ref[i].astype(F32)
    rows = jnp.concatenate(
        [acc if s == 0 else pltpu.roll(acc, 128 - 32 * s, 1) for s in range(4)], axis=0
    )
    for g, ref in enumerate((a_ref, b_ref, c_ref)):
        ref[...] = rows[g * 72 : (g + 1) * 72].T[0:32]


def call(kernel, out, specs, scratch=(), outs=None, name=None, vmem=None):
    return pl.pallas_call(
        kernel,
        out_shape=tuple(jax.ShapeDtypeStruct(s, d) for s, d in out),
        in_specs=list(specs),
        out_specs=outs or tuple(VMEM for _ in out),
        scratch_shapes=list(scratch),
        name=name,
        compiler_params=pltpu.CompilerParams(vmem_limit_bytes=vmem) if vmem else None,
    )


def ring(count, step):
    return [(i, (i + step) % count) for i in range(count)]


XY = ("yh", "yl", "xh", "xl")
Z = ("zh", "zm", "zl")


def body(hi, low, kh, kl, kj, tgt, land):
    dma = pltpu.SemaphoreType.DMA
    west, east, edges = call(
        pack_lon,
        [((H + LH, 8, C), BF16)] * 2 + [((2, 7, W, C), BF16)],
        [SMEM] + [HBM] * 3,
        [pltpu.VMEM((2, H, 8, C), BF16), pltpu.VMEM((2, H, 8, C), BF16), pltpu.VMEM((LH, LW, C), BF16), dma((9,))],
        name="pack_lon",
        vmem=FULL,
    )(land, hi, tgt, low)
    from_e = lax.ppermute(west, LON, ring(32, -1))
    from_w = lax.ppermute(east, LON, ring(32, 1))
    north, south = call(
        pack_lat, [((PK, C), BF16)] * 2, [SMEM] + [VMEM] * 3, name="pack_lat", vmem=6 * MIB
    )(land, edges, from_w, from_e)
    from_s = lax.ppermute(north, LAT, ring(8, -1))
    from_n = lax.ppermute(south, LAT, ring(8, 1))
    pos = jnp.stack([lax.axis_index(LAT), lax.axis_index("core")]).astype(jnp.int32)
    keep, send = call(
        main,
        [((3584, C), F32), ((3584, C), BF16)],
        [SMEM] * 2 + [HBM] * 3 + [VMEM] * 4 + [HBM] * 3,
        [
            pltpu.VMEM((1792, 768), BF16),
            pltpu.VMEM((1728, 768), BF16),
            pltpu.VMEM((1664, 768), BF16),
            pltpu.VMEM((352, 768), BF16),
            pltpu.VMEM((1792 + 2 * PAD, C), F32),
            pltpu.VMEM((1728, C), BF16),
            pltpu.VMEM((320, C), BF16),
            pltpu.VMEM((1600, C), BF16),
            pltpu.VMEM((1536, C), BF16),
            pltpu.VMEM((256, C), BF16),
            pltpu.VMEM((1664, C), BF16),
            pltpu.VMEM((2304, C), BF16),
            pltpu.VMEM((3, 2304, C), F32),
            pltpu.VMEM((576, 128), BF16),
            pltpu.VMEM((H, W, C), BF16),
            pltpu.VMEM((H, W, C), BF16),
            pltpu.VMEM((LH, LW, C), BF16),
            pltpu.VMEM((2304, C), BF16),
            pltpu.VMEM((2304, C), BF16),
            pltpu.VMEM((2304, C), BF16),
            dma((6,)),
            dma((3,)),
        ],
        outs=(HBM, VMEM),
        name="main",
        vmem=MAIN_LIMIT,
    )(
        pos, land, hi, tgt, low, from_w, from_e, from_n, from_s,
        kh.reshape(9 * C, C), kl.reshape(9 * C, C), kj.reshape(9 * C, C),
    )
    recv = lax.ppermute(send, "core", ring(2, 1))
    (parts,) = call(merge, [((16, 8, 56, 128), BF16)], [VMEM] * 2, name="merge", vmem=12 * MIB)(keep, recv)
    parts = lax.all_to_all(parts, XY, 0, 0, tiled=True)
    (parts,) = call(total, [((8, 56, 128), F32)], [VMEM], name="total", vmem=6 * MIB)(parts)
    parts = lax.all_to_all(parts, Z, 0, 0, tiled=True)
    grads = call(finish, [((32, 72), F32)] * 3, [VMEM], name="finish", vmem=2 * MIB)(parts)
    return tuple(g.T for g in grads)


def solution(mesh):
    fine = Mesh(mesh.devices.reshape((2,) * 8), LAT + LON)
    tile = P(LAT, LON, None)
    return jax.shard_map(
        body,
        mesh=fine,
        in_specs=(tile, tile, P(), P(), P(), tile, P(LAT, LON)),
        out_specs=(P(LON, LAT),) * 3,
        check_vma=False,
    )
```

```python
import jax
import jax.numpy as jnp
from jax import lax
from jax.experimental import pallas as pl
from jax.experimental.pallas import tpu as pltpu
from jax.sharding import Mesh, PartitionSpec as P

F32 = jnp.float32
BF16 = jnp.bfloat16
C = 256
H, W = 48, 24
LH, LW = 16, 8
WW = 32
LWW = 16
LAT = ("yh", "yl", "xh")
LON = ("zh", "zm", "zl", "xl", "core")
SCALE = 2.0 / (H * W * H * W)
NINTH = 1.0 / 9.0
PK = 304
MIB = 1024 * 1024
FULL = 60 * 1024 * 1024
MAIN_LIMIT = 64 * MIB - 12_000_000
JOIN_LIMIT = 64 * MIB - 12_300_000
REST_LIMIT = 64 * MIB - 13_500_000
VMEM = pl.BlockSpec(memory_space=pltpu.VMEM)
SMEM = pl.BlockSpec(memory_space=pltpu.SMEM)
HBM = pl.BlockSpec(memory_space=pltpu.HBM)


def up_matrix():
    def weight(m, r, cell):
        side = jnp.where(cell == m, 2.0, jnp.where(cell == m + r - 1, 1.0, 0.0))
        return jnp.where(r == 1, jnp.where(cell == m, 3.0, 0.0), side)

    i = lax.broadcasted_iota(jnp.int32, (18, 1, 8 * LWW), 0)
    e = lax.broadcasted_iota(jnp.int32, (18, 1, 8 * LWW), 2) // LWW
    j = lax.broadcasted_iota(jnp.int32, (1, WW, 8 * LWW), 1) + 2
    f = lax.broadcasted_iota(jnp.int32, (1, WW, 8 * LWW), 2) % LWW
    both = weight(i // 3 + 1, i % 3, e) * weight(j // 3 + 1, j % 3, f)
    return both.reshape(18 * WW, 8 * LWW).astype(BF16)


def down_matrix():
    def weight(tap):
        return jnp.maximum(3 - jnp.abs(tap - 2), 0).astype(F32)

    m = lax.broadcasted_iota(jnp.int32, (8, 1, 26 * WW), 0)
    d = lax.broadcasted_iota(jnp.int32, (8, 1, 26 * WW), 2) // WW
    f = lax.broadcasted_iota(jnp.int32, (1, LWW, 26 * WW), 1) - 3
    j = lax.broadcasted_iota(jnp.int32, (1, LWW, 26 * WW), 2) % WW - 3
    both = weight(d - 3 * m) * jnp.where((f >= 0) & (f < LW), weight(j - 3 * f), 0.0)
    return both.reshape(8 * LWW, 26 * WW).astype(BF16)


def pack_lon(land_ref, hi_ref, tgt_ref, low_ref, west_ref, east_ref, edge_ref, hi_v, tgt_v, low_v, sem):
    copies = [
        pltpu.make_async_copy(src.at[:, pl.ds(start, 8), :], dst.at[side], sem.at[2 * n + side])
        for n, (src, dst) in enumerate(((hi_ref, hi_v), (tgt_ref, tgt_v)))
        for side, start in enumerate((0, 16))
    ]
    copies.append(pltpu.make_async_copy(low_ref, low_v, sem.at[4]))
    for side in range(2):
        copies.append(pltpu.make_async_copy(hi_ref.at[pl.ds(44 * side, 4)], edge_ref.at[side, 0:4], sem.at[5 + side]))
        copies.append(pltpu.make_async_copy(tgt_ref.at[pl.ds(46 * side, 2)], edge_ref.at[side, 4:6], sem.at[7 + side]))
    for copy in copies:
        copy.start()
    land = land_ref[0, 0]
    sub = lax.broadcasted_iota(jnp.int32, (H, 8, C), 1)
    land_a = (land // 32).astype(F32)
    land_b = (land % 32).astype(F32)
    lands = jnp.where(sub == 6, land_a, land_b)
    for copy in copies:
        copy.wait()
    west = jnp.where(
        sub < 4, hi_v[0].astype(F32), jnp.where(sub < 6, pltpu.roll(tgt_v[0].astype(F32), 4, 1), lands)
    )
    east = jnp.where(
        sub < 4,
        pltpu.roll(hi_v[1].astype(F32), 4, 1),
        jnp.where(sub < 6, pltpu.roll(tgt_v[1].astype(F32), 6, 1), lands),
    )
    west_ref[0:H] = west.astype(BF16)
    east_ref[0:H] = east.astype(BF16)
    west_ref[H:] = low_v[...]
    east_ref[H:] = low_v[...]
    for side in range(2):
        edge_ref[side, 6] = low_v[13 * side : 13 * side + 3].astype(F32).reshape(24, C).astype(BF16)


def widen_pixels(own, left, right):
    turned = [pltpu.roll(own[:, 8 * g : 8 * g + 8], 4, 1) for g in range(3)]
    parts = [left] + turned + [right]
    low_half = lax.broadcasted_iota(jnp.int32, left.shape, 1) < 4
    return jnp.concatenate([jnp.where(low_half, parts[g], parts[g + 1]) for g in range(4)], axis=1)


def widen_hi(own, wpk, epk):
    return widen_pixels(own, wpk, pltpu.roll(epk, 4, 1))


def widen_tgt(own, wpk, epk):
    return widen_pixels(own, pltpu.roll(wpk, 6, 1), epk)


def widen_low(own, w_low, e_low):
    own, w_low, e_low = (pltpu.roll(v, 3, 1) for v in (own, w_low, e_low))
    head = lax.broadcasted_iota(jnp.int32, own.shape, 1) < 3
    return jnp.concatenate([jnp.where(head, w_low, own), jnp.where(head, own, e_low)], axis=1)


def land_row(part, own, wpk, epk):
    col = lax.broadcasted_iota(jnp.int32, (WW, C), 0)
    left = wpk[0, part : part + 1, :]
    right = epk[0, part : part + 1, :]
    return jnp.where(col < 4, left, jnp.where(col < 4 + W, own, right))


def pack_lat(land_ref, own_ref, w_ref, e_ref, north_ref, south_ref):
    land = land_ref[0, 0]
    wpk = w_ref[0:1].astype(F32)
    epk = e_ref[0:1].astype(F32)
    lands = jnp.concatenate(
        [
            land_row(6, (land // 32).astype(F32), wpk, epk),
            land_row(7, (land % 32).astype(F32), wpk, epk),
        ],
        axis=0,
    ).astype(BF16)
    for side, out_ref in enumerate((north_ref, south_ref)):
        def edge(ref, depth, size, base=0):
            start = base + (size - depth) * side
            return ref[start : start + depth].astype(F32)

        own = own_ref[side].astype(F32)
        hi = widen_hi(own[0:4], edge(w_ref, 4, H), edge(e_ref, 4, H))
        tgt = widen_tgt(own[4:6], edge(w_ref, 2, H), edge(e_ref, 2, H))
        low = widen_low(own[6].reshape(3, 8, C), edge(w_ref, 3, LH, H), edge(e_ref, 3, LH, H))
        out_ref[0:128] = hi.reshape(128, C).astype(BF16)
        out_ref[128:192] = tgt.reshape(64, C).astype(BF16)
        out_ref[192:240] = low.reshape(48, C).astype(BF16)
        out_ref[240:304] = lands


def put3(dst, start, v):
    rows = v.shape[0]
    dst[pl.ds(start, rows), 0:C] = pltpu.roll(v, 1, 0).astype(BF16)
    dst[pl.ds(start, rows), C : 2 * C] = v.astype(BF16)
    dst[pl.ds(start, rows), 2 * C : 3 * C] = pltpu.roll(v, rows - 1, 0).astype(BF16)


def window(src, start, rows, stride):
    return jnp.concatenate(
        [src[pl.ds(pl.multiple_of(start + d * stride, 16), rows), :] for d in range(3)], axis=1
    )


def own_columns(rows):
    col = lax.broadcasted_iota(jnp.int32, (rows // WW, WW, C), 1).reshape(rows, C)
    return (col >= 4) & (col < 4 + W)


def zero_at(flag, ref, start, rows):
    @pl.when(flag)
    def _():
        ref[start : start + rows, :] = jnp.zeros((rows, ref.shape[1]), ref.dtype)


def contract(x_ref, g_val, base, stride, rows, out):
    for d in range(3):
        out[d * 768 : (d + 1) * 768, :] = lax.dot_general(
            x_ref[base + d * stride : base + d * stride + rows, :],
            g_val,
            (((0,), (0,)), ((), ())),
            preferred_element_type=F32,
        )


def block_start(t, half):
    return pl.multiple_of((t % 8 * 4 + t // 8 * 2 + half) * 72, 8)


def hand_out(g_ref, keep_ref, send_ref, core, sem):
    for t in range(16):
        pltpu.make_async_copy(g_ref.at[pl.ds(block_start(t, core), 72)], keep_ref.at[t], sem).start()

    def one(t, _):
        send_ref[t] = g_ref[pl.ds(block_start(t, 1 - core), 72), :].astype(BF16)
        return 0

    lax.fori_loop(0, 16, one, 0)


def wait_out(src, dst, sem):
    pltpu.make_async_copy(src, dst, sem).wait()


def forward(
    pos_ref, land_ref, hi_hbm, tgt_hbm, low_hbm, w_ref, e_ref, n_ref, s_ref, kh_hbm, kl_hbm, kj_hbm,
    keep_ref, send_ref, x3_hbm, o3_hbm, l3_hbm, ha_hbm, la_hbm,
    x3_ref, j3_ref, o3_ref, l3_ref, ha_ref, la_ref, og_ref, tg_ref, g_ref, up_ref,
    hi_v, tgt_v, low_v, kh_ref, kl_ref, kj_ref, sem, out_sem, keep_sem,
):
    fetch = [
        pltpu.make_async_copy(src, dst, sem.at[n])
        for n, (src, dst) in enumerate(
            (
                (low_hbm, low_v),
                (hi_hbm, hi_v),
                (kl_hbm, kl_ref),
                (kh_hbm, kh_ref),
                (tgt_hbm, tgt_v),
                (kj_hbm, kj_ref),
            )
        )
    ]
    for copy in fetch:
        copy.start()
    fetch_low, fetch_hi, fetch_kl, fetch_kh, fetch_tgt, fetch_kj = fetch
    leave = [
        pltpu.make_async_copy(src, dst, out_sem.at[n])
        for n, (src, dst) in enumerate(
            ((x3_ref, x3_hbm), (o3_ref, o3_hbm), (l3_ref, l3_hbm), (ha_ref, ha_hbm), (la_ref, la_hbm))
        )
    ]
    leave_x3, leave_o3, leave_l3, leave_ha, leave_la = leave
    first = pos_ref[0] == 0
    last = pos_ref[0] == 7
    core = pos_ref[1]
    up_ref[...] = up_matrix()

    put3(l3_ref, 0, n_ref[192:240, :].astype(F32))
    put3(l3_ref, 304, s_ref[192:240, :].astype(F32))
    put3(x3_ref, 0, n_ref[0:128, :].astype(F32))
    put3(x3_ref, 1664, s_ref[0:128, :].astype(F32))
    zero_at(first, l3_ref, 0, 48)
    zero_at(last, l3_ref, 304, 48)
    zero_at(first, x3_ref, 0, 128)
    zero_at(last, x3_ref, 1664, 128)
    fetch_low.wait()
    put3(
        l3_ref,
        48,
        widen_low(low_v[...].astype(F32), w_ref[H:].astype(F32), e_ref[H:].astype(F32)).reshape(256, C),
    )
    leave_l3.start()
    fetch_hi.wait()

    def widen_rows(t, _):
        rows = pl.ds(pl.multiple_of(t * 8, 8), 8)
        wide = widen_hi(hi_v[rows].astype(F32), w_ref[rows].astype(F32), e_ref[rows].astype(F32))
        put3(x3_ref, pl.multiple_of(128 + t * 256, 128), wide.reshape(256, C))
        return 0

    lax.fori_loop(0, 6, widen_rows, 0)
    leave_x3.start()
    fetch_kl.wait()
    la_ref[...] = jnp.maximum(
        jnp.dot(window(l3_ref, 0, 320, LWW), kl_ref[...], preferred_element_type=F32), 0.0
    ).astype(BF16)
    zero_at(first, la_ref, 0, 32)
    zero_at(last, la_ref, 288, 32)
    leave_la.start()
    fetch_kh.wait()

    def high(b, _):
        s = pl.multiple_of(b * 576, 64)
        act = jnp.maximum(
            jnp.dot(window(x3_ref, s, 576, WW), kh_ref[...], preferred_element_type=F32), 0.0
        ).astype(BF16)
        ha_ref[pl.ds(s, 576), :] = act
        cells = la_ref[pl.ds(pl.multiple_of(b * 96, 32), 128), :]
        lift = jnp.dot(up_ref[...], cells, preferred_element_type=F32) * NINTH
        put3(j3_ref, s, act.astype(F32) + lift)
        return 0

    lax.fori_loop(0, 3, high, 0)
    leave_ha.start()
    zero_at(first, j3_ref, 0, 96)
    zero_at(last, j3_ref, 51 * WW, 96)
    tg_ref[0:64, :] = n_ref[128:192, :]
    tg_ref[1600:1664, :] = s_ref[128:192, :]
    fetch_tgt.wait()

    def widen_targets(t, _):
        rows = pl.ds(pl.multiple_of(t * 8, 8), 8)
        wide = widen_tgt(tgt_v[rows].astype(F32), w_ref[rows].astype(F32), e_ref[rows].astype(F32))
        tg_ref[pl.ds(pl.multiple_of(64 + t * 256, 64), 256), :] = wide.reshape(256, C).astype(BF16)
        return 0

    lax.fori_loop(0, 6, widen_targets, 0)
    fetch_kj.wait()

    def weight_of(high_part, low_part):
        return ((high_part * 32.0 + low_part) * SCALE)[None]

    own = land_ref[0, 0]
    wland = w_ref[0:1].astype(F32)
    eland = e_ref[0:1].astype(F32)
    top = weight_of(n_ref[240:272, :].astype(F32), n_ref[272:304, :].astype(F32))
    mid = weight_of(
        land_row(6, (own // 32).astype(F32), wland, eland), land_row(7, (own % 32).astype(F32), wland, eland)
    )
    bot = weight_of(s_ref[240:272, :].astype(F32), s_ref[272:304, :].astype(F32))

    def join(b, _):
        s = pl.multiple_of(b * 416, 32)
        y = jnp.dot(window(j3_ref, s, 416, WW), kj_ref[...], preferred_element_type=F32)
        diff = (y - tg_ref[pl.ds(s, 416), :].astype(F32)).reshape(13, WW, C)
        row = lax.broadcasted_iota(jnp.int32, (13, WW, C), 0) + b * 13
        weight = jnp.where(row < 2, top, jnp.where(row >= 50, bot, mid))
        grad = (weight * diff).reshape(416, C)
        put3(o3_ref, s, grad)
        og_ref[pl.ds(s, 416), :] = jnp.where(own_columns(416), grad, 0.0).astype(BF16)
        return 0

    lax.fori_loop(0, 4, join, 0)
    zero_at(first, o3_ref, 0, 64)
    zero_at(last, o3_ref, 50 * WW, 64)
    leave_o3.start()
    contract(j3_ref, og_ref[64:1600, :], 64, WW, 1536, g_ref)
    hand_out(g_ref, keep_ref, send_ref, core, keep_sem)
    for copy in leave:
        copy.wait()
    wait_out(g_ref.at[0:1152], keep_ref.at[:], keep_sem)


def backward(
    pos_ref, x3_hbm, o3_hbm, l3_hbm, ha_hbm, la_hbm, kj_hbm,
    keep_ref, send_ref,
    x3_ref, o3_ref, l3_ref, ha_ref, la_ref, jg_ref, hg_ref, lg_ref, kj_ref, kt_ref, g_ref, sem, keep_sem,
):
    fetch = [
        pltpu.make_async_copy(src, dst, sem.at[n])
        for n, (src, dst) in enumerate(
            (
                (kj_hbm, kj_ref),
                (o3_hbm, o3_ref),
                (ha_hbm, ha_ref),
                (x3_hbm, x3_ref),
                (la_hbm, la_ref),
                (l3_hbm, l3_ref),
            )
        )
    ]
    for copy in fetch:
        copy.start()
    fetch_kj, fetch_o3, fetch_ha, fetch_x3, fetch_la, fetch_l3 = fetch
    first = pos_ref[0] == 0
    last = pos_ref[0] == 7
    core = pos_ref[1]
    fetch_kj.wait()
    for tap in range(9):
        kt_ref[(8 - tap) * C : (9 - tap) * C, :] = kj_ref[tap * C : (tap + 1) * C, :].T
    fetch_o3.wait()
    fetch_ha.wait()

    def back(b, _):
        s = pl.multiple_of(b * 320, 32)
        y = jnp.dot(window(o3_ref, s, 320, WW), kt_ref[...], preferred_element_type=F32)
        jg_ref[pl.ds(s, 320), :] = y.astype(BF16)
        on = ha_ref[pl.ds(pl.multiple_of(s + 64, 32), 320), :].astype(F32) > 0
        hg_ref[pl.ds(s, 320), :] = jnp.where(own_columns(320) & on, y, 0.0).astype(BF16)
        return 0

    lax.fori_loop(0, 5, back, 0)
    zero_at(first, jg_ref, 0, 32)
    zero_at(last, jg_ref, 49 * WW, 32)
    fetch_la.wait()
    fetch_l3.wait()
    fetch_x3.wait()
    contract(x3_ref, hg_ref[32:1568, :], 96, WW, 1536, g_ref.at[0])
    hand_out(g_ref.at[0], keep_ref.at[0], send_ref.at[0], core, keep_sem.at[0])
    down = down_matrix()
    for b in range(2):
        lifted = jnp.dot(down, jg_ref[b * 768 : b * 768 + 832, :], preferred_element_type=F32) * NINTH
        on = la_ref[32 + b * 128 : 160 + b * 128, :].astype(F32) > 0
        lg_ref[b * 128 : (b + 1) * 128, :] = jnp.where(on, lifted, 0.0).astype(BF16)
    contract(l3_ref, lg_ref[...], 32, LWW, 256, g_ref.at[1])
    hand_out(g_ref.at[1], keep_ref.at[1], send_ref.at[1], core, keep_sem.at[1])
    for n in range(2):
        wait_out(g_ref.at[n, 0:1152], keep_ref.at[n], keep_sem.at[n])


def regroup_lanes(parts, rows):
    quarter = lax.broadcasted_iota(jnp.int32, (rows, 128), 1) // 32
    for q in range(4):
        out = None
        for g in range(4):
            shift = ((g - q) * 32) % 128
            turned = pltpu.roll(parts[g], shift, 1) if shift else parts[g]
            out = turned if out is None else jnp.where(quarter == g, turned, out)
        yield q, out


def merge(keep_hbm, recv_ref, out_ref, keep_ref, sem):
    copies = [pltpu.make_async_copy(keep_hbm.at[n], keep_ref.at[n], sem.at[n]) for n in range(keep_ref.shape[0])]
    for copy in copies:
        copy.start()
    for n, copy in enumerate(copies):
        copy.wait()

        def one(t, _):
            xl = t // 2
            p = t % 2
            blocks = []
            for g in range(4):
                at = xl * 8 + 2 * g + p
                blocks.append(keep_ref[n, at] + recv_ref[n, at].astype(F32))
            for h in range(2):
                parts = [v[:, h * 128 : (h + 1) * 128] for v in blocks]
                for q, out in regroup_lanes(parts, 72):
                    out_ref[(h * 4 + q) * 2 + xl, n * 2 + p] = out.astype(BF16)
            return 0

        lax.fori_loop(0, 4, one, 0)


def total(join_ref, rest_ref, out_ref):
    quarter = lax.broadcasted_iota(jnp.int32, (56, 128), 1) // 32
    for p in range(2):
        sums = []
        for ref, n in ((rest_ref, p), (rest_ref, 2 + p), (join_ref, p)):
            acc = ref[0, n].astype(F32)
            for i in range(1, 16):
                acc = acc + ref[i, n].astype(F32)
            sums.append(acc)
        rows = jnp.concatenate(sums + [jnp.zeros((8, 128), F32)], axis=0)
        for g in range(4):
            out = None
            for s in range(4):
                shift = ((s - g) * 32) % 128
                part = rows[s * 56 : (s + 1) * 56]
                turned = pltpu.roll(part, shift, 1) if shift else part
                out = turned if out is None else jnp.where(quarter == s, turned, out)
            out_ref[2 * g + p] = out


def finish(in_ref, a_ref, b_ref, c_ref):
    acc = in_ref[0].astype(F32)
    for i in range(1, 8):
        acc = acc + in_ref[i].astype(F32)
    rows = jnp.concatenate(
        [acc if s == 0 else pltpu.roll(acc, 128 - 32 * s, 1) for s in range(4)], axis=0
    )
    for g, ref in enumerate((a_ref, b_ref, c_ref)):
        ref[...] = rows[g * 72 : (g + 1) * 72].T[0:32]


def call(kernel, out, specs, scratch=(), outs=None, vmem=None):
    return pl.pallas_call(
        kernel,
        out_shape=tuple(jax.ShapeDtypeStruct(s, d) for s, d in out),
        in_specs=list(specs),
        out_specs=outs or tuple(VMEM for _ in out),
        scratch_shapes=list(scratch),
        compiler_params=pltpu.CompilerParams(vmem_limit_bytes=vmem) if vmem else None,
    )


def ring(count, step):
    return [(i, (i + step) % count) for i in range(count)]


XY = ("yh", "yl", "xh", "xl")
Z = ("zh", "zm", "zl")


def step(hi, low, kh, kl, kj, tgt, land):
    dma = pltpu.SemaphoreType.DMA
    west, east, edges = call(
        pack_lon,
        [((H + LH, 8, C), BF16)] * 2 + [((2, 7, W, C), BF16)],
        [SMEM] + [HBM] * 3,
        [pltpu.VMEM((2, H, 8, C), BF16), pltpu.VMEM((2, H, 8, C), BF16), pltpu.VMEM((LH, LW, C), BF16), dma((9,))],
        vmem=FULL,
    )(land, hi, tgt, low)
    from_e = lax.ppermute(west, LON, ring(32, -1))
    from_w = lax.ppermute(east, LON, ring(32, 1))
    north, south = call(pack_lat, [((PK, C), BF16)] * 2, [SMEM] + [VMEM] * 3, vmem=6 * MIB)(land, edges, from_w, from_e)
    from_s = lax.ppermute(north, LAT, ring(8, -1))
    from_n = lax.ppermute(south, LAT, ring(8, 1))
    pos = jnp.stack([lax.axis_index(LAT), lax.axis_index("core")]).astype(jnp.int32)
    weights = [k.reshape(9 * C, C) for k in (kh, kl, kj)]
    stored = [((1792, 768), BF16), ((1664, 768), BF16), ((352, 768), BF16), ((1728, C), BF16), ((320, C), BF16)]
    x3, o3, l3, ha, la = (pltpu.VMEM(*one) for one in stored)
    keep_join, send_join, *saved = call(
        forward,
        [((16, 72, C), F32), ((16, 72, C), BF16)] + stored,
        [SMEM] * 2 + [HBM] * 3 + [VMEM] * 4 + [HBM] * 3,
        [
            x3, pltpu.VMEM((1728, 768), BF16), o3, l3, ha, la,
            pltpu.VMEM((1664, C), BF16),
            pltpu.VMEM((1664, C), BF16),
            pltpu.VMEM((2304, C), F32),
            pltpu.VMEM((576, 128), BF16),
            pltpu.VMEM((H, W, C), BF16),
            pltpu.VMEM((H, W, C), BF16),
            pltpu.VMEM((LH, LW, C), BF16),
            pltpu.VMEM((2304, C), BF16),
            pltpu.VMEM((2304, C), BF16),
            pltpu.VMEM((2304, C), BF16),
            dma((6,)),
            dma((5,)),
            dma(()),
        ],
        outs=(HBM, VMEM) + (HBM,) * 5,
        vmem=MAIN_LIMIT,
    )(pos, land, hi, tgt, low, from_w, from_e, from_n, from_s, *weights)
    recv_join = lax.ppermute(send_join, "core", ring(2, 1))
    keep_rest, send_rest = call(
        backward,
        [((2, 16, 72, C), F32), ((2, 16, 72, C), BF16)],
        [SMEM] + [HBM] * 6,
        [
            x3, o3, l3, ha, la,
            pltpu.VMEM((1600, C), BF16),
            pltpu.VMEM((1600, C), BF16),
            pltpu.VMEM((256, C), BF16),
            pltpu.VMEM((2304, C), BF16),
            pltpu.VMEM((2304, C), BF16),
            pltpu.VMEM((2, 2304, C), F32),
            dma((6,)),
            dma((2,)),
        ],
        outs=(HBM, VMEM),
        vmem=FULL,
    )(pos, *saved, weights[2])

    def merged(keep, recv, count, limit):
        (out,) = call(
            merge,
            [((16, 2 * count, 72, 128), BF16)],
            [HBM, VMEM],
            [pltpu.VMEM((count, 16, 72, C), F32), dma((count,))],
            vmem=limit,
        )(keep, recv)
        return out

    parts_join = merged(keep_join[None], recv_join[None], 1, JOIN_LIMIT)
    parts_join = lax.all_to_all(parts_join, XY, 0, 0, tiled=True)
    recv_rest = lax.ppermute(send_rest, "core", ring(2, 1))
    parts_rest = merged(keep_rest, recv_rest, 2, REST_LIMIT)
    parts_rest = lax.all_to_all(parts_rest, XY, 0, 0, tiled=True)
    (parts,) = call(total, [((8, 56, 128), F32)], [VMEM] * 2, vmem=6 * MIB)(parts_join, parts_rest)
    parts = lax.all_to_all(parts, Z, 0, 0, tiled=True)
    grads = call(finish, [((32, 72), F32)] * 3, [VMEM], vmem=2 * MIB)(parts)
    return tuple(g.T for g in grads)


def solution(mesh):
    fine = Mesh(mesh.devices.reshape((2,) * 8), LAT + LON)
    tile = P(LAT, LON, None)
    return jax.shard_map(
        step,
        mesh=fine,
        in_specs=(tile, tile, P(), P(), P(), tile, P(LAT, LON)),
        out_specs=(P(LON, LAT),) * 3,
        check_vma=False,
    )
```

```python
import jax
import jax.numpy as jnp
from jax import lax
from jax.experimental import pallas as pl
from jax.experimental.pallas import tpu as pltpu
from jax.sharding import Mesh, PartitionSpec as P

F32 = jnp.float32
BF16 = jnp.bfloat16
C = 256
H, W = 48, 24
LH, LW = 16, 8
WW = 32
LWW = 16
LAT = ("yh", "yl", "xh")
LON = ("zh", "zm", "zl", "xl", "core")
SCALE = 2.0 / (H * W * H * W)
NINTH = 1.0 / 9.0
PK = 304
MIB = 1024 * 1024
FULL = 60 * 1024 * 1024
MAIN_LIMIT = 64 * MIB - 12_000_000
MERGE_LIMIT = 64 * MIB - 15_500_000
VMEM = pl.BlockSpec(memory_space=pltpu.VMEM)
SMEM = pl.BlockSpec(memory_space=pltpu.SMEM)
HBM = pl.BlockSpec(memory_space=pltpu.HBM)


def up_matrix():
    def weight(m, r, cell):
        side = jnp.where(cell == m, 2.0, jnp.where(cell == m + r - 1, 1.0, 0.0))
        return jnp.where(r == 1, jnp.where(cell == m, 3.0, 0.0), side)

    i = lax.broadcasted_iota(jnp.int32, (18, 1, 8 * LWW), 0)
    e = lax.broadcasted_iota(jnp.int32, (18, 1, 8 * LWW), 2) // LWW
    j = lax.broadcasted_iota(jnp.int32, (1, WW, 8 * LWW), 1) + 2
    f = lax.broadcasted_iota(jnp.int32, (1, WW, 8 * LWW), 2) % LWW
    both = weight(i // 3 + 1, i % 3, e) * weight(j // 3 + 1, j % 3, f)
    return both.reshape(18 * WW, 8 * LWW).astype(BF16)


def down_matrix():
    def weight(tap):
        return jnp.maximum(3 - jnp.abs(tap - 2), 0).astype(F32)

    m = lax.broadcasted_iota(jnp.int32, (8, 1, 26 * WW), 0)
    d = lax.broadcasted_iota(jnp.int32, (8, 1, 26 * WW), 2) // WW
    f = lax.broadcasted_iota(jnp.int32, (1, LWW, 26 * WW), 1) - 3
    j = lax.broadcasted_iota(jnp.int32, (1, LWW, 26 * WW), 2) % WW - 3
    both = weight(d - 3 * m) * jnp.where((f >= 0) & (f < LW), weight(j - 3 * f), 0.0)
    return both.reshape(8 * LWW, 26 * WW).astype(BF16)


def pack_lon(land_ref, hi_ref, tgt_ref, low_ref, west_ref, east_ref, edge_ref, hi_v, tgt_v, low_v, sem):
    copies = [
        pltpu.make_async_copy(src.at[:, pl.ds(start, 8), :], dst.at[side], sem.at[2 * n + side])
        for n, (src, dst) in enumerate(((hi_ref, hi_v), (tgt_ref, tgt_v)))
        for side, start in enumerate((0, 16))
    ]
    copies.append(pltpu.make_async_copy(low_ref, low_v, sem.at[4]))
    for side in range(2):
        copies.append(pltpu.make_async_copy(hi_ref.at[pl.ds(44 * side, 4)], edge_ref.at[side, 0:4], sem.at[5 + side]))
        copies.append(pltpu.make_async_copy(tgt_ref.at[pl.ds(46 * side, 2)], edge_ref.at[side, 4:6], sem.at[7 + side]))
    for copy in copies:
        copy.start()
    land = land_ref[0, 0]
    sub = lax.broadcasted_iota(jnp.int32, (H, 8, C), 1)
    row = lax.broadcasted_iota(jnp.int32, (H, 8, C), 0)
    lands = jnp.where(row % 2 == 0, (land // 32).astype(F32), (land % 32).astype(F32))
    for copy in copies:
        copy.wait()
    low = low_v[...].astype(F32)

    def rest(start):
        cells = jnp.stack([pltpu.roll(low, (7 - start - b) % 8, 1) for b in range(3)], axis=1)
        return jnp.where(sub == 6, lands, cells.reshape(H, 8, C))

    west = jnp.where(
        sub < 4, hi_v[0].astype(F32), jnp.where(sub < 6, pltpu.roll(tgt_v[0].astype(F32), 4, 1), rest(0))
    )
    east = jnp.where(
        sub < 4,
        pltpu.roll(hi_v[1].astype(F32), 4, 1),
        jnp.where(sub < 6, pltpu.roll(tgt_v[1].astype(F32), 6, 1), rest(5)),
    )
    west_ref[...] = west.astype(BF16)
    east_ref[...] = east.astype(BF16)
    for side in range(2):
        edge_ref[side, 6] = low_v[13 * side : 13 * side + 3].astype(F32).reshape(24, C).astype(BF16)


def widen_pixels(own, left, right):
    turned = [pltpu.roll(own[:, 8 * g : 8 * g + 8], 4, 1) for g in range(3)]
    parts = [left] + turned + [right]
    low_half = lax.broadcasted_iota(jnp.int32, left.shape, 1) < 4
    return jnp.concatenate([jnp.where(low_half, parts[g], parts[g + 1]) for g in range(4)], axis=1)


def widen_hi(own, wpk, epk):
    return widen_pixels(own, wpk, pltpu.roll(epk, 4, 1))


def widen_tgt(own, wpk, epk):
    return widen_pixels(own, pltpu.roll(wpk, 6, 1), epk)


def widen_low(own, wpk, epk):
    rows = own.shape[0]
    own = pltpu.roll(own, 3, 1)
    sub = lax.broadcasted_iota(jnp.int32, own.shape, 1)
    wpk = wpk.reshape(rows, 3, 8, C)
    epk = epk.reshape(rows, 3, 8, C)
    left, right = own, own
    for b in range(3):
        left = jnp.where(sub == b, pltpu.roll(wpk[:, b], b + 1, 1), left)
        right = jnp.where(sub == 3 + b, pltpu.roll(epk[:, b], b + 4, 1), right)
    return jnp.concatenate([left, right], axis=1)


def land_row(part, own, wpk, epk):
    col = lax.broadcasted_iota(jnp.int32, (WW, C), 0)
    left = wpk[part, 6:7, :]
    right = epk[part, 6:7, :]
    return jnp.where(col < 4, left, jnp.where(col < 4 + W, own, right))


def pack_lat(land_ref, own_ref, w_ref, e_ref, north_ref, south_ref):
    land = land_ref[0, 0]
    wpk = w_ref[0:2].astype(F32)
    epk = e_ref[0:2].astype(F32)
    lands = jnp.concatenate(
        [
            land_row(0, (land // 32).astype(F32), wpk, epk),
            land_row(1, (land % 32).astype(F32), wpk, epk),
        ],
        axis=0,
    ).astype(BF16)
    for side, out_ref in enumerate((north_ref, south_ref)):
        def edge(ref, depth):
            start = (H - depth) * side
            return ref[start : start + depth].astype(F32)

        own = own_ref[side].astype(F32)
        hi = widen_hi(own[0:4], edge(w_ref, 4), edge(e_ref, 4))
        tgt = widen_tgt(own[4:6], edge(w_ref, 2), edge(e_ref, 2))
        low = widen_low(own[6].reshape(3, 8, C), edge(w_ref, 9), edge(e_ref, 9))
        out_ref[0:128] = hi.reshape(128, C).astype(BF16)
        out_ref[128:192] = tgt.reshape(64, C).astype(BF16)
        out_ref[192:240] = low.reshape(48, C).astype(BF16)
        out_ref[240:304] = lands


def put3(dst, start, v):
    rows = v.shape[0]
    dst[pl.ds(start, rows), 0:C] = pltpu.roll(v, 1, 0).astype(BF16)
    dst[pl.ds(start, rows), C : 2 * C] = v.astype(BF16)
    dst[pl.ds(start, rows), 2 * C : 3 * C] = pltpu.roll(v, rows - 1, 0).astype(BF16)


def window(src, start, rows, stride):
    return jnp.concatenate(
        [src[pl.ds(pl.multiple_of(start + d * stride, 16), rows), :] for d in range(3)], axis=1
    )


def own_columns(rows):
    col = lax.broadcasted_iota(jnp.int32, (rows // WW, WW, C), 1).reshape(rows, C)
    return (col >= 4) & (col < 4 + W)


def zero_at(flag, ref, start, rows):
    @pl.when(flag)
    def _():
        ref[start : start + rows, :] = jnp.zeros((rows, ref.shape[1]), ref.dtype)


def contract(x_ref, g_val, base, stride, rows, out):
    for d in range(3):
        out[d * 768 : (d + 1) * 768, :] = lax.dot_general(
            x_ref[base + d * stride : base + d * stride + rows, :],
            g_val,
            (((0,), (0,)), ((), ())),
            preferred_element_type=F32,
        )


def block_start(t, half):
    return pl.multiple_of((t % 8 * 4 + t // 8 * 2 + half) * 72, 8)


def hand_out(g_ref, keep_hbm, sent_ref, send_hbm, core, keep_sem, send_sem):
    for t in range(16):
        pltpu.make_async_copy(g_ref.at[pl.ds(block_start(t, core), 72)], keep_hbm.at[t], keep_sem).start()

    def one(t, _):
        sent_ref[t] = g_ref[pl.ds(block_start(t, 1 - core), 72), :].astype(BF16)
        return 0

    lax.fori_loop(0, 16, one, 0)
    pltpu.make_async_copy(sent_ref, send_hbm, send_sem).start()


def main(
    pos_ref, land_ref, hi_hbm, tgt_hbm, low_hbm, w_ref, e_ref, n_ref, s_ref, kh_hbm, kl_hbm, kj_hbm,
    keep_hbm, send_hbm,
    x3_ref, j3_ref, o3_ref, l3_ref, ha_ref, la_ref, og_ref, tg_ref, jg_ref, lg_ref, g_ref, sent_ref, up_ref,
    hi_v, tgt_v, low_v, kh_ref, kl_ref, kj_ref, kt_ref, sem, keep_sem, send_sem,
):
    fetch = [
        pltpu.make_async_copy(src, dst, sem.at[n])
        for n, (src, dst) in enumerate(
            (
                (low_hbm, low_v),
                (hi_hbm, hi_v),
                (kl_hbm, kl_ref),
                (kh_hbm, kh_ref),
                (tgt_hbm, tgt_v),
                (kj_hbm, kj_ref),
            )
        )
    ]
    for copy in fetch:
        copy.start()
    fetch_low, fetch_hi, fetch_kl, fetch_kh, fetch_tgt, fetch_kj = fetch
    first = pos_ref[0] == 0
    last = pos_ref[0] == 7
    core = pos_ref[1]
    up_ref[...] = up_matrix()

    put3(l3_ref, 0, n_ref[192:240, :].astype(F32))
    put3(l3_ref, 304, s_ref[192:240, :].astype(F32))
    put3(x3_ref, 0, n_ref[0:128, :].astype(F32))
    put3(x3_ref, 1664, s_ref[0:128, :].astype(F32))
    zero_at(first, l3_ref, 0, 48)
    zero_at(last, l3_ref, 304, 48)
    zero_at(first, x3_ref, 0, 128)
    zero_at(last, x3_ref, 1664, 128)
    fetch_low.wait()
    put3(
        l3_ref,
        48,
        widen_low(low_v[...].astype(F32), w_ref[...].astype(F32), e_ref[...].astype(F32)).reshape(256, C),
    )
    fetch_hi.wait()

    def widen_rows(t, _):
        rows = pl.ds(pl.multiple_of(t * 8, 8), 8)
        wide = widen_hi(hi_v[rows].astype(F32), w_ref[rows].astype(F32), e_ref[rows].astype(F32))
        put3(x3_ref, pl.multiple_of(128 + t * 256, 128), wide.reshape(256, C))
        return 0

    lax.fori_loop(0, 6, widen_rows, 0)
    fetch_kl.wait()
    la_ref[...] = jnp.maximum(
        jnp.dot(window(l3_ref, 0, 320, LWW), kl_ref[...], preferred_element_type=F32), 0.0
    ).astype(BF16)
    zero_at(first, la_ref, 0, 32)
    zero_at(last, la_ref, 288, 32)
    fetch_kh.wait()

    def high(b, _):
        s = pl.multiple_of(b * 576, 64)
        act = jnp.maximum(
            jnp.dot(window(x3_ref, s, 576, WW), kh_ref[...], preferred_element_type=F32), 0.0
        ).astype(BF16)
        ha_ref[pl.ds(s, 576), :] = act
        cells = la_ref[pl.ds(pl.multiple_of(b * 96, 32), 128), :]
        lift = jnp.dot(up_ref[...], cells, preferred_element_type=F32) * NINTH
        put3(j3_ref, s, act.astype(F32) + lift)
        return 0

    lax.fori_loop(0, 3, high, 0)
    zero_at(first, j3_ref, 0, 96)
    zero_at(last, j3_ref, 51 * WW, 96)
    tg_ref[0:64, :] = n_ref[128:192, :]
    tg_ref[1600:1664, :] = s_ref[128:192, :]
    fetch_tgt.wait()

    def widen_targets(t, _):
        rows = pl.ds(pl.multiple_of(t * 8, 8), 8)
        wide = widen_tgt(tgt_v[rows].astype(F32), w_ref[rows].astype(F32), e_ref[rows].astype(F32))
        tg_ref[pl.ds(pl.multiple_of(64 + t * 256, 64), 256), :] = wide.reshape(256, C).astype(BF16)
        return 0

    lax.fori_loop(0, 6, widen_targets, 0)
    fetch_kj.wait()

    def weight_of(high_part, low_part):
        return ((high_part * 32.0 + low_part) * SCALE)[None]

    own = land_ref[0, 0]
    wland = w_ref[0:2].astype(F32)
    eland = e_ref[0:2].astype(F32)
    top = weight_of(n_ref[240:272, :].astype(F32), n_ref[272:304, :].astype(F32))
    mid = weight_of(
        land_row(0, (own // 32).astype(F32), wland, eland), land_row(1, (own % 32).astype(F32), wland, eland)
    )
    bot = weight_of(s_ref[240:272, :].astype(F32), s_ref[272:304, :].astype(F32))

    def join(b, _):
        s = pl.multiple_of(b * 416, 32)
        y = jnp.dot(window(j3_ref, s, 416, WW), kj_ref[...], preferred_element_type=F32)
        diff = (y - tg_ref[pl.ds(s, 416), :].astype(F32)).reshape(13, WW, C)
        row = lax.broadcasted_iota(jnp.int32, (13, WW, C), 0) + b * 13
        weight = jnp.where(row < 2, top, jnp.where(row >= 50, bot, mid))
        grad = (weight * diff).reshape(416, C)
        put3(o3_ref, s, grad)
        og_ref[pl.ds(s, 416), :] = jnp.where(own_columns(416), grad, 0.0).astype(BF16)
        return 0

    lax.fori_loop(0, 4, join, 0)
    zero_at(first, o3_ref, 0, 64)
    zero_at(last, o3_ref, 50 * WW, 64)
    contract(j3_ref, og_ref[64:1600, :], 64, WW, 1536, g_ref.at[2])
    hand_out(g_ref.at[2], keep_hbm.at[2], sent_ref.at[2], send_hbm.at[2], core, keep_sem.at[2], send_sem.at[2])
    for tap in range(9):
        kt_ref[(8 - tap) * C : (9 - tap) * C, :] = kj_ref[tap * C : (tap + 1) * C, :].T

    def back(b, _):
        s = pl.multiple_of(b * 320, 32)
        y = jnp.dot(window(o3_ref, s, 320, WW), kt_ref[...], preferred_element_type=F32)
        jg_ref[pl.ds(s, 320), :] = y.astype(BF16)
        on = ha_ref[pl.ds(pl.multiple_of(s + 64, 32), 320), :].astype(F32) > 0
        og_ref[pl.ds(s, 320), :] = jnp.where(own_columns(320) & on, y, 0.0).astype(BF16)
        return 0

    lax.fori_loop(0, 5, back, 0)
    zero_at(first, jg_ref, 0, 32)
    zero_at(last, jg_ref, 49 * WW, 32)
    contract(x3_ref, og_ref[32:1568, :], 96, WW, 1536, g_ref.at[0])
    hand_out(g_ref.at[0], keep_hbm.at[0], sent_ref.at[0], send_hbm.at[0], core, keep_sem.at[0], send_sem.at[0])
    down = down_matrix()
    for b in range(2):
        lifted = jnp.dot(down, jg_ref[b * 768 : b * 768 + 832, :], preferred_element_type=F32) * NINTH
        on = la_ref[32 + b * 128 : 160 + b * 128, :].astype(F32) > 0
        lg_ref[b * 128 : (b + 1) * 128, :] = jnp.where(on, lifted, 0.0).astype(BF16)
    contract(l3_ref, lg_ref[...], 32, LWW, 256, g_ref.at[1])
    hand_out(g_ref.at[1], keep_hbm.at[1], sent_ref.at[1], send_hbm.at[1], core, keep_sem.at[1], send_sem.at[1])
    for n in range(3):
        pltpu.make_async_copy(g_ref.at[n, 0:1152], keep_hbm.at[n], keep_sem.at[n]).wait()
        pltpu.make_async_copy(sent_ref.at[n], send_hbm.at[n], send_sem.at[n]).wait()


def regroup_lanes(parts, rows):
    quarter = lax.broadcasted_iota(jnp.int32, (rows, 128), 1) // 32
    for q in range(4):
        out = None
        for g in range(4):
            shift = ((g - q) * 32) % 128
            turned = pltpu.roll(parts[g], shift, 1) if shift else parts[g]
            out = turned if out is None else jnp.where(quarter == g, turned, out)
        yield q, out


def merge(keep_hbm, recv_ref, out_ref, keep_ref, sem):
    copies = [
        pltpu.make_async_copy(keep_hbm.at[n, pl.ds(8 * xl, 8)], keep_ref.at[n, pl.ds(8 * xl, 8)], sem.at[2 * n + xl])
        for n in range(3)
        for xl in range(2)
    ]
    for copy in copies:
        copy.start()
    for n in range(3):
        for xl in range(2):
            copies[2 * n + xl].wait()

            def one(p, _):
                blocks = []
                for g in range(4):
                    at = xl * 8 + 2 * g + p
                    blocks.append(keep_ref[n, at] + recv_ref[n, at].astype(F32))
                for h in range(2):
                    parts = [v[:, h * 128 : (h + 1) * 128] for v in blocks]
                    for q, out in regroup_lanes(parts, 72):
                        out_ref[(h * 4 + q) * 2 + xl, n * 2 + p] = out.astype(BF16)
                return 0

            lax.fori_loop(0, 2, one, 0)


def total(in_ref, out_ref):
    quarter = lax.broadcasted_iota(jnp.int32, (56, 128), 1) // 32
    for p in range(2):
        sums = []
        for n in range(3):
            acc = in_ref[0, 2 * n + p].astype(F32)
            for i in range(1, 16):
                acc = acc + in_ref[i, 2 * n + p].astype(F32)
            sums.append(acc)
        rows = jnp.concatenate(sums + [jnp.zeros((8, 128), F32)], axis=0)
        for g in range(4):
            out = None
            for s in range(4):
                shift = ((s - g) * 32) % 128
                part = rows[s * 56 : (s + 1) * 56]
                turned = pltpu.roll(part, shift, 1) if shift else part
                out = turned if out is None else jnp.where(quarter == s, turned, out)
            out_ref[2 * g + p] = out


def finish(in_ref, a_ref, b_ref, c_ref):
    acc = in_ref[0].astype(F32)
    for i in range(1, 8):
        acc = acc + in_ref[i].astype(F32)
    rows = jnp.concatenate(
        [acc if s == 0 else pltpu.roll(acc, 128 - 32 * s, 1) for s in range(4)], axis=0
    )
    for g, ref in enumerate((a_ref, b_ref, c_ref)):
        ref[...] = rows[g * 72 : (g + 1) * 72].T[0:32]


def call(kernel, out, specs, scratch=(), outs=None, name=None, vmem=None):
    return pl.pallas_call(
        kernel,
        out_shape=tuple(jax.ShapeDtypeStruct(s, d) for s, d in out),
        in_specs=list(specs),
        out_specs=outs or tuple(VMEM for _ in out),
        scratch_shapes=list(scratch),
        name=name,
        compiler_params=pltpu.CompilerParams(vmem_limit_bytes=vmem) if vmem else None,
    )


def ring(count, step):
    return [(i, (i + step) % count) for i in range(count)]


XY = ("yh", "yl", "xh", "xl")
Z = ("zh", "zm", "zl")


def body(hi, low, kh, kl, kj, tgt, land):
    dma = pltpu.SemaphoreType.DMA
    west, east, edges = call(
        pack_lon,
        [((H, 8, C), BF16)] * 2 + [((2, 7, W, C), BF16)],
        [SMEM] + [HBM] * 3,
        [pltpu.VMEM((2, H, 8, C), BF16), pltpu.VMEM((2, H, 8, C), BF16), pltpu.VMEM((LH, LW, C), BF16), dma((9,))],
        name="pack_lon",
        vmem=FULL,
    )(land, hi, tgt, low)
    from_e = lax.ppermute(west, LON, ring(32, -1))
    from_w = lax.ppermute(east, LON, ring(32, 1))
    north, south = call(
        pack_lat, [((PK, C), BF16)] * 2, [SMEM] + [VMEM] * 3, name="pack_lat", vmem=6 * MIB
    )(land, edges, from_w, from_e)
    from_s = lax.ppermute(north, LAT, ring(8, -1))
    from_n = lax.ppermute(south, LAT, ring(8, 1))
    pos = jnp.stack([lax.axis_index(LAT), lax.axis_index("core")]).astype(jnp.int32)
    keep, send = call(
        main,
        [((3, 16, 72, C), F32), ((3, 16, 72, C), BF16)],
        [SMEM] * 2 + [HBM] * 3 + [VMEM] * 4 + [HBM] * 3,
        [
            pltpu.VMEM((1792, 768), BF16),
            pltpu.VMEM((1728, 768), BF16),
            pltpu.VMEM((1664, 768), BF16),
            pltpu.VMEM((352, 768), BF16),
            pltpu.VMEM((1728, C), BF16),
            pltpu.VMEM((320, C), BF16),
            pltpu.VMEM((1664, C), BF16),
            pltpu.VMEM((1664, C), BF16),
            pltpu.VMEM((1600, C), BF16),
            pltpu.VMEM((256, C), BF16),
            pltpu.VMEM((3, 2304, C), F32),
            pltpu.VMEM((3, 16, 72, C), BF16),
            pltpu.VMEM((576, 128), BF16),
            pltpu.VMEM((H, W, C), BF16),
            pltpu.VMEM((H, W, C), BF16),
            pltpu.VMEM((LH, LW, C), BF16),
            pltpu.VMEM((2304, C), BF16),
            pltpu.VMEM((2304, C), BF16),
            pltpu.VMEM((2304, C), BF16),
            pltpu.VMEM((2304, C), BF16),
            dma((6,)),
            dma((3,)),
            dma((3,)),
        ],
        outs=(HBM, HBM),
        name="main",
        vmem=MAIN_LIMIT,
    )(pos, land, hi, tgt, low, from_w, from_e, from_n, from_s, *[k.reshape(9 * C, C) for k in (kh, kl, kj)])
    recv = lax.ppermute(send, "core", ring(2, 1))
    (parts,) = call(
        merge,
        [((16, 6, 72, 128), BF16)],
        [HBM, VMEM],
        [pltpu.VMEM((3, 16, 72, C), F32), dma((6,))],
        name="merge",
        vmem=MERGE_LIMIT,
    )(keep, recv)
    parts = lax.all_to_all(parts, XY, 0, 0, tiled=True)
    (parts,) = call(total, [((8, 56, 128), F32)], [VMEM], name="total", vmem=6 * MIB)(parts)
    parts = lax.all_to_all(parts, Z, 0, 0, tiled=True)
    grads = call(finish, [((32, 72), F32)] * 3, [VMEM], name="finish", vmem=2 * MIB)(parts)
    return tuple(g.T for g in grads)


def solution(mesh):
    fine = Mesh(mesh.devices.reshape((2,) * 8), LAT + LON)
    tile = P(LAT, LON, None)
    mapped = jax.shard_map(
        body,
        mesh=fine,
        in_specs=(tile, tile, P(), P(), P(), tile, P(LAT, LON)),
        out_specs=(P(LON, LAT),) * 3,
        check_vma=False,
    )
    return mapped
```

```python
import jax
import jax.numpy as jnp
from jax import lax
from jax.experimental import pallas as pl
from jax.experimental.pallas import tpu as pltpu
from jax.sharding import Mesh, PartitionSpec as P

F32 = jnp.float32
BF16 = jnp.bfloat16
C = 256
H, W = 48, 24
LH, LW = 16, 8
WW = 32
LWW = 16
LAT = ("yh", "yl", "xh")
LON = ("zh", "zm", "zl", "xl", "core")
SCALE = 2.0 / (H * W * H * W)
NINTH = 1.0 / 9.0
PK = 304
MIB = 1024 * 1024
FULL = 60 * 1024 * 1024
MAIN_LIMIT = 64 * MIB - 12_000_000
MERGE_LIMIT = 64 * MIB - 15_500_000
VMEM = pl.BlockSpec(memory_space=pltpu.VMEM)
SMEM = pl.BlockSpec(memory_space=pltpu.SMEM)
HBM = pl.BlockSpec(memory_space=pltpu.HBM)


def up_matrix():
    def weight(m, r, cell):
        side = jnp.where(cell == m, 2.0, jnp.where(cell == m + r - 1, 1.0, 0.0))
        return jnp.where(r == 1, jnp.where(cell == m, 3.0, 0.0), side)

    i = lax.broadcasted_iota(jnp.int32, (18, 1, 8 * LWW), 0)
    e = lax.broadcasted_iota(jnp.int32, (18, 1, 8 * LWW), 2) // LWW
    j = lax.broadcasted_iota(jnp.int32, (1, WW, 8 * LWW), 1) + 2
    f = lax.broadcasted_iota(jnp.int32, (1, WW, 8 * LWW), 2) % LWW
    both = weight(i // 3 + 1, i % 3, e) * weight(j // 3 + 1, j % 3, f)
    return both.reshape(18 * WW, 8 * LWW).astype(BF16)


def down_matrix():
    def weight(tap):
        return jnp.maximum(3 - jnp.abs(tap - 2), 0).astype(F32)

    m = lax.broadcasted_iota(jnp.int32, (8, 1, 26 * WW), 0)
    d = lax.broadcasted_iota(jnp.int32, (8, 1, 26 * WW), 2) // WW
    f = lax.broadcasted_iota(jnp.int32, (1, LWW, 26 * WW), 1) - 3
    j = lax.broadcasted_iota(jnp.int32, (1, LWW, 26 * WW), 2) % WW - 3
    both = weight(d - 3 * m) * jnp.where((f >= 0) & (f < LW), weight(j - 3 * f), 0.0)
    return both.reshape(8 * LWW, 26 * WW).astype(BF16)


def pack_lon(land_ref, hi_ref, tgt_ref, low_ref, west_ref, east_ref, edge_ref, hi_v, tgt_v, low_v, sem):
    copies = [
        pltpu.make_async_copy(src.at[:, pl.ds(start, 8), :], dst.at[side], sem.at[2 * n + side])
        for n, (src, dst) in enumerate(((hi_ref, hi_v), (tgt_ref, tgt_v)))
        for side, start in enumerate((0, 16))
    ]
    copies.append(pltpu.make_async_copy(low_ref, low_v, sem.at[4]))
    for side in range(2):
        copies.append(pltpu.make_async_copy(hi_ref.at[pl.ds(44 * side, 4)], edge_ref.at[side, 0:4], sem.at[5 + side]))
        copies.append(pltpu.make_async_copy(tgt_ref.at[pl.ds(46 * side, 2)], edge_ref.at[side, 4:6], sem.at[7 + side]))
    for copy in copies:
        copy.start()
    land = land_ref[0, 0]
    sub = lax.broadcasted_iota(jnp.int32, (H, 8, C), 1)
    row = lax.broadcasted_iota(jnp.int32, (H, 8, C), 0)
    lands = jnp.where(row % 2 == 0, (land // 32).astype(F32), (land % 32).astype(F32))
    for copy in copies:
        copy.wait()
    low = low_v[...].astype(F32)

    def rest(start):
        cells = jnp.stack([pltpu.roll(low, (7 - start - b) % 8, 1) for b in range(3)], axis=1)
        return jnp.where(sub == 6, lands, cells.reshape(H, 8, C))

    west = jnp.where(
        sub < 4, hi_v[0].astype(F32), jnp.where(sub < 6, pltpu.roll(tgt_v[0].astype(F32), 4, 1), rest(0))
    )
    east = jnp.where(
        sub < 4,
        pltpu.roll(hi_v[1].astype(F32), 4, 1),
        jnp.where(sub < 6, pltpu.roll(tgt_v[1].astype(F32), 6, 1), rest(5)),
    )
    west_ref[...] = west.astype(BF16)
    east_ref[...] = east.astype(BF16)
    for side in range(2):
        edge_ref[side, 6] = low_v[13 * side : 13 * side + 3].astype(F32).reshape(24, C).astype(BF16)


def widen_pixels(own, left, right):
    turned = [pltpu.roll(own[:, 8 * g : 8 * g + 8], 4, 1) for g in range(3)]
    parts = [left] + turned + [right]
    low_half = lax.broadcasted_iota(jnp.int32, left.shape, 1) < 4
    return jnp.concatenate([jnp.where(low_half, parts[g], parts[g + 1]) for g in range(4)], axis=1)


def widen_hi(own, wpk, epk):
    return widen_pixels(own, wpk, pltpu.roll(epk, 4, 1))


def widen_tgt(own, wpk, epk):
    return widen_pixels(own, pltpu.roll(wpk, 6, 1), epk)


def widen_low(own, wpk, epk):
    rows = own.shape[0]
    own = pltpu.roll(own, 3, 1)
    sub = lax.broadcasted_iota(jnp.int32, own.shape, 1)
    wpk = wpk.reshape(rows, 3, 8, C)
    epk = epk.reshape(rows, 3, 8, C)
    left, right = own, own
    for b in range(3):
        left = jnp.where(sub == b, pltpu.roll(wpk[:, b], b + 1, 1), left)
        right = jnp.where(sub == 3 + b, pltpu.roll(epk[:, b], b + 4, 1), right)
    return jnp.concatenate([left, right], axis=1)


def land_row(part, own, wpk, epk):
    col = lax.broadcasted_iota(jnp.int32, (WW, C), 0)
    left = wpk[part, 6:7, :]
    right = epk[part, 6:7, :]
    return jnp.where(col < 4, left, jnp.where(col < 4 + W, own, right))


def pack_lat(land_ref, own_ref, w_ref, e_ref, north_ref, south_ref):
    land = land_ref[0, 0]
    wpk = w_ref[0:2].astype(F32)
    epk = e_ref[0:2].astype(F32)
    lands = jnp.concatenate(
        [
            land_row(0, (land // 32).astype(F32), wpk, epk),
            land_row(1, (land % 32).astype(F32), wpk, epk),
        ],
        axis=0,
    ).astype(BF16)
    for side, out_ref in enumerate((north_ref, south_ref)):
        def edge(ref, depth):
            start = (H - depth) * side
            return ref[start : start + depth].astype(F32)

        own = own_ref[side].astype(F32)
        hi = widen_hi(own[0:4], edge(w_ref, 4), edge(e_ref, 4))
        tgt = widen_tgt(own[4:6], edge(w_ref, 2), edge(e_ref, 2))
        low = widen_low(own[6].reshape(3, 8, C), edge(w_ref, 9), edge(e_ref, 9))
        out_ref[0:128] = hi.reshape(128, C).astype(BF16)
        out_ref[128:192] = tgt.reshape(64, C).astype(BF16)
        out_ref[192:240] = low.reshape(48, C).astype(BF16)
        out_ref[240:304] = lands


def put3(dst, start, v):
    rows = v.shape[0]
    dst[pl.ds(start, rows), 0:C] = pltpu.roll(v, 1, 0).astype(BF16)
    dst[pl.ds(start, rows), C : 2 * C] = v.astype(BF16)
    dst[pl.ds(start, rows), 2 * C : 3 * C] = pltpu.roll(v, rows - 1, 0).astype(BF16)


def window(src, start, rows, stride):
    return jnp.concatenate(
        [src[pl.ds(pl.multiple_of(start + d * stride, 16), rows), :] for d in range(3)], axis=1
    )


def own_columns(rows):
    col = lax.broadcasted_iota(jnp.int32, (rows // WW, WW, C), 1).reshape(rows, C)
    return (col >= 4) & (col < 4 + W)


def zero_at(flag, ref, start, rows):
    @pl.when(flag)
    def _():
        ref[start : start + rows, :] = jnp.zeros((rows, ref.shape[1]), ref.dtype)


def contract(x_ref, g_val, base, stride, rows, out):
    for d in range(3):
        out[d * 768 : (d + 1) * 768, :] = lax.dot_general(
            x_ref[base + d * stride : base + d * stride + rows, :],
            g_val,
            (((0,), (0,)), ((), ())),
            preferred_element_type=F32,
        )


def block_start(t, half):
    return pl.multiple_of((t % 8 * 4 + t // 8 * 2 + half) * 72, 8)


def hand_out(g_ref, keep_hbm, sent_ref, send_hbm, core, keep_sem, send_sem):
    for t in range(16):
        pltpu.make_async_copy(g_ref.at[pl.ds(block_start(t, core), 72)], keep_hbm.at[t], keep_sem).start()

    for t in range(16):
        sent_ref[t] = g_ref[pl.ds(block_start(t, 1 - core), 72), :].astype(BF16)
    pltpu.make_async_copy(sent_ref, send_hbm, send_sem).start()


def main(
    pos_ref, land_ref, hi_hbm, tgt_hbm, low_hbm, w_ref, e_ref, n_ref, s_ref, kh_hbm, kl_hbm, kj_hbm,
    keep_hbm, send_hbm,
    x3_ref, j3_ref, o3_ref, l3_ref, ha_ref, la_ref, og_ref, tg_ref, jg_ref, lg_ref, g_ref, sent_ref, up_ref,
    hi_v, tgt_v, low_v, kh_ref, kl_ref, kj_ref, kt_ref, sem, keep_sem, send_sem,
):
    fetch = [
        pltpu.make_async_copy(src, dst, sem.at[n])
        for n, (src, dst) in enumerate(
            (
                (low_hbm, low_v),
                (hi_hbm, hi_v),
                (kl_hbm, kl_ref),
                (kh_hbm, kh_ref),
                (tgt_hbm, tgt_v),
                (kj_hbm, kj_ref),
            )
        )
    ]
    for copy in fetch:
        copy.start()
    fetch_low, fetch_hi, fetch_kl, fetch_kh, fetch_tgt, fetch_kj = fetch
    first = pos_ref[0] == 0
    last = pos_ref[0] == 7
    core = pos_ref[1]
    up_ref[...] = up_matrix()

    put3(l3_ref, 0, n_ref[192:240, :].astype(F32))
    put3(l3_ref, 304, s_ref[192:240, :].astype(F32))
    put3(x3_ref, 0, n_ref[0:128, :].astype(F32))
    put3(x3_ref, 1664, s_ref[0:128, :].astype(F32))
    zero_at(first, l3_ref, 0, 48)
    zero_at(last, l3_ref, 304, 48)
    zero_at(first, x3_ref, 0, 128)
    zero_at(last, x3_ref, 1664, 128)
    fetch_low.wait()
    fetch_kl.wait()
    fetch_hi.wait()
    put3(
        l3_ref,
        48,
        widen_low(low_v[...].astype(F32), w_ref[...].astype(F32), e_ref[...].astype(F32)).reshape(256, C),
    )
    def widen_rows(t, _):
        rows = pl.ds(pl.multiple_of(t * 8, 8), 8)
        wide = widen_hi(hi_v[rows].astype(F32), w_ref[rows].astype(F32), e_ref[rows].astype(F32))
        put3(x3_ref, pl.multiple_of(128 + t * 256, 128), wide.reshape(256, C))
        return 0

    lax.fori_loop(0, 6, widen_rows, 0, unroll=True)
    la_ref[...] = jnp.maximum(
        jnp.dot(window(l3_ref, 0, 320, LWW), kl_ref[...], preferred_element_type=F32), 0.0
    ).astype(BF16)
    zero_at(first, la_ref, 0, 32)
    zero_at(last, la_ref, 288, 32)
    fetch_tgt.wait()
    fetch_kh.wait()
    tg_ref[0:64, :] = n_ref[128:192, :]
    tg_ref[1600:1664, :] = s_ref[128:192, :]
    def widen_targets(t, _):
        rows = pl.ds(pl.multiple_of(t * 8, 8), 8)
        wide = widen_tgt(tgt_v[rows].astype(F32), w_ref[rows].astype(F32), e_ref[rows].astype(F32))
        tg_ref[pl.ds(pl.multiple_of(64 + t * 256, 64), 256), :] = wide.reshape(256, C).astype(BF16)
        return 0

    lax.fori_loop(0, 6, widen_targets, 0, unroll=True)
    def high(b, _):
        s = pl.multiple_of(b * 576, 64)
        act = jnp.maximum(
            jnp.dot(window(x3_ref, s, 576, WW), kh_ref[...], preferred_element_type=F32), 0.0
        ).astype(BF16)
        ha_ref[pl.ds(s, 576), :] = act
        cells = la_ref[pl.ds(pl.multiple_of(b * 96, 32), 128), :]
        lift = jnp.dot(up_ref[...], cells, preferred_element_type=F32) * NINTH
        put3(j3_ref, s, act.astype(F32) + lift)
        return 0

    lax.fori_loop(0, 3, high, 0, unroll=True)
    zero_at(first, j3_ref, 0, 96)
    zero_at(last, j3_ref, 51 * WW, 96)
    fetch_kj.wait()

    def weight_of(high_part, low_part):
        return ((high_part * 32.0 + low_part) * SCALE)[None]

    own = land_ref[0, 0]
    wland = w_ref[0:2].astype(F32)
    eland = e_ref[0:2].astype(F32)
    top = weight_of(n_ref[240:272, :].astype(F32), n_ref[272:304, :].astype(F32))
    mid = weight_of(
        land_row(0, (own // 32).astype(F32), wland, eland), land_row(1, (own % 32).astype(F32), wland, eland)
    )
    bot = weight_of(s_ref[240:272, :].astype(F32), s_ref[272:304, :].astype(F32))

    def join(b, _):
        s = pl.multiple_of(b * 832, 32)
        y = jnp.dot(window(j3_ref, s, 832, WW), kj_ref[...], preferred_element_type=F32)
        diff = (y - tg_ref[pl.ds(s, 832), :].astype(F32)).reshape(26, WW, C)
        row = lax.broadcasted_iota(jnp.int32, (26, WW, C), 0) + b * 26
        weight = jnp.where(row < 2, top, jnp.where(row >= 50, bot, mid))
        grad = (weight * diff).reshape(832, C)
        put3(o3_ref, s, grad)
        og_ref[pl.ds(s, 832), :] = jnp.where(own_columns(832), grad, 0.0).astype(BF16)
        return 0

    lax.fori_loop(0, 2, join, 0, unroll=True)
    zero_at(first, o3_ref, 0, 64)
    zero_at(last, o3_ref, 50 * WW, 64)
    contract(j3_ref, og_ref[64:1600, :], 64, WW, 1536, g_ref.at[2])
    hand_out(g_ref.at[2], keep_hbm.at[2], sent_ref.at[2], send_hbm.at[2], core, keep_sem.at[2], send_sem.at[2])
    for tap in range(9):
        kt_ref[(8 - tap) * C : (9 - tap) * C, :] = kj_ref[tap * C : (tap + 1) * C, :].T

    def back(b, _):
        s = pl.multiple_of(b * 800, 32)
        y = jnp.dot(window(o3_ref, s, 800, WW), kt_ref[...], preferred_element_type=F32)
        jg_ref[pl.ds(s, 800), :] = y.astype(BF16)
        on = ha_ref[pl.ds(pl.multiple_of(s + 64, 32), 800), :].astype(F32) > 0
        og_ref[pl.ds(s, 800), :] = jnp.where(own_columns(800) & on, y, 0.0).astype(BF16)
        return 0

    lax.fori_loop(0, 2, back, 0, unroll=True)
    zero_at(first, jg_ref, 0, 32)
    zero_at(last, jg_ref, 49 * WW, 32)
    contract(x3_ref, og_ref[32:1568, :], 96, WW, 1536, g_ref.at[0])
    hand_out(g_ref.at[0], keep_hbm.at[0], sent_ref.at[0], send_hbm.at[0], core, keep_sem.at[0], send_sem.at[0])
    down = down_matrix()
    for b in range(2):
        lifted = jnp.dot(down, jg_ref[b * 768 : b * 768 + 832, :], preferred_element_type=F32) * NINTH
        on = la_ref[32 + b * 128 : 160 + b * 128, :].astype(F32) > 0
        lg_ref[b * 128 : (b + 1) * 128, :] = jnp.where(on, lifted, 0.0).astype(BF16)
    contract(l3_ref, lg_ref[...], 32, LWW, 256, g_ref.at[1])
    hand_out(g_ref.at[1], keep_hbm.at[1], sent_ref.at[1], send_hbm.at[1], core, keep_sem.at[1], send_sem.at[1])
    for n in range(3):
        pltpu.make_async_copy(g_ref.at[n, 0:1152], keep_hbm.at[n], keep_sem.at[n]).wait()
        pltpu.make_async_copy(sent_ref.at[n], send_hbm.at[n], send_sem.at[n]).wait()


def regroup_lanes(parts, rows):
    quarter = lax.broadcasted_iota(jnp.int32, (rows, 128), 1) // 32
    for q in range(4):
        out = None
        for g in range(4):
            shift = ((g - q) * 32) % 128
            turned = pltpu.roll(parts[g], shift, 1) if shift else parts[g]
            out = turned if out is None else jnp.where(quarter == g, turned, out)
        yield q, out


def merge(keep_hbm, recv_ref, out_ref, keep_ref, sem):
    copies = [
        pltpu.make_async_copy(keep_hbm.at[n, pl.ds(8 * xl, 8)], keep_ref.at[n, pl.ds(8 * xl, 8)], sem.at[2 * n + xl])
        for n in range(3)
        for xl in range(2)
    ]
    for copy in copies:
        copy.start()
    for n in range(3):
        for xl in range(2):
            copies[2 * n + xl].wait()

            def one(p, _):
                blocks = []
                for g in range(4):
                    at = xl * 8 + 2 * g + p
                    blocks.append(keep_ref[n, at] + recv_ref[n, at].astype(F32))
                for h in range(2):
                    parts = [v[:, h * 128 : (h + 1) * 128] for v in blocks]
                    for q, out in regroup_lanes(parts, 72):
                        out_ref[(h * 4 + q) * 4 + 2 * xl + p, n] = out.astype(BF16)
                return 0

            lax.fori_loop(0, 2, one, 0)


def total(in_ref, out_ref):
    quarter = lax.broadcasted_iota(jnp.int32, (56, 128), 1) // 32
    sums = []
    for n in range(3):
        acc = in_ref[0, n].astype(F32)
        for i in range(1, 32):
            acc = acc + in_ref[i, n].astype(F32)
        sums.append(acc)
    rows = jnp.concatenate(sums + [jnp.zeros((8, 128), F32)], axis=0)
    for g in range(4):
        out = None
        for s in range(4):
            shift = ((s - g) * 32) % 128
            part = rows[s * 56 : (s + 1) * 56]
            turned = pltpu.roll(part, shift, 1) if shift else part
            out = turned if out is None else jnp.where(quarter == s, turned, out)
        out_ref[g] = out


def finish(in_ref, a_ref, b_ref, c_ref):
    acc = in_ref[0].astype(F32)
    for i in range(1, 4):
        acc = acc + in_ref[i].astype(F32)
    rows = jnp.concatenate(
        [acc if s == 0 else pltpu.roll(acc, 128 - 32 * s, 1) for s in range(4)], axis=0
    )
    for g, ref in enumerate((a_ref, b_ref, c_ref)):
        ref[...] = rows[g * 72 : (g + 1) * 72].T[0:32]


def call(kernel, out, specs, scratch=(), outs=None, name=None, vmem=None):
    return pl.pallas_call(
        kernel,
        out_shape=tuple(jax.ShapeDtypeStruct(s, d) for s, d in out),
        in_specs=list(specs),
        out_specs=outs or tuple(VMEM for _ in out),
        scratch_shapes=list(scratch),
        name=name,
        compiler_params=pltpu.CompilerParams(vmem_limit_bytes=vmem) if vmem else None,
    )


def ring(count, step):
    return [(i, (i + step) % count) for i in range(count)]


FIRST = ("yh", "yl", "xh", "xl", "zl")
SECOND = ("zh", "zm")


def body(hi, low, kh, kl, kj, tgt, land):
    dma = pltpu.SemaphoreType.DMA
    west, east, edges = call(
        pack_lon,
        [((H, 8, C), BF16)] * 2 + [((2, 7, W, C), BF16)],
        [SMEM] + [HBM] * 3,
        [pltpu.VMEM((2, H, 8, C), BF16), pltpu.VMEM((2, H, 8, C), BF16), pltpu.VMEM((LH, LW, C), BF16), dma((9,))],
        name="pack_lon",
        vmem=FULL,
    )(land, hi, tgt, low)
    from_e = lax.ppermute(west, LON, ring(32, -1))
    from_w = lax.ppermute(east, LON, ring(32, 1))
    north, south = call(
        pack_lat, [((PK, C), BF16)] * 2, [SMEM] + [VMEM] * 3, name="pack_lat", vmem=6 * MIB
    )(land, edges, from_w, from_e)
    from_s = lax.ppermute(north, LAT, ring(8, -1))
    from_n = lax.ppermute(south, LAT, ring(8, 1))
    pos = jnp.stack([lax.axis_index(LAT), lax.axis_index("core")]).astype(jnp.int32)
    keep, send = call(
        main,
        [((3, 16, 72, C), F32), ((3, 16, 72, C), BF16)],
        [SMEM] * 2 + [HBM] * 3 + [VMEM] * 4 + [HBM] * 3,
        [
            pltpu.VMEM((1792, 768), BF16),
            pltpu.VMEM((1728, 768), BF16),
            pltpu.VMEM((1664, 768), BF16),
            pltpu.VMEM((352, 768), BF16),
            pltpu.VMEM((1728, C), BF16),
            pltpu.VMEM((320, C), BF16),
            pltpu.VMEM((1664, C), BF16),
            pltpu.VMEM((1664, C), BF16),
            pltpu.VMEM((1600, C), BF16),
            pltpu.VMEM((256, C), BF16),
            pltpu.VMEM((3, 2304, C), F32),
            pltpu.VMEM((3, 16, 72, C), BF16),
            pltpu.VMEM((576, 128), BF16),
            pltpu.VMEM((H, W, C), BF16),
            pltpu.VMEM((H, W, C), BF16),
            pltpu.VMEM((LH, LW, C), BF16),
            pltpu.VMEM((2304, C), BF16),
            pltpu.VMEM((2304, C), BF16),
            pltpu.VMEM((2304, C), BF16),
            pltpu.VMEM((2304, C), BF16),
            dma((6,)),
            dma((3,)),
            dma((3,)),
        ],
        outs=(HBM, HBM),
        name="main",
        vmem=MAIN_LIMIT,
    )(pos, land, hi, tgt, low, from_w, from_e, from_n, from_s, *[k.reshape(9 * C, C) for k in (kh, kl, kj)])
    recv = lax.ppermute(send, "core", ring(2, 1))
    (parts,) = call(
        merge,
        [((32, 3, 72, 128), BF16)],
        [HBM, VMEM],
        [pltpu.VMEM((3, 16, 72, C), F32), dma((6,))],
        name="merge",
        vmem=MERGE_LIMIT,
    )(keep, recv)
    parts = lax.all_to_all(parts, FIRST, 0, 0, tiled=True)
    (parts,) = call(total, [((4, 56, 128), F32)], [VMEM], name="total", vmem=6 * MIB)(parts)
    parts = lax.all_to_all(parts, SECOND, 0, 0, tiled=True)
    grads = call(finish, [((32, 72), F32)] * 3, [VMEM], name="finish", vmem=2 * MIB)(parts)
    return tuple(g.T for g in grads)


def solution(mesh):
    fine = Mesh(mesh.devices.reshape((2,) * 8), LAT + LON)
    tile = P(LAT, LON, None)
    mapped = jax.shard_map(
        body,
        mesh=fine,
        in_specs=(tile, tile, P(), P(), P(), tile, P(LAT, LON)),
        out_specs=(P(LON, LAT),) * 3,
        check_vma=False,
    )
    return mapped
```

```python
import jax
import jax.numpy as jnp
from jax import lax
from jax.experimental import pallas as pl
from jax.experimental.pallas import tpu as pltpu
from jax.sharding import Mesh, PartitionSpec as P

F32 = jnp.float32
BF16 = jnp.bfloat16
C = 256
H, W = 48, 24
LH, LW = 16, 8
WW = 32
LWW = 16
LAT = ("yh", "yl", "xh")
LON = ("zh", "zm", "zl", "xl", "core")
SCALE = 2.0 / (H * W * H * W)
NINTH = 1.0 / 9.0
PK = 304
MIB = 1024 * 1024
FULL = 60 * 1024 * 1024
MAIN_LIMIT = 64 * MIB - 12_000_000
MERGE_LIMIT = 64 * MIB - 15_500_000
VMEM = pl.BlockSpec(memory_space=pltpu.VMEM)
SMEM = pl.BlockSpec(memory_space=pltpu.SMEM)
HBM = pl.BlockSpec(memory_space=pltpu.HBM)


def up_matrix():
    def weight(m, r, cell):
        side = jnp.where(cell == m, 2.0, jnp.where(cell == m + r - 1, 1.0, 0.0))
        return jnp.where(r == 1, jnp.where(cell == m, 3.0, 0.0), side)

    i = lax.broadcasted_iota(jnp.int32, (18, 1, 8 * LWW), 0)
    e = lax.broadcasted_iota(jnp.int32, (18, 1, 8 * LWW), 2) // LWW
    j = lax.broadcasted_iota(jnp.int32, (1, WW, 8 * LWW), 1) + 2
    f = lax.broadcasted_iota(jnp.int32, (1, WW, 8 * LWW), 2) % LWW
    both = weight(i // 3 + 1, i % 3, e) * weight(j // 3 + 1, j % 3, f)
    return both.reshape(18 * WW, 8 * LWW).astype(BF16)


def down_matrix():
    def weight(tap):
        return jnp.maximum(3 - jnp.abs(tap - 2), 0).astype(F32)

    m = lax.broadcasted_iota(jnp.int32, (8, 1, 26 * WW), 0)
    d = lax.broadcasted_iota(jnp.int32, (8, 1, 26 * WW), 2) // WW
    f = lax.broadcasted_iota(jnp.int32, (1, LWW, 26 * WW), 1) - 3
    j = lax.broadcasted_iota(jnp.int32, (1, LWW, 26 * WW), 2) % WW - 3
    both = weight(d - 3 * m) * jnp.where((f >= 0) & (f < LW), weight(j - 3 * f), 0.0)
    return both.reshape(8 * LWW, 26 * WW).astype(BF16)


def pack_lon(land_ref, hi_ref, tgt_ref, low_ref, west_ref, east_ref, edge_ref, hi_v, tgt_v, low_v, sem):
    copies = [
        pltpu.make_async_copy(src.at[:, pl.ds(start, 8), :], dst.at[side], sem.at[2 * n + side])
        for n, (src, dst) in enumerate(((hi_ref, hi_v), (tgt_ref, tgt_v)))
        for side, start in enumerate((0, 16))
    ]
    copies.append(pltpu.make_async_copy(low_ref, low_v, sem.at[4]))
    for side in range(2):
        copies.append(pltpu.make_async_copy(hi_ref.at[pl.ds(44 * side, 4)], edge_ref.at[side, 0:4], sem.at[5 + side]))
        copies.append(pltpu.make_async_copy(tgt_ref.at[pl.ds(46 * side, 2)], edge_ref.at[side, 4:6], sem.at[7 + side]))
    for copy in copies:
        copy.start()
    land = land_ref[0, 0]
    sub = lax.broadcasted_iota(jnp.int32, (H, 8, C), 1)
    row = lax.broadcasted_iota(jnp.int32, (H, 8, C), 0)
    lands = jnp.where(row % 2 == 0, (land // 32).astype(F32), (land % 32).astype(F32))
    for copy in copies:
        copy.wait()
    low = low_v[...].astype(F32)

    def rest(start):
        cells = jnp.stack([pltpu.roll(low, (7 - start - b) % 8, 1) for b in range(3)], axis=1)
        return jnp.where(sub == 6, lands, cells.reshape(H, 8, C))

    west = jnp.where(
        sub < 4, hi_v[0].astype(F32), jnp.where(sub < 6, pltpu.roll(tgt_v[0].astype(F32), 4, 1), rest(0))
    )
    east = jnp.where(
        sub < 4,
        pltpu.roll(hi_v[1].astype(F32), 4, 1),
        jnp.where(sub < 6, pltpu.roll(tgt_v[1].astype(F32), 6, 1), rest(5)),
    )
    west_ref[...] = west.astype(BF16)
    east_ref[...] = east.astype(BF16)
    for side in range(2):
        edge_ref[side, 6] = low_v[13 * side : 13 * side + 3].astype(F32).reshape(24, C).astype(BF16)


def widen_pixels(own, left, right):
    turned = [pltpu.roll(own[:, 8 * g : 8 * g + 8], 4, 1) for g in range(3)]
    parts = [left] + turned + [right]
    low_half = lax.broadcasted_iota(jnp.int32, left.shape, 1) < 4
    return jnp.concatenate([jnp.where(low_half, parts[g], parts[g + 1]) for g in range(4)], axis=1)


def widen_hi(own, wpk, epk):
    return widen_pixels(own, wpk, pltpu.roll(epk, 4, 1))


def widen_tgt(own, wpk, epk):
    return widen_pixels(own, pltpu.roll(wpk, 6, 1), epk)


def widen_low(own, wpk, epk):
    rows = own.shape[0]
    own = pltpu.roll(own, 3, 1)
    sub = lax.broadcasted_iota(jnp.int32, own.shape, 1)
    wpk = wpk.reshape(rows, 3, 8, C)
    epk = epk.reshape(rows, 3, 8, C)
    left, right = own, own
    for b in range(3):
        left = jnp.where(sub == b, pltpu.roll(wpk[:, b], b + 1, 1), left)
        right = jnp.where(sub == 3 + b, pltpu.roll(epk[:, b], b + 4, 1), right)
    return jnp.concatenate([left, right], axis=1)


def land_row(part, own, wpk, epk):
    col = lax.broadcasted_iota(jnp.int32, (WW, C), 0)
    left = wpk[part, 6:7, :]
    right = epk[part, 6:7, :]
    return jnp.where(col < 4, left, jnp.where(col < 4 + W, own, right))


def pack_lat(land_ref, own_ref, w_ref, e_ref, north_ref, south_ref):
    land = land_ref[0, 0]
    wpk = w_ref[0:2].astype(F32)
    epk = e_ref[0:2].astype(F32)
    lands = jnp.concatenate(
        [
            land_row(0, (land // 32).astype(F32), wpk, epk),
            land_row(1, (land % 32).astype(F32), wpk, epk),
        ],
        axis=0,
    ).astype(BF16)
    for side, out_ref in enumerate((north_ref, south_ref)):
        def edge(ref, depth):
            start = (H - depth) * side
            return ref[start : start + depth].astype(F32)

        own = own_ref[side].astype(F32)
        hi = widen_hi(own[0:4], edge(w_ref, 4), edge(e_ref, 4))
        tgt = widen_tgt(own[4:6], edge(w_ref, 2), edge(e_ref, 2))
        low = widen_low(own[6].reshape(3, 8, C), edge(w_ref, 9), edge(e_ref, 9))
        out_ref[0:128] = hi.reshape(128, C).astype(BF16)
        out_ref[128:192] = tgt.reshape(64, C).astype(BF16)
        out_ref[192:240] = low.reshape(48, C).astype(BF16)
        out_ref[240:304] = lands


def put3(dst, start, v):
    rows = v.shape[0]
    dst[pl.ds(start, rows), 0:C] = pltpu.roll(v, 1, 0).astype(BF16)
    dst[pl.ds(start, rows), C : 2 * C] = v.astype(BF16)
    dst[pl.ds(start, rows), 2 * C : 3 * C] = pltpu.roll(v, rows - 1, 0).astype(BF16)


def window(src, start, rows, stride):
    return jnp.concatenate(
        [src[pl.ds(pl.multiple_of(start + d * stride, 16), rows), :] for d in range(3)], axis=1
    )


def own_columns(rows):
    col = lax.broadcasted_iota(jnp.int32, (rows // WW, WW, C), 1).reshape(rows, C)
    return (col >= 4) & (col < 4 + W)


def zero_at(flag, ref, start, rows):
    @pl.when(flag)
    def _():
        ref[start : start + rows, :] = jnp.zeros((rows, ref.shape[1]), ref.dtype)


def contract(x_ref, g_val, base, stride, rows, out):
    for d in range(3):
        out[d * 768 : (d + 1) * 768, :] = lax.dot_general(
            x_ref[base + d * stride : base + d * stride + rows, :],
            g_val,
            (((0,), (0,)), ((), ())),
            preferred_element_type=F32,
        )


def block_start(t, half):
    return pl.multiple_of((t % 8 * 4 + t // 8 * 2 + half) * 72, 8)


def hand_out(g_ref, keep_hbm, sent_ref, send_hbm, core, keep_sem, send_sem):
    for t in range(16):
        pltpu.make_async_copy(g_ref.at[pl.ds(block_start(t, core), 72)], keep_hbm.at[t], keep_sem).start()

    for t in range(16):
        sent_ref[t] = g_ref[pl.ds(block_start(t, 1 - core), 72), :].astype(BF16)
    pltpu.make_async_copy(sent_ref, send_hbm, send_sem).start()


def inner(hi_hbm, tgt_hbm, w_ref, e_ref, kh_hbm, x3_hbm, ha_hbm, tgw_hbm, x3_ref, ha_ref, tgw_ref, hi_v, tgt_v, kh_ref, sem):
    fetch = [
        pltpu.make_async_copy(src, dst, sem.at[n])
        for n, (src, dst) in enumerate(((hi_hbm, hi_v), (kh_hbm, kh_ref), (tgt_hbm, tgt_v)))
    ]
    for copy in fetch:
        copy.start()
    leave = [
        pltpu.make_async_copy(src, dst, sem.at[3 + n])
        for n, (src, dst) in enumerate(((x3_ref, x3_hbm), (tgw_ref, tgw_hbm), (ha_ref, ha_hbm)))
    ]
    fetch[0].wait()

    def widen_rows(t, _):
        rows = pl.ds(pl.multiple_of(t * 8, 8), 8)
        wide = widen_hi(hi_v[rows].astype(F32), w_ref[rows].astype(F32), e_ref[rows].astype(F32))
        put3(x3_ref, pl.multiple_of(t * 256, 128), wide.reshape(256, C))
        return 0

    lax.fori_loop(0, 6, widen_rows, 0)
    leave[0].start()
    fetch[1].wait()
    fetch[2].wait()

    def widen_targets(t, _):
        rows = pl.ds(pl.multiple_of(t * 8, 8), 8)
        wide = widen_tgt(tgt_v[rows].astype(F32), w_ref[rows].astype(F32), e_ref[rows].astype(F32))
        tgw_ref[pl.ds(pl.multiple_of(t * 256, 128), 256), :] = wide.reshape(256, C).astype(BF16)
        return 0

    def conv(b, _):
        s = pl.multiple_of(b * 736, 32)
        ha_ref[pl.ds(s, 736), :] = jnp.maximum(
            jnp.dot(window(x3_ref, s, 736, WW), kh_ref[...], preferred_element_type=F32), 0.0
        ).astype(BF16)
        return 0

    lax.fori_loop(0, 6, widen_targets, 0, unroll=True)
    lax.fori_loop(0, 2, conv, 0, unroll=True)
    leave[1].start()
    leave[2].start()
    for copy in leave:
        copy.wait()


def main(
    pos_ref, land_ref, low_hbm, w_ref, e_ref, n_ref, s_ref, x3_hbm, ha_hbm, tgw_hbm, kh_hbm, kl_hbm, kj_hbm,
    keep_hbm, send_hbm,
    x3_ref, j3_ref, o3_ref, l3_ref, ha_ref, la_ref, og_ref, tg_ref, jg_ref, lg_ref, g_ref, sent_ref, up_ref,
    low_v, kh_ref, kl_ref, kj_ref, kt_ref, sem, keep_sem, send_sem,
):
    fetch = [
        pltpu.make_async_copy(src, dst, sem.at[n])
        for n, (src, dst) in enumerate(
            (
                (low_hbm, low_v),
                (kl_hbm, kl_ref),
                (kh_hbm, kh_ref),
                (x3_hbm, x3_ref.at[128:1664]),
                (ha_hbm, ha_ref.at[128:1600]),
                (kj_hbm, kj_ref),
                (tgw_hbm, tg_ref.at[64:1600]),
            )
        )
    ]
    for copy in fetch:
        copy.start()
    fetch_low, fetch_kl, fetch_kh, fetch_x3, fetch_ha, fetch_kj, fetch_tgt = fetch
    first = pos_ref[0] == 0
    last = pos_ref[0] == 7
    core = pos_ref[1]
    up_ref[...] = up_matrix()

    put3(l3_ref, 0, n_ref[192:240, :].astype(F32))
    put3(l3_ref, 304, s_ref[192:240, :].astype(F32))
    put3(x3_ref, 0, n_ref[0:128, :].astype(F32))
    put3(x3_ref, 1664, s_ref[0:128, :].astype(F32))
    tg_ref[0:64, :] = n_ref[128:192, :]
    tg_ref[1600:1664, :] = s_ref[128:192, :]
    zero_at(first, l3_ref, 0, 48)
    zero_at(last, l3_ref, 304, 48)
    zero_at(first, x3_ref, 0, 128)
    zero_at(last, x3_ref, 1664, 128)

    def weight_of(high_part, low_part):
        return ((high_part * 32.0 + low_part) * SCALE)[None]

    own = land_ref[0, 0]
    wland = w_ref[0:2].astype(F32)
    eland = e_ref[0:2].astype(F32)
    top = weight_of(n_ref[240:272, :].astype(F32), n_ref[272:304, :].astype(F32))
    mid = weight_of(
        land_row(0, (own // 32).astype(F32), wland, eland), land_row(1, (own % 32).astype(F32), wland, eland)
    )
    bot = weight_of(s_ref[240:272, :].astype(F32), s_ref[272:304, :].astype(F32))
    fetch_low.wait()
    put3(
        l3_ref,
        48,
        widen_low(low_v[...].astype(F32), w_ref[...].astype(F32), e_ref[...].astype(F32)).reshape(256, C),
    )
    fetch_kl.wait()
    la_ref[...] = jnp.maximum(
        jnp.dot(window(l3_ref, 0, 320, LWW), kl_ref[...], preferred_element_type=F32), 0.0
    ).astype(BF16)
    zero_at(first, la_ref, 0, 32)
    zero_at(last, la_ref, 288, 32)
    fetch_kh.wait()
    fetch_x3.wait()
    fetch_ha.wait()
    edges = jnp.concatenate([window(x3_ref, 0, 128, WW), window(x3_ref, 1600, 128, WW)], axis=0)
    act = jnp.maximum(jnp.dot(edges, kh_ref[...], preferred_element_type=F32), 0.0).astype(BF16)
    ha_ref[0:128, :] = act[0:128]
    ha_ref[1600:1728, :] = act[128:256]

    def high(b, _):
        s = pl.multiple_of(b * 576, 64)
        cells = la_ref[pl.ds(pl.multiple_of(b * 96, 32), 128), :]
        lift = jnp.dot(up_ref[...], cells, preferred_element_type=F32) * NINTH
        put3(j3_ref, s, ha_ref[pl.ds(s, 576), :].astype(F32) + lift)
        return 0

    lax.fori_loop(0, 3, high, 0, unroll=True)
    zero_at(first, j3_ref, 0, 96)
    zero_at(last, j3_ref, 51 * WW, 96)
    fetch_kj.wait()
    fetch_tgt.wait()

    def join(b, _):
        s = pl.multiple_of(b * 832, 32)
        y = jnp.dot(window(j3_ref, s, 832, WW), kj_ref[...], preferred_element_type=F32)
        diff = (y - tg_ref[pl.ds(s, 832), :].astype(F32)).reshape(26, WW, C)
        row = lax.broadcasted_iota(jnp.int32, (26, WW, C), 0) + b * 26
        weight = jnp.where(row < 2, top, jnp.where(row >= 50, bot, mid))
        grad = (weight * diff).reshape(832, C)
        put3(o3_ref, s, grad)
        og_ref[pl.ds(s, 832), :] = jnp.where(own_columns(832), grad, 0.0).astype(BF16)
        return 0

    lax.fori_loop(0, 2, join, 0, unroll=True)
    zero_at(first, o3_ref, 0, 64)
    zero_at(last, o3_ref, 50 * WW, 64)
    contract(j3_ref, og_ref[64:1600, :], 64, WW, 1536, g_ref.at[2])
    hand_out(g_ref.at[2], keep_hbm.at[2], sent_ref.at[2], send_hbm.at[2], core, keep_sem.at[2], send_sem.at[2])
    for tap in range(9):
        kt_ref[(8 - tap) * C : (9 - tap) * C, :] = kj_ref[tap * C : (tap + 1) * C, :].T

    def back(b, _):
        s = pl.multiple_of(b * 800, 32)
        y = jnp.dot(window(o3_ref, s, 800, WW), kt_ref[...], preferred_element_type=F32)
        jg_ref[pl.ds(s, 800), :] = y.astype(BF16)
        on = ha_ref[pl.ds(pl.multiple_of(s + 64, 32), 800), :].astype(F32) > 0
        og_ref[pl.ds(s, 800), :] = jnp.where(own_columns(800) & on, y, 0.0).astype(BF16)
        return 0

    lax.fori_loop(0, 2, back, 0, unroll=True)
    zero_at(first, jg_ref, 0, 32)
    zero_at(last, jg_ref, 49 * WW, 32)
    contract(x3_ref, og_ref[32:1568, :], 96, WW, 1536, g_ref.at[0])
    hand_out(g_ref.at[0], keep_hbm.at[0], sent_ref.at[0], send_hbm.at[0], core, keep_sem.at[0], send_sem.at[0])
    down = down_matrix()
    for b in range(2):
        lifted = jnp.dot(down, jg_ref[b * 768 : b * 768 + 832, :], preferred_element_type=F32) * NINTH
        on = la_ref[32 + b * 128 : 160 + b * 128, :].astype(F32) > 0
        lg_ref[b * 128 : (b + 1) * 128, :] = jnp.where(on, lifted, 0.0).astype(BF16)
    contract(l3_ref, lg_ref[...], 32, LWW, 256, g_ref.at[1])
    hand_out(g_ref.at[1], keep_hbm.at[1], sent_ref.at[1], send_hbm.at[1], core, keep_sem.at[1], send_sem.at[1])
    for n in range(3):
        pltpu.make_async_copy(g_ref.at[n, 0:1152], keep_hbm.at[n], keep_sem.at[n]).wait()
        pltpu.make_async_copy(sent_ref.at[n], send_hbm.at[n], send_sem.at[n]).wait()


def regroup_lanes(parts, rows):
    quarter = lax.broadcasted_iota(jnp.int32, (rows, 128), 1) // 32
    for q in range(4):
        out = None
        for g in range(4):
            shift = ((g - q) * 32) % 128
            turned = pltpu.roll(parts[g], shift, 1) if shift else parts[g]
            out = turned if out is None else jnp.where(quarter == g, turned, out)
        yield q, out


def merge(keep_hbm, recv_ref, out_ref, keep_ref, sem):
    copies = [
        pltpu.make_async_copy(keep_hbm.at[n, pl.ds(8 * xl, 8)], keep_ref.at[n, pl.ds(8 * xl, 8)], sem.at[2 * n + xl])
        for n in range(3)
        for xl in range(2)
    ]
    for copy in copies:
        copy.start()
    for n in range(3):
        for xl in range(2):
            copies[2 * n + xl].wait()

            def one(p, _):
                blocks = []
                for g in range(4):
                    at = xl * 8 + 2 * g + p
                    blocks.append(keep_ref[n, at] + recv_ref[n, at].astype(F32))
                for h in range(2):
                    parts = [v[:, h * 128 : (h + 1) * 128] for v in blocks]
                    for q, out in regroup_lanes(parts, 72):
                        out_ref[(h * 4 + q) * 4 + 2 * xl + p, n] = out.astype(BF16)
                return 0

            lax.fori_loop(0, 2, one, 0)


def total(in_ref, out_ref):
    quarter = lax.broadcasted_iota(jnp.int32, (56, 128), 1) // 32
    sums = []
    for n in range(3):
        acc = in_ref[0, n].astype(F32)
        for i in range(1, 32):
            acc = acc + in_ref[i, n].astype(F32)
        sums.append(acc)
    rows = jnp.concatenate(sums + [jnp.zeros((8, 128), F32)], axis=0)
    for g in range(4):
        out = None
        for s in range(4):
            shift = ((s - g) * 32) % 128
            part = rows[s * 56 : (s + 1) * 56]
            turned = pltpu.roll(part, shift, 1) if shift else part
            out = turned if out is None else jnp.where(quarter == s, turned, out)
        out_ref[g] = out


def finish(in_ref, a_ref, b_ref, c_ref):
    acc = in_ref[0].astype(F32)
    for i in range(1, 4):
        acc = acc + in_ref[i].astype(F32)
    rows = jnp.concatenate(
        [acc if s == 0 else pltpu.roll(acc, 128 - 32 * s, 1) for s in range(4)], axis=0
    )
    for g, ref in enumerate((a_ref, b_ref, c_ref)):
        ref[...] = rows[g * 72 : (g + 1) * 72].T[0:32]


def call(kernel, out, specs, scratch=(), outs=None, vmem=None):
    return pl.pallas_call(
        kernel,
        out_shape=tuple(jax.ShapeDtypeStruct(s, d) for s, d in out),
        in_specs=list(specs),
        out_specs=outs or tuple(VMEM for _ in out),
        scratch_shapes=list(scratch),
        compiler_params=pltpu.CompilerParams(vmem_limit_bytes=vmem) if vmem else None,
    )


def ring(count, step):
    return [(i, (i + step) % count) for i in range(count)]


FIRST = ("yh", "yl", "xh", "xl", "zl")
SECOND = ("zh", "zm")


def step(hi, low, kh, kl, kj, tgt, land):
    dma = pltpu.SemaphoreType.DMA
    west, east, edges = call(
        pack_lon,
        [((H, 8, C), BF16)] * 2 + [((2, 7, W, C), BF16)],
        [SMEM] + [HBM] * 3,
        [pltpu.VMEM((2, H, 8, C), BF16), pltpu.VMEM((2, H, 8, C), BF16), pltpu.VMEM((LH, LW, C), BF16), dma((9,))],
        vmem=FULL,
    )(land, hi, tgt, low)
    from_e = lax.ppermute(west, LON, ring(32, -1))
    from_w = lax.ppermute(east, LON, ring(32, 1))
    north, south = call(pack_lat, [((PK, C), BF16)] * 2, [SMEM] + [VMEM] * 3, vmem=6 * MIB)(land, edges, from_w, from_e)
    from_s = lax.ppermute(north, LAT, ring(8, -1))
    from_n = lax.ppermute(south, LAT, ring(8, 1))
    pos = jnp.stack([lax.axis_index(LAT), lax.axis_index("core")]).astype(jnp.int32)
    weights = [k.reshape(9 * C, C) for k in (kh, kl, kj)]
    saved = call(
        inner,
        [((1536, 768), BF16), ((1472, C), BF16), ((1536, C), BF16)],
        [HBM] * 2 + [VMEM] * 2 + [HBM],
        [
            pltpu.VMEM((1536, 768), BF16),
            pltpu.VMEM((1472, C), BF16),
            pltpu.VMEM((1536, C), BF16),
            pltpu.VMEM((H, W, C), BF16),
            pltpu.VMEM((H, W, C), BF16),
            pltpu.VMEM((2304, C), BF16),
            dma((6,)),
        ],
        outs=(HBM,) * 3,
        vmem=MAIN_LIMIT,
    )(hi, tgt, from_w, from_e, weights[0])
    keep, send = call(
        main,
        [((3, 16, 72, C), F32), ((3, 16, 72, C), BF16)],
        [SMEM] * 2 + [HBM] + [VMEM] * 4 + [HBM] * 6,
        [
            pltpu.VMEM((1792, 768), BF16),
            pltpu.VMEM((1728, 768), BF16),
            pltpu.VMEM((1664, 768), BF16),
            pltpu.VMEM((352, 768), BF16),
            pltpu.VMEM((1728, C), BF16),
            pltpu.VMEM((320, C), BF16),
            pltpu.VMEM((1664, C), BF16),
            pltpu.VMEM((1664, C), BF16),
            pltpu.VMEM((1600, C), BF16),
            pltpu.VMEM((256, C), BF16),
            pltpu.VMEM((3, 2304, C), F32),
            pltpu.VMEM((3, 16, 72, C), BF16),
            pltpu.VMEM((576, 128), BF16),
            pltpu.VMEM((LH, LW, C), BF16),
            pltpu.VMEM((2304, C), BF16),
            pltpu.VMEM((2304, C), BF16),
            pltpu.VMEM((2304, C), BF16),
            pltpu.VMEM((2304, C), BF16),
            dma((7,)),
            dma((3,)),
            dma((3,)),
        ],
        outs=(HBM, HBM),
        vmem=MAIN_LIMIT,
    )(pos, land, low, from_w, from_e, from_n, from_s, *saved, *weights)
    recv = lax.ppermute(send, "core", ring(2, 1))
    (parts,) = call(
        merge, [((32, 3, 72, 128), BF16)], [HBM, VMEM], [pltpu.VMEM((3, 16, 72, C), F32), dma((6,))], vmem=MERGE_LIMIT
    )(keep, recv)
    parts = lax.all_to_all(parts, FIRST, 0, 0, tiled=True)
    (parts,) = call(total, [((4, 56, 128), F32)], [VMEM], vmem=6 * MIB)(parts)
    parts = lax.all_to_all(parts, SECOND, 0, 0, tiled=True)
    grads = call(finish, [((32, 72), F32)] * 3, [VMEM], vmem=2 * MIB)(parts)
    return tuple(g.T for g in grads)


def solution(mesh):
    fine = Mesh(mesh.devices.reshape((2,) * 8), LAT + LON)
    tile = P(LAT, LON, None)
    return jax.shard_map(
        step,
        mesh=fine,
        in_specs=(tile, tile, P(), P(), P(), tile, P(LAT, LON)),
        out_specs=(P(LON, LAT),) * 3,
        check_vma=False,
    )
```

```python
import jax
import jax.numpy as jnp
from jax import lax
from jax.experimental import pallas as pl
from jax.experimental.pallas import tpu as pltpu
from jax.sharding import Mesh, PartitionSpec as P

F32 = jnp.float32
BF16 = jnp.bfloat16
C = 256
H, W = 48, 24
LH, LW = 16, 8
WW = 32
LWW = 16
LAT = ("yh", "yl", "xh")
LON = ("zh", "zm", "zl", "xl", "core")
SCALE = 2.0 / (H * W * H * W)
NINTH = 1.0 / 9.0
PK = 240
MIB = 1024 * 1024
MAIN_LIMIT = 64 * MIB - 12_000_000
LON_LIMIT = 64 * MIB - 11_200_000
MERGE_LIMIT = 64 * MIB - 15_500_000
VMEM = pl.BlockSpec(memory_space=pltpu.VMEM)
SMEM = pl.BlockSpec(memory_space=pltpu.SMEM)
HBM = pl.BlockSpec(memory_space=pltpu.HBM)


def up_matrix():
    def weight(m, r, cell):
        side = jnp.where(cell == m, 2.0, jnp.where(cell == m + r - 1, 1.0, 0.0))
        return jnp.where(r == 1, jnp.where(cell == m, 3.0, 0.0), side)

    i = lax.broadcasted_iota(jnp.int32, (18, 1, 8 * LWW), 0)
    e = lax.broadcasted_iota(jnp.int32, (18, 1, 8 * LWW), 2) // LWW
    j = lax.broadcasted_iota(jnp.int32, (1, WW, 8 * LWW), 1) + 2
    f = lax.broadcasted_iota(jnp.int32, (1, WW, 8 * LWW), 2) % LWW
    both = weight(i // 3 + 1, i % 3, e) * weight(j // 3 + 1, j % 3, f)
    return both.reshape(18 * WW, 8 * LWW).astype(BF16)


def down_matrix():
    def weight(tap):
        return jnp.maximum(3 - jnp.abs(tap - 2), 0).astype(F32)

    m = lax.broadcasted_iota(jnp.int32, (8, 1, 26 * WW), 0)
    d = lax.broadcasted_iota(jnp.int32, (8, 1, 26 * WW), 2) // WW
    f = lax.broadcasted_iota(jnp.int32, (1, LWW, 26 * WW), 1) - 3
    j = lax.broadcasted_iota(jnp.int32, (1, LWW, 26 * WW), 2) % WW - 3
    both = weight(d - 3 * m) * jnp.where((f >= 0) & (f < LW), weight(j - 3 * f), 0.0)
    return both.reshape(8 * LWW, 26 * WW).astype(BF16)


def pack_lon(land_ref, hi_ref, tgt_ref, low_ref, west_ref, east_ref, edge_ref, hi_v, tgt_v, low_v, sem):
    copies = [
        pltpu.make_async_copy(src.at[:, pl.ds(start, 8), :], dst.at[side], sem.at[2 * n + side])
        for n, (src, dst) in enumerate(((hi_ref, hi_v), (tgt_ref, tgt_v)))
        for side, start in enumerate((0, 16))
    ]
    copies.append(pltpu.make_async_copy(low_ref, low_v, sem.at[4]))
    for side in range(2):
        copies.append(pltpu.make_async_copy(hi_ref.at[pl.ds(44 * side, 4)], edge_ref.at[side, 0:4], sem.at[5 + side]))
        copies.append(pltpu.make_async_copy(tgt_ref.at[pl.ds(46 * side, 2)], edge_ref.at[side, 4:6], sem.at[7 + side]))
    for copy in copies:
        copy.start()
    land = land_ref[0, 0]
    sub = lax.broadcasted_iota(jnp.int32, (H, 8, C), 1)
    row = lax.broadcasted_iota(jnp.int32, (H, 8, C), 0)
    lands = jnp.where(row % 2 == 0, (land // 32).astype(F32), (land % 32).astype(F32))
    for copy in copies:
        copy.wait()
    low = low_v[...].astype(F32)

    def rest(start):
        cells = jnp.stack([pltpu.roll(low, (7 - start - b) % 8, 1) for b in range(3)], axis=1)
        return jnp.where(sub == 6, lands, cells.reshape(H, 8, C))

    west = jnp.where(
        sub < 4, hi_v[0].astype(F32), jnp.where(sub < 6, pltpu.roll(tgt_v[0].astype(F32), 4, 1), rest(0))
    )
    east = jnp.where(
        sub < 4,
        pltpu.roll(hi_v[1].astype(F32), 4, 1),
        jnp.where(sub < 6, pltpu.roll(tgt_v[1].astype(F32), 6, 1), rest(5)),
    )
    west_ref[...] = west.astype(BF16)
    east_ref[...] = east.astype(BF16)
    for side in range(2):
        edge_ref[side, 6] = low_v[13 * side : 13 * side + 3].astype(F32).reshape(24, C).astype(BF16)


def widen_pixels(own, left, right):
    turned = [pltpu.roll(own[:, 8 * g : 8 * g + 8], 4, 1) for g in range(3)]
    parts = [left] + turned + [right]
    low_half = lax.broadcasted_iota(jnp.int32, left.shape, 1) < 4
    return jnp.concatenate([jnp.where(low_half, parts[g], parts[g + 1]) for g in range(4)], axis=1)


def widen_hi(own, wpk, epk):
    return widen_pixels(own, wpk, pltpu.roll(epk, 4, 1))


def widen_tgt(own, wpk, epk):
    return widen_pixels(own, pltpu.roll(wpk, 6, 1), epk)


def widen_low(own, wpk, epk):
    rows = own.shape[0]
    own = pltpu.roll(own, 3, 1)
    sub = lax.broadcasted_iota(jnp.int32, own.shape, 1)
    wpk = wpk.reshape(rows, 3, 8, C)
    epk = epk.reshape(rows, 3, 8, C)
    left, right = own, own
    for b in range(3):
        left = jnp.where(sub == b, pltpu.roll(wpk[:, b], b + 1, 1), left)
        right = jnp.where(sub == 3 + b, pltpu.roll(epk[:, b], b + 4, 1), right)
    return jnp.concatenate([left, right], axis=1)


def land_columns(left, own, right):
    col = lax.broadcasted_iota(jnp.int32, (WW, C), 0)
    weight = jnp.where(col < 4, left, jnp.where(col < 4 + W, own, right))
    return (weight * SCALE)[None]


def pack_lat(land_ref, own_ref, w_ref, e_ref, north_ref, south_ref):
    land = land_ref[0, 0]
    wpk = w_ref[0:2].astype(F32)
    epk = e_ref[0:2].astype(F32)
    area = lax.broadcasted_iota(jnp.int32, (3, LWW, C), 0)
    col = lax.broadcasted_iota(jnp.int32, (3, LWW, C), 1)

    def lands(part, own):
        left = wpk[part, 6:7, :][None]
        right = epk[part, 6:7, :][None]
        return jnp.where(area == 0, left, jnp.where(area == 1, own, right))

    high_part = lands(0, (land // 32).astype(F32))
    low_part = lands(1, (land % 32).astype(F32))
    for side, out_ref in enumerate((north_ref, south_ref)):
        def edge(ref, depth):
            start = (H - depth) * side
            return ref[start : start + depth].astype(F32)

        own = own_ref[side].astype(F32)
        hi = widen_hi(own[0:4], edge(w_ref, 4), edge(e_ref, 4))
        tgt = widen_tgt(own[4:6], edge(w_ref, 2), edge(e_ref, 2))
        low = widen_low(own[6].reshape(3, 8, C), edge(w_ref, 9), edge(e_ref, 9))
        low = jnp.where(col == 14, high_part, jnp.where(col == 15, low_part, low))
        out_ref[0:128] = hi.reshape(128, C).astype(BF16)
        out_ref[128:192] = tgt.reshape(64, C).astype(BF16)
        out_ref[192:240] = low.reshape(48, C).astype(BF16)


def put3(dst, start, v):
    rows = v.shape[0]
    dst[pl.ds(start, rows), 0:C] = pltpu.roll(v, 1, 0).astype(BF16)
    dst[pl.ds(start, rows), C : 2 * C] = v.astype(BF16)
    dst[pl.ds(start, rows), 2 * C : 3 * C] = pltpu.roll(v, rows - 1, 0).astype(BF16)


def window(src, start, rows, stride):
    return jnp.concatenate(
        [src[pl.ds(pl.multiple_of(start + d * stride, 16), rows), :] for d in range(3)], axis=1
    )


def own_columns(rows):
    col = lax.broadcasted_iota(jnp.int32, (rows // WW, WW, C), 1).reshape(rows, C)
    return (col >= 4) & (col < 4 + W)


def zero_at(flag, ref, start, rows):
    @pl.when(flag)
    def _():
        ref[start : start + rows, :] = jnp.zeros((rows, ref.shape[1]), ref.dtype)


def contract(x_ref, g_val, base, stride, rows, out):
    for d in range(3):
        out[d * 768 : (d + 1) * 768, :] = lax.dot_general(
            x_ref[base + d * stride : base + d * stride + rows, :],
            g_val,
            (((0,), (0,)), ((), ())),
            preferred_element_type=F32,
        )


def block_start(t, half):
    return pl.multiple_of((t % 8 * 4 + t // 8 * 2 + half) * 72, 8)


def hand_out(g_ref, keep_hbm, sent_ref, send_hbm, core, keep_sem, send_sem):
    for t in range(16):
        pltpu.make_async_copy(g_ref.at[pl.ds(block_start(t, core), 72)], keep_hbm.at[t], keep_sem).start()

    for t in range(16):
        sent_ref[t] = g_ref[pl.ds(block_start(t, 1 - core), 72), :].astype(BF16)
    pltpu.make_async_copy(sent_ref, send_hbm, send_sem).start()


def inner(hi_hbm, tgt_hbm, w_ref, e_ref, kh_hbm, x3_hbm, ha_hbm, tgw_hbm, x3_ref, ha_ref, tgw_ref, hi_v, tgt_v, kh_ref, sem):
    fetch = [
        pltpu.make_async_copy(src, dst, sem.at[n])
        for n, (src, dst) in enumerate(((hi_hbm, hi_v), (kh_hbm, kh_ref), (tgt_hbm, tgt_v)))
    ]
    for copy in fetch:
        copy.start()
    leave = [
        pltpu.make_async_copy(src, dst, sem.at[3 + n])
        for n, (src, dst) in enumerate(((x3_ref, x3_hbm), (tgw_ref, tgw_hbm), (ha_ref, ha_hbm)))
    ]
    fetch[0].wait()

    def widen_rows(t, _):
        rows = pl.ds(pl.multiple_of(t * 8, 8), 8)
        wide = widen_hi(hi_v[rows].astype(F32), w_ref[rows].astype(F32), e_ref[rows].astype(F32))
        put3(x3_ref, pl.multiple_of(t * 256, 128), wide.reshape(256, C))
        return 0

    lax.fori_loop(0, 6, widen_rows, 0)
    leave[0].start()
    fetch[1].wait()
    fetch[2].wait()

    def widen_targets(t, _):
        rows = pl.ds(pl.multiple_of(t * 8, 8), 8)
        wide = widen_tgt(tgt_v[rows].astype(F32), w_ref[rows].astype(F32), e_ref[rows].astype(F32))
        tgw_ref[pl.ds(pl.multiple_of(t * 256, 128), 256), :] = wide.reshape(256, C).astype(BF16)
        return 0

    def conv(b, _):
        s = pl.multiple_of(b * 736, 32)
        ha_ref[pl.ds(s, 736), :] = jnp.maximum(
            jnp.dot(window(x3_ref, s, 736, WW), kh_ref[...], preferred_element_type=F32), 0.0
        ).astype(BF16)
        return 0

    lax.fori_loop(0, 6, widen_targets, 0, unroll=True)
    lax.fori_loop(0, 2, conv, 0, unroll=True)
    leave[1].start()
    leave[2].start()
    for copy in leave:
        copy.wait()


def main(
    pos_ref, land_ref, low_hbm, w_ref, e_ref, n_ref, s_ref, x3_hbm, ha_hbm, tgw_hbm, kh_hbm, kl_hbm, kj_hbm,
    keep_hbm, send_hbm,
    x3_ref, j3_ref, o3_ref, l3_ref, ha_ref, la_ref, og_ref, tg_ref, jg_ref, lg_ref, g_ref, sent_ref, up_ref,
    low_v, kh_ref, kl_ref, kj_ref, kt_ref, sem, keep_sem, send_sem,
):
    fetch = [
        pltpu.make_async_copy(src, dst, sem.at[n])
        for n, (src, dst) in enumerate(
            (
                (low_hbm, low_v),
                (kl_hbm, kl_ref),
                (kh_hbm, kh_ref),
                (x3_hbm, x3_ref.at[128:1664]),
                (ha_hbm, ha_ref.at[128:1600]),
                (kj_hbm, kj_ref),
                (tgw_hbm, tg_ref.at[64:1600]),
            )
        )
    ]
    for copy in fetch:
        copy.start()
    fetch_low, fetch_kl, fetch_kh, fetch_x3, fetch_ha, fetch_kj, fetch_tgt = fetch
    first = pos_ref[0] == 0
    last = pos_ref[0] == 7
    core = pos_ref[1]
    up_ref[...] = up_matrix()

    put3(l3_ref, 0, n_ref[192:240, :].astype(F32))
    put3(l3_ref, 304, s_ref[192:240, :].astype(F32))
    put3(x3_ref, 0, n_ref[0:128, :].astype(F32))
    put3(x3_ref, 1664, s_ref[0:128, :].astype(F32))
    tg_ref[0:64, :] = n_ref[128:192, :]
    tg_ref[1600:1664, :] = s_ref[128:192, :]
    zero_at(first, l3_ref, 0, 48)
    zero_at(last, l3_ref, 304, 48)
    zero_at(first, x3_ref, 0, 128)
    zero_at(last, x3_ref, 1664, 128)

    def lands_of(ref):
        rows = ref[192:240, :].astype(F32)
        pairs = [rows[16 * n + 14 : 16 * n + 16] for n in range(3)]
        return land_columns(*[pair[0:1] * 32.0 + pair[1:2] for pair in pairs])

    top = lands_of(n_ref)
    bot = lands_of(s_ref)
    mid = land_columns(
        w_ref[0, 6:7, :].astype(F32) * 32.0 + w_ref[1, 6:7, :].astype(F32),
        land_ref[0, 0].astype(F32),
        e_ref[0, 6:7, :].astype(F32) * 32.0 + e_ref[1, 6:7, :].astype(F32),
    )
    fetch_low.wait()
    put3(
        l3_ref,
        48,
        widen_low(low_v[...].astype(F32), w_ref[...].astype(F32), e_ref[...].astype(F32)).reshape(256, C),
    )
    fetch_kl.wait()
    la_ref[...] = jnp.maximum(
        jnp.dot(window(l3_ref, 0, 320, LWW), kl_ref[...], preferred_element_type=F32), 0.0
    ).astype(BF16)
    zero_at(first, la_ref, 0, 32)
    zero_at(last, la_ref, 288, 32)
    fetch_kh.wait()
    fetch_x3.wait()
    fetch_ha.wait()
    edges = jnp.concatenate([window(x3_ref, 0, 128, WW), window(x3_ref, 1600, 128, WW)], axis=0)
    act = jnp.maximum(jnp.dot(edges, kh_ref[...], preferred_element_type=F32), 0.0).astype(BF16)
    ha_ref[0:128, :] = act[0:128]
    ha_ref[1600:1728, :] = act[128:256]

    def high(b, _):
        s = pl.multiple_of(b * 576, 64)
        cells = la_ref[pl.ds(pl.multiple_of(b * 96, 32), 128), :]
        lift = jnp.dot(up_ref[...], cells, preferred_element_type=F32) * NINTH
        put3(j3_ref, s, ha_ref[pl.ds(s, 576), :].astype(F32) + lift)
        return 0

    lax.fori_loop(0, 3, high, 0, unroll=True)
    zero_at(first, j3_ref, 0, 96)
    zero_at(last, j3_ref, 51 * WW, 96)
    fetch_kj.wait()
    fetch_tgt.wait()

    def join(b, _):
        s = pl.multiple_of(b * 832, 32)
        y = jnp.dot(window(j3_ref, s, 832, WW), kj_ref[...], preferred_element_type=F32)
        diff = (y - tg_ref[pl.ds(s, 832), :].astype(F32)).reshape(26, WW, C)
        row = lax.broadcasted_iota(jnp.int32, (26, WW, C), 0) + b * 26
        weight = jnp.where(row < 2, top, jnp.where(row >= 50, bot, mid))
        grad = (weight * diff).reshape(832, C)
        put3(o3_ref, s, grad)
        og_ref[pl.ds(s, 832), :] = jnp.where(own_columns(832), grad, 0.0).astype(BF16)
        return 0

    lax.fori_loop(0, 2, join, 0, unroll=True)
    zero_at(first, o3_ref, 0, 64)
    zero_at(last, o3_ref, 50 * WW, 64)
    contract(j3_ref, og_ref[64:1600, :], 64, WW, 1536, g_ref.at[2])
    hand_out(g_ref.at[2], keep_hbm.at[2], sent_ref.at[2], send_hbm.at[2], core, keep_sem.at[2], send_sem.at[2])
    for tap in range(9):
        kt_ref[(8 - tap) * C : (9 - tap) * C, :] = kj_ref[tap * C : (tap + 1) * C, :].T

    def back(b, _):
        s = pl.multiple_of(b * 800, 32)
        y = jnp.dot(window(o3_ref, s, 800, WW), kt_ref[...], preferred_element_type=F32)
        jg_ref[pl.ds(s, 800), :] = y.astype(BF16)
        on = ha_ref[pl.ds(pl.multiple_of(s + 64, 32), 800), :].astype(F32) > 0
        og_ref[pl.ds(s, 800), :] = jnp.where(own_columns(800) & on, y, 0.0).astype(BF16)
        return 0

    lax.fori_loop(0, 2, back, 0, unroll=True)
    zero_at(first, jg_ref, 0, 32)
    zero_at(last, jg_ref, 49 * WW, 32)
    contract(x3_ref, og_ref[32:1568, :], 96, WW, 1536, g_ref.at[0])
    hand_out(g_ref.at[0], keep_hbm.at[0], sent_ref.at[0], send_hbm.at[0], core, keep_sem.at[0], send_sem.at[0])
    down = down_matrix()
    for b in range(2):
        lifted = jnp.dot(down, jg_ref[b * 768 : b * 768 + 832, :], preferred_element_type=F32) * NINTH
        on = la_ref[32 + b * 128 : 160 + b * 128, :].astype(F32) > 0
        lg_ref[b * 128 : (b + 1) * 128, :] = jnp.where(on, lifted, 0.0).astype(BF16)
    contract(l3_ref, lg_ref[...], 32, LWW, 256, g_ref.at[1])
    hand_out(g_ref.at[1], keep_hbm.at[1], sent_ref.at[1], send_hbm.at[1], core, keep_sem.at[1], send_sem.at[1])
    for n in range(3):
        pltpu.make_async_copy(g_ref.at[n, 0:1152], keep_hbm.at[n], keep_sem.at[n]).wait()
        pltpu.make_async_copy(sent_ref.at[n], send_hbm.at[n], send_sem.at[n]).wait()


def merge(keep_hbm, recv_ref, out_ref, keep_ref, sem):
    copies = [
        pltpu.make_async_copy(keep_hbm.at[n, pl.ds(8 * xl, 8)], keep_ref.at[n, pl.ds(8 * xl, 8)], sem.at[2 * n + xl])
        for n in range(3)
        for xl in range(2)
    ]
    for copy in copies:
        copy.start()
    quarter = lax.broadcasted_iota(jnp.int32, (72, 128), 1) // 32
    for n in range(3):
        for xl in range(2):
            copies[2 * n + xl].wait()

            def one(p, _):
                for h in range(2):
                    lanes = slice(h * 128, (h + 1) * 128)
                    parts = []
                    for g in range(4):
                        at = xl * 8 + 2 * g + p
                        v = keep_ref[n, at, :, lanes] + recv_ref[n, at, :, lanes].astype(F32)
                        parts.append(pltpu.roll(v, 32 * g, 1) if g else v)
                    for q in range(4):
                        out = parts[(3 - q) % 4]
                        for s in range(3):
                            out = jnp.where(quarter == s, parts[(s - q) % 4], out)
                        out_ref[(h * 4 + q) * 4 + 2 * xl + p, n] = out.astype(BF16)
                return 0

            lax.fori_loop(0, 2, one, 0)


def total(pos_ref, in_ref, out_ref):
    quarter = lax.broadcasted_iota(jnp.int32, (56, 128), 1) // 32
    back = (4 - pos_ref[0] % 4) % 4 * 32
    sums = []
    for n in range(3):
        acc = in_ref[0, n].astype(F32)
        for i in range(1, 32):
            acc = acc + in_ref[i, n].astype(F32)
        sums.append(acc)
    rows = pltpu.roll(jnp.concatenate(sums + [jnp.zeros((8, 128), F32)], axis=0), back, 1)
    for g in range(4):
        out = None
        for s in range(4):
            shift = ((s - g) * 32) % 128
            part = rows[s * 56 : (s + 1) * 56]
            turned = pltpu.roll(part, shift, 1) if shift else part
            out = turned if out is None else jnp.where(quarter == s, turned, out)
        out_ref[g] = out


def finish(in_ref, a_ref, b_ref, c_ref):
    acc = in_ref[0].astype(F32)
    for i in range(1, 4):
        acc = acc + in_ref[i].astype(F32)
    rows = jnp.concatenate(
        [acc if s == 0 else pltpu.roll(acc, 128 - 32 * s, 1) for s in range(4)], axis=0
    )
    for g, ref in enumerate((a_ref, b_ref, c_ref)):
        ref[...] = rows[g * 72 : (g + 1) * 72].T[0:32]


def call(kernel, out, specs, scratch=(), outs=None, vmem=None):
    return pl.pallas_call(
        kernel,
        out_shape=tuple(jax.ShapeDtypeStruct(s, d) for s, d in out),
        in_specs=list(specs),
        out_specs=outs or tuple(VMEM for _ in out),
        scratch_shapes=list(scratch),
        compiler_params=pltpu.CompilerParams(vmem_limit_bytes=vmem) if vmem else None,
    )


def ring(count, step):
    return [(i, (i + step) % count) for i in range(count)]


FIRST = ("yh", "yl", "xh", "xl", "zl")
SECOND = ("zh", "zm")


def step(hi, low, kh, kl, kj, tgt, land):
    dma = pltpu.SemaphoreType.DMA
    west, east, edges = call(
        pack_lon,
        [((H, 8, C), BF16)] * 2 + [((2, 7, W, C), BF16)],
        [SMEM] + [HBM] * 3,
        [pltpu.VMEM((2, H, 8, C), BF16), pltpu.VMEM((2, H, 8, C), BF16), pltpu.VMEM((LH, LW, C), BF16), dma((9,))],
        vmem=LON_LIMIT,
    )(land, hi, tgt, low)
    from_e = lax.ppermute(west, LON, ring(32, -1))
    from_w = lax.ppermute(east, LON, ring(32, 1))
    north, south = call(pack_lat, [((PK, C), BF16)] * 2, [SMEM] + [VMEM] * 3, vmem=6 * MIB)(land, edges, from_w, from_e)
    from_s = lax.ppermute(north, LAT, ring(8, -1))
    from_n = lax.ppermute(south, LAT, ring(8, 1))
    pos = jnp.stack([lax.axis_index(LAT), lax.axis_index("core")]).astype(jnp.int32)
    weights = [k.reshape(9 * C, C) for k in (kh, kl, kj)]
    saved = call(
        inner,
        [((1536, 768), BF16), ((1472, C), BF16), ((1536, C), BF16)],
        [HBM] * 2 + [VMEM] * 2 + [HBM],
        [
            pltpu.VMEM((1536, 768), BF16),
            pltpu.VMEM((1472, C), BF16),
            pltpu.VMEM((1536, C), BF16),
            pltpu.VMEM((H, W, C), BF16),
            pltpu.VMEM((H, W, C), BF16),
            pltpu.VMEM((2304, C), BF16),
            dma((6,)),
        ],
        outs=(HBM,) * 3,
        vmem=MAIN_LIMIT,
    )(hi, tgt, from_w, from_e, weights[0])
    keep, send = call(
        main,
        [((3, 16, 72, C), F32), ((3, 16, 72, C), BF16)],
        [SMEM] * 2 + [HBM] + [VMEM] * 4 + [HBM] * 6,
        [
            pltpu.VMEM((1792, 768), BF16),
            pltpu.VMEM((1728, 768), BF16),
            pltpu.VMEM((1664, 768), BF16),
            pltpu.VMEM((352, 768), BF16),
            pltpu.VMEM((1728, C), BF16),
            pltpu.VMEM((320, C), BF16),
            pltpu.VMEM((1664, C), BF16),
            pltpu.VMEM((1664, C), BF16),
            pltpu.VMEM((1600, C), BF16),
            pltpu.VMEM((256, C), BF16),
            pltpu.VMEM((3, 2304, C), F32),
            pltpu.VMEM((3, 16, 72, C), BF16),
            pltpu.VMEM((576, 128), BF16),
            pltpu.VMEM((LH, LW, C), BF16),
            pltpu.VMEM((2304, C), BF16),
            pltpu.VMEM((2304, C), BF16),
            pltpu.VMEM((2304, C), BF16),
            pltpu.VMEM((2304, C), BF16),
            dma((7,)),
            dma((3,)),
            dma((3,)),
        ],
        outs=(HBM, HBM),
        vmem=MAIN_LIMIT,
    )(pos, land, low, from_w, from_e, from_n, from_s, *saved, *weights)
    recv = lax.ppermute(send, "core", ring(2, 1))
    (parts,) = call(
        merge, [((32, 3, 72, 128), BF16)], [HBM, VMEM], [pltpu.VMEM((3, 16, 72, C), F32), dma((6,))], vmem=MERGE_LIMIT
    )(keep, recv)
    parts = lax.all_to_all(parts, FIRST, 0, 0, tiled=True)
    (parts,) = call(total, [((4, 56, 128), F32)], [SMEM, VMEM], vmem=6 * MIB)(pos, parts)
    parts = lax.all_to_all(parts, SECOND, 0, 0, tiled=True)
    grads = call(finish, [((32, 72), F32)] * 3, [VMEM], vmem=2 * MIB)(parts)
    return tuple(g.T for g in grads)


def solution(mesh):
    fine = Mesh(mesh.devices.reshape((2,) * 8), LAT + LON)
    tile = P(LAT, LON, None)
    return jax.shard_map(
        step,
        mesh=fine,
        in_specs=(tile, tile, P(), P(), P(), tile, P(LAT, LON)),
        out_specs=(P(LON, LAT),) * 3,
        check_vma=False,
    )
```

```python
import jax
import jax.numpy as jnp
from jax import lax
from jax.experimental import pallas as pl
from jax.experimental.pallas import tpu as pltpu
from jax.sharding import Mesh, PartitionSpec as P

F32 = jnp.float32
BF16 = jnp.bfloat16
C = 256
H, W = 48, 24
LH, LW = 16, 8
WW = 32
LWW = 16
LAT = ("yh", "yl", "xh")
LON = ("zh", "zm", "zl", "xl", "core")
SCALE = 2.0 / (H * W * H * W)
NINTH = 1.0 / 9.0
PK = 240
MIB = 1024 * 1024
MAIN_LIMIT = 64 * MIB - 12_000_000
LON_LIMIT = 64 * MIB - 11_200_000
MERGE_LIMIT = 64 * MIB - 15_500_000
VMEM = pl.BlockSpec(memory_space=pltpu.VMEM)
SMEM = pl.BlockSpec(memory_space=pltpu.SMEM)
HBM = pl.BlockSpec(memory_space=pltpu.HBM)


def up_matrix():
    def weight(m, r, cell):
        side = jnp.where(cell == m, 2.0, jnp.where(cell == m + r - 1, 1.0, 0.0))
        return jnp.where(r == 1, jnp.where(cell == m, 3.0, 0.0), side)

    i = lax.broadcasted_iota(jnp.int32, (18, 1, 8 * LWW), 0)
    e = lax.broadcasted_iota(jnp.int32, (18, 1, 8 * LWW), 2) // LWW
    j = lax.broadcasted_iota(jnp.int32, (1, WW, 8 * LWW), 1) + 2
    f = lax.broadcasted_iota(jnp.int32, (1, WW, 8 * LWW), 2) % LWW
    both = weight(i // 3 + 1, i % 3, e) * weight(j // 3 + 1, j % 3, f)
    return both.reshape(18 * WW, 8 * LWW).astype(BF16)


def down_matrix():
    def weight(tap):
        return jnp.maximum(3 - jnp.abs(tap - 2), 0).astype(F32)

    m = lax.broadcasted_iota(jnp.int32, (8, 1, 26 * WW), 0)
    d = lax.broadcasted_iota(jnp.int32, (8, 1, 26 * WW), 2) // WW
    f = lax.broadcasted_iota(jnp.int32, (1, LWW, 26 * WW), 1) - 3
    j = lax.broadcasted_iota(jnp.int32, (1, LWW, 26 * WW), 2) % WW - 3
    both = weight(d - 3 * m) * jnp.where((f >= 0) & (f < LW), weight(j - 3 * f), 0.0)
    return both.reshape(8 * LWW, 26 * WW).astype(BF16)


def pack_lon(land_ref, hi_ref, tgt_ref, low_ref, west_ref, east_ref, edge_ref, hi_v, tgt_v, low_v, sem):
    copies = [
        pltpu.make_async_copy(src.at[:, pl.ds(start, 8), :], dst.at[side], sem.at[2 * n + side])
        for n, (src, dst) in enumerate(((hi_ref, hi_v), (tgt_ref, tgt_v)))
        for side, start in enumerate((0, 16))
    ]
    copies.append(pltpu.make_async_copy(low_ref, low_v, sem.at[4]))
    for side in range(2):
        copies.append(pltpu.make_async_copy(hi_ref.at[pl.ds(44 * side, 4)], edge_ref.at[side, 0:4], sem.at[5 + side]))
        copies.append(pltpu.make_async_copy(tgt_ref.at[pl.ds(46 * side, 2)], edge_ref.at[side, 4:6], sem.at[7 + side]))
    for copy in copies:
        copy.start()
    land = land_ref[0, 0]
    sub = lax.broadcasted_iota(jnp.int32, (H, 8, C), 1)
    row = lax.broadcasted_iota(jnp.int32, (H, 8, C), 0)
    lands = jnp.where(row % 2 == 0, (land // 32).astype(F32), (land % 32).astype(F32))
    for copy in copies:
        copy.wait()
    low = low_v[...].astype(F32)

    def rest(start):
        cells = jnp.stack([pltpu.roll(low, (7 - start - b) % 8, 1) for b in range(3)], axis=1)
        return jnp.where(sub == 6, lands, cells.reshape(H, 8, C))

    west = jnp.where(
        sub < 4, hi_v[0].astype(F32), jnp.where(sub < 6, pltpu.roll(tgt_v[0].astype(F32), 4, 1), rest(0))
    )
    east = jnp.where(
        sub < 4,
        pltpu.roll(hi_v[1].astype(F32), 4, 1),
        jnp.where(sub < 6, pltpu.roll(tgt_v[1].astype(F32), 6, 1), rest(5)),
    )
    west_ref[...] = west.astype(BF16)
    east_ref[...] = east.astype(BF16)
    for side in range(2):
        edge_ref[side, 6] = low_v[13 * side : 13 * side + 3].astype(F32).reshape(24, C).astype(BF16)


def widen_pixels(own, left, right):
    turned = [pltpu.roll(own[:, 8 * g : 8 * g + 8], 4, 1) for g in range(3)]
    parts = [left] + turned + [right]
    low_half = lax.broadcasted_iota(jnp.int32, left.shape, 1) < 4
    return jnp.concatenate([jnp.where(low_half, parts[g], parts[g + 1]) for g in range(4)], axis=1)


def widen_hi(own, wpk, epk):
    return widen_pixels(own, wpk, pltpu.roll(epk, 4, 1))


def widen_tgt(own, wpk, epk):
    return widen_pixels(own, pltpu.roll(wpk, 6, 1), epk)


def widen_low(own, wpk, epk):
    rows = own.shape[0]
    own = pltpu.roll(own, 3, 1)
    sub = lax.broadcasted_iota(jnp.int32, own.shape, 1)
    wpk = wpk.reshape(rows, 3, 8, C)
    epk = epk.reshape(rows, 3, 8, C)
    left, right = own, own
    for b in range(3):
        left = jnp.where(sub == b, pltpu.roll(wpk[:, b], b + 1, 1), left)
        right = jnp.where(sub == 3 + b, pltpu.roll(epk[:, b], b + 4, 1), right)
    return jnp.concatenate([left, right], axis=1)


def land_columns(left, own, right):
    col = lax.broadcasted_iota(jnp.int32, (WW, C), 0)
    weight = jnp.where(col < 4, left, jnp.where(col < 4 + W, own, right))
    return (weight * SCALE)[None]


def pack_lat(land_ref, own_ref, w_ref, e_ref, north_ref, south_ref):
    land = land_ref[0, 0]
    wpk = w_ref[0:2].astype(F32)
    epk = e_ref[0:2].astype(F32)
    area = lax.broadcasted_iota(jnp.int32, (3, LWW, C), 0)
    col = lax.broadcasted_iota(jnp.int32, (3, LWW, C), 1)

    def lands(part, own):
        left = wpk[part, 6:7, :][None]
        right = epk[part, 6:7, :][None]
        return jnp.where(area == 0, left, jnp.where(area == 1, own, right))

    high_part = lands(0, (land // 32).astype(F32))
    low_part = lands(1, (land % 32).astype(F32))
    for side, out_ref in enumerate((north_ref, south_ref)):
        def edge(ref, depth):
            start = (H - depth) * side
            return ref[start : start + depth].astype(F32)

        own = own_ref[side].astype(F32)
        hi = widen_hi(own[0:4], edge(w_ref, 4), edge(e_ref, 4))
        tgt = widen_tgt(own[4:6], edge(w_ref, 2), edge(e_ref, 2))
        low = widen_low(own[6].reshape(3, 8, C), edge(w_ref, 9), edge(e_ref, 9))
        low = jnp.where(col == 14, high_part, jnp.where(col == 15, low_part, low))
        out_ref[0:128] = hi.reshape(128, C).astype(BF16)
        out_ref[128:192] = tgt.reshape(64, C).astype(BF16)
        out_ref[192:240] = low.reshape(48, C).astype(BF16)


def put3(dst, start, v):
    rows = v.shape[0]
    dst[pl.ds(start, rows), 0:C] = pltpu.roll(v, 1, 0).astype(BF16)
    dst[pl.ds(start, rows), C : 2 * C] = v.astype(BF16)
    dst[pl.ds(start, rows), 2 * C : 3 * C] = pltpu.roll(v, rows - 1, 0).astype(BF16)


def window(src, start, rows, stride):
    return jnp.concatenate(
        [src[pl.ds(pl.multiple_of(start + d * stride, 16), rows), :] for d in range(3)], axis=1
    )


def own_columns(rows):
    col = lax.broadcasted_iota(jnp.int32, (rows // WW, WW, C), 1).reshape(rows, C)
    return (col >= 4) & (col < 4 + W)


def zero_at(flag, ref, start, rows):
    @pl.when(flag)
    def _():
        ref[start : start + rows, :] = jnp.zeros((rows, ref.shape[1]), ref.dtype)


def contract(x_ref, g_val, base, stride, rows, out):
    turned = g_val.T
    for d in range(3):
        out[d * 768 : (d + 1) * 768, :] = jnp.dot(
            turned, x_ref[base + d * stride : base + d * stride + rows, :], preferred_element_type=F32
        ).T


def block_start(t, half):
    return pl.multiple_of((t % 8 * 4 + t // 8 * 2 + half) * 72, 8)


def hand_out(g_ref, keep_hbm, sent_ref, send_hbm, core, keep_sem, send_sem):
    for t in range(16):
        pltpu.make_async_copy(g_ref.at[pl.ds(block_start(t, core), 72)], keep_hbm.at[t], keep_sem).start()

    for t in range(16):
        sent_ref[t] = g_ref[pl.ds(block_start(t, 1 - core), 72), :].astype(BF16)
    pltpu.make_async_copy(sent_ref, send_hbm, send_sem).start()


def inner(hi_hbm, tgt_hbm, w_ref, e_ref, kh_hbm, x3_hbm, ha_hbm, tgw_hbm, x3_ref, ha_ref, tgw_ref, hi_v, tgt_v, kh_ref, sem):
    fetch = [
        pltpu.make_async_copy(src, dst, sem.at[n])
        for n, (src, dst) in enumerate(((hi_hbm, hi_v), (kh_hbm, kh_ref), (tgt_hbm, tgt_v)))
    ]
    for copy in fetch:
        copy.start()
    leave = [
        pltpu.make_async_copy(src, dst, sem.at[3 + n])
        for n, (src, dst) in enumerate(((x3_ref, x3_hbm), (tgw_ref, tgw_hbm), (ha_ref, ha_hbm)))
    ]
    fetch[0].wait()

    def widen_rows(t, _):
        rows = pl.ds(pl.multiple_of(t * 8, 8), 8)
        wide = widen_hi(hi_v[rows].astype(F32), w_ref[rows].astype(F32), e_ref[rows].astype(F32))
        put3(x3_ref, pl.multiple_of(t * 256, 128), wide.reshape(256, C))
        return 0

    lax.fori_loop(0, 6, widen_rows, 0)
    leave[0].start()
    fetch[1].wait()
    fetch[2].wait()

    def widen_targets(t, _):
        rows = pl.ds(pl.multiple_of(t * 8, 8), 8)
        wide = widen_tgt(tgt_v[rows].astype(F32), w_ref[rows].astype(F32), e_ref[rows].astype(F32))
        tgw_ref[pl.ds(pl.multiple_of(t * 256, 128), 256), :] = wide.reshape(256, C).astype(BF16)
        return 0

    def conv(b, _):
        s = pl.multiple_of(b * 736, 32)
        ha_ref[pl.ds(s, 736), :] = jnp.maximum(
            jnp.dot(window(x3_ref, s, 736, WW), kh_ref[...], preferred_element_type=F32), 0.0
        ).astype(BF16)
        return 0

    lax.fori_loop(0, 6, widen_targets, 0, unroll=True)
    lax.fori_loop(0, 2, conv, 0, unroll=True)
    leave[1].start()
    leave[2].start()
    for copy in leave:
        copy.wait()


def main(
    pos_ref, land_ref, low_hbm, w_ref, e_ref, n_ref, s_ref, x3_hbm, ha_hbm, tgw_hbm, kh_hbm, kl_hbm, kj_hbm,
    keep_hbm, send_hbm,
    x3_ref, j3_ref, o3_ref, l3_ref, ha_ref, la_ref, og_ref, tg_ref, jg_ref, lg_ref, g_ref, sent_ref, up_ref,
    low_v, kh_ref, kl_ref, kj_ref, kt_ref, sem, keep_sem, send_sem,
):
    fetch = [
        pltpu.make_async_copy(src, dst, sem.at[n])
        for n, (src, dst) in enumerate(
            (
                (low_hbm, low_v),
                (kl_hbm, kl_ref),
                (kh_hbm, kh_ref),
                (x3_hbm, x3_ref.at[128:1664]),
                (ha_hbm, ha_ref.at[128:1600]),
                (kj_hbm, kj_ref),
                (tgw_hbm, tg_ref.at[64:1600]),
            )
        )
    ]
    for copy in fetch:
        copy.start()
    fetch_low, fetch_kl, fetch_kh, fetch_x3, fetch_ha, fetch_kj, fetch_tgt = fetch
    first = pos_ref[0] == 0
    last = pos_ref[0] == 7
    core = pos_ref[1]
    up_ref[...] = up_matrix()

    put3(l3_ref, 0, n_ref[192:240, :].astype(F32))
    put3(l3_ref, 304, s_ref[192:240, :].astype(F32))
    put3(x3_ref, 0, n_ref[0:128, :].astype(F32))
    put3(x3_ref, 1664, s_ref[0:128, :].astype(F32))
    tg_ref[0:64, :] = n_ref[128:192, :]
    tg_ref[1600:1664, :] = s_ref[128:192, :]
    zero_at(first, l3_ref, 0, 48)
    zero_at(last, l3_ref, 304, 48)
    zero_at(first, x3_ref, 0, 128)
    zero_at(last, x3_ref, 1664, 128)

    def lands_of(ref):
        rows = ref[192:240, :].astype(F32)
        pairs = [rows[16 * n + 14 : 16 * n + 16] for n in range(3)]
        return land_columns(*[pair[0:1] * 32.0 + pair[1:2] for pair in pairs])

    top = lands_of(n_ref)
    bot = lands_of(s_ref)
    mid = land_columns(
        w_ref[0, 6:7, :].astype(F32) * 32.0 + w_ref[1, 6:7, :].astype(F32),
        land_ref[0, 0].astype(F32),
        e_ref[0, 6:7, :].astype(F32) * 32.0 + e_ref[1, 6:7, :].astype(F32),
    )
    fetch_low.wait()
    put3(
        l3_ref,
        48,
        widen_low(low_v[...].astype(F32), w_ref[...].astype(F32), e_ref[...].astype(F32)).reshape(256, C),
    )
    fetch_kl.wait()
    la_ref[...] = jnp.maximum(
        jnp.dot(window(l3_ref, 0, 320, LWW), kl_ref[...], preferred_element_type=F32), 0.0
    ).astype(BF16)
    zero_at(first, la_ref, 0, 32)
    zero_at(last, la_ref, 288, 32)
    fetch_kh.wait()
    fetch_x3.wait()
    fetch_ha.wait()
    edges = jnp.concatenate([window(x3_ref, 0, 128, WW), window(x3_ref, 1600, 128, WW)], axis=0)
    act = jnp.maximum(jnp.dot(edges, kh_ref[...], preferred_element_type=F32), 0.0).astype(BF16)
    ha_ref[0:128, :] = act[0:128]
    ha_ref[1600:1728, :] = act[128:256]

    def high(b, _):
        s = pl.multiple_of(b * 576, 64)
        cells = la_ref[pl.ds(pl.multiple_of(b * 96, 32), 128), :]
        lift = jnp.dot(up_ref[...], cells, preferred_element_type=F32) * NINTH
        put3(j3_ref, s, ha_ref[pl.ds(s, 576), :].astype(F32) + lift)
        return 0

    lax.fori_loop(0, 3, high, 0, unroll=True)
    zero_at(first, j3_ref, 0, 96)
    zero_at(last, j3_ref, 51 * WW, 96)
    fetch_kj.wait()
    fetch_tgt.wait()

    def join(b, _):
        s = pl.multiple_of(b * 832, 32)
        y = jnp.dot(window(j3_ref, s, 832, WW), kj_ref[...], preferred_element_type=F32)
        diff = (y - tg_ref[pl.ds(s, 832), :].astype(F32)).reshape(26, WW, C)
        row = lax.broadcasted_iota(jnp.int32, (26, WW, C), 0) + b * 26
        weight = jnp.where(row < 2, top, jnp.where(row >= 50, bot, mid))
        grad = (weight * diff).reshape(832, C)
        put3(o3_ref, s, grad)
        og_ref[pl.ds(s, 832), :] = jnp.where(own_columns(832), grad, 0.0).astype(BF16)
        return 0

    lax.fori_loop(0, 2, join, 0, unroll=True)
    zero_at(first, o3_ref, 0, 64)
    zero_at(last, o3_ref, 50 * WW, 64)
    contract(j3_ref, og_ref[64:1600, :], 64, WW, 1536, g_ref.at[2])
    hand_out(g_ref.at[2], keep_hbm.at[2], sent_ref.at[2], send_hbm.at[2], core, keep_sem.at[2], send_sem.at[2])
    for tap in range(9):
        kt_ref[(8 - tap) * C : (9 - tap) * C, :] = kj_ref[tap * C : (tap + 1) * C, :].T

    def back(b, _):
        s = pl.multiple_of(b * 800, 32)
        y = jnp.dot(window(o3_ref, s, 800, WW), kt_ref[...], preferred_element_type=F32)
        jg_ref[pl.ds(s, 800), :] = y.astype(BF16)
        on = ha_ref[pl.ds(pl.multiple_of(s + 64, 32), 800), :].astype(F32) > 0
        og_ref[pl.ds(s, 800), :] = jnp.where(own_columns(800) & on, y, 0.0).astype(BF16)
        return 0

    lax.fori_loop(0, 2, back, 0, unroll=True)
    zero_at(first, jg_ref, 0, 32)
    zero_at(last, jg_ref, 49 * WW, 32)
    contract(x3_ref, og_ref[32:1568, :], 96, WW, 1536, g_ref.at[0])
    hand_out(g_ref.at[0], keep_hbm.at[0], sent_ref.at[0], send_hbm.at[0], core, keep_sem.at[0], send_sem.at[0])
    down = down_matrix()
    for b in range(2):
        lifted = jnp.dot(down, jg_ref[b * 768 : b * 768 + 832, :], preferred_element_type=F32) * NINTH
        on = la_ref[32 + b * 128 : 160 + b * 128, :].astype(F32) > 0
        lg_ref[b * 128 : (b + 1) * 128, :] = jnp.where(on, lifted, 0.0).astype(BF16)
    contract(l3_ref, lg_ref[...], 32, LWW, 256, g_ref.at[1])
    hand_out(g_ref.at[1], keep_hbm.at[1], sent_ref.at[1], send_hbm.at[1], core, keep_sem.at[1], send_sem.at[1])
    for n in range(3):
        pltpu.make_async_copy(g_ref.at[n, 0:1152], keep_hbm.at[n], keep_sem.at[n]).wait()
        pltpu.make_async_copy(sent_ref.at[n], send_hbm.at[n], send_sem.at[n]).wait()


def merge(keep_hbm, recv_ref, out_ref, keep_ref, sem):
    copies = [
        pltpu.make_async_copy(keep_hbm.at[n, pl.ds(8 * xl, 8)], keep_ref.at[n, pl.ds(8 * xl, 8)], sem.at[2 * n + xl])
        for n in range(3)
        for xl in range(2)
    ]
    for copy in copies:
        copy.start()
    quarter = lax.broadcasted_iota(jnp.int32, (72, 128), 1) // 32
    for n in range(3):
        for xl in range(2):
            copies[2 * n + xl].wait()

            def one(p, _):
                for h in range(2):
                    lanes = slice(h * 128, (h + 1) * 128)
                    parts = []
                    for g in range(4):
                        at = xl * 8 + 2 * g + p
                        v = keep_ref[n, at, :, lanes] + recv_ref[n, at, :, lanes].astype(F32)
                        parts.append(pltpu.roll(v, 32 * g, 1) if g else v)
                    for q in range(4):
                        out = parts[(3 - q) % 4]
                        for s in range(3):
                            out = jnp.where(quarter == s, parts[(s - q) % 4], out)
                        out_ref[(h * 4 + q) * 4 + 2 * xl + p, n] = out.astype(BF16)
                return 0

            lax.fori_loop(0, 2, one, 0)


def total(pos_ref, in_ref, out_ref):
    quarter = lax.broadcasted_iota(jnp.int32, (56, 128), 1) // 32
    mine = pos_ref[0] % 4
    sums = []
    for n in range(3):
        acc = in_ref[0, n].astype(F32)
        for i in range(1, 32):
            acc = acc + in_ref[i, n].astype(F32)
        sums.append(acc)
    rows = jnp.concatenate(sums + [jnp.zeros((8, 128), F32)], axis=0)
    for at in range(4):
        out = None
        for s in range(4):
            shift = ((s - at) * 32) % 128
            part = rows[s * 56 : (s + 1) * 56]
            turned = pltpu.roll(part, shift, 1) if shift else part
            out = turned if out is None else jnp.where(quarter == s, turned, out)
        out_ref[(at + 4 - mine) % 4] = out


def finish(in_ref, a_ref, b_ref, c_ref):
    acc = in_ref[0].astype(F32)
    for i in range(1, 4):
        acc = acc + in_ref[i].astype(F32)
    rows = jnp.concatenate(
        [acc if s == 0 else pltpu.roll(acc, 128 - 32 * s, 1) for s in range(4)], axis=0
    )
    for g, ref in enumerate((a_ref, b_ref, c_ref)):
        ref[...] = rows[g * 72 : (g + 1) * 72].T[0:32]


def call(kernel, out, specs, scratch=(), outs=None, vmem=None):
    return pl.pallas_call(
        kernel,
        out_shape=tuple(jax.ShapeDtypeStruct(s, d) for s, d in out),
        in_specs=list(specs),
        out_specs=outs or tuple(VMEM for _ in out),
        scratch_shapes=list(scratch),
        compiler_params=pltpu.CompilerParams(vmem_limit_bytes=vmem) if vmem else None,
    )


def ring(count, step):
    return [(i, (i + step) % count) for i in range(count)]


FIRST = ("yh", "yl", "xh", "xl", "zl")
SECOND = ("zh", "zm")


def step(hi, low, kh, kl, kj, tgt, land):
    dma = pltpu.SemaphoreType.DMA
    west, east, edges = call(
        pack_lon,
        [((H, 8, C), BF16)] * 2 + [((2, 7, W, C), BF16)],
        [SMEM] + [HBM] * 3,
        [pltpu.VMEM((2, H, 8, C), BF16), pltpu.VMEM((2, H, 8, C), BF16), pltpu.VMEM((LH, LW, C), BF16), dma((9,))],
        vmem=LON_LIMIT,
    )(land, hi, tgt, low)
    from_e = lax.ppermute(west, LON, ring(32, -1))
    from_w = lax.ppermute(east, LON, ring(32, 1))
    north, south = call(pack_lat, [((PK, C), BF16)] * 2, [SMEM] + [VMEM] * 3, vmem=6 * MIB)(land, edges, from_w, from_e)
    from_s = lax.ppermute(north, LAT, ring(8, -1))
    from_n = lax.ppermute(south, LAT, ring(8, 1))
    pos = jnp.stack([lax.axis_index(LAT), lax.axis_index("core")]).astype(jnp.int32)
    weights = [k.reshape(9 * C, C) for k in (kh, kl, kj)]
    saved = call(
        inner,
        [((1536, 768), BF16), ((1472, C), BF16), ((1536, C), BF16)],
        [HBM] * 2 + [VMEM] * 2 + [HBM],
        [
            pltpu.VMEM((1536, 768), BF16),
            pltpu.VMEM((1472, C), BF16),
            pltpu.VMEM((1536, C), BF16),
            pltpu.VMEM((H, W, C), BF16),
            pltpu.VMEM((H, W, C), BF16),
            pltpu.VMEM((2304, C), BF16),
            dma((6,)),
        ],
        outs=(HBM,) * 3,
        vmem=MAIN_LIMIT,
    )(hi, tgt, from_w, from_e, weights[0])
    keep, send = call(
        main,
        [((3, 16, 72, C), F32), ((3, 16, 72, C), BF16)],
        [SMEM] * 2 + [HBM] + [VMEM] * 4 + [HBM] * 6,
        [
            pltpu.VMEM((1792, 768), BF16),
            pltpu.VMEM((1728, 768), BF16),
            pltpu.VMEM((1664, 768), BF16),
            pltpu.VMEM((352, 768), BF16),
            pltpu.VMEM((1728, C), BF16),
            pltpu.VMEM((320, C), BF16),
            pltpu.VMEM((1664, C), BF16),
            pltpu.VMEM((1664, C), BF16),
            pltpu.VMEM((1600, C), BF16),
            pltpu.VMEM((256, C), BF16),
            pltpu.VMEM((3, 2304, C), F32),
            pltpu.VMEM((3, 16, 72, C), BF16),
            pltpu.VMEM((576, 128), BF16),
            pltpu.VMEM((LH, LW, C), BF16),
            pltpu.VMEM((2304, C), BF16),
            pltpu.VMEM((2304, C), BF16),
            pltpu.VMEM((2304, C), BF16),
            pltpu.VMEM((2304, C), BF16),
            dma((7,)),
            dma((3,)),
            dma((3,)),
        ],
        outs=(HBM, HBM),
        vmem=MAIN_LIMIT,
    )(pos, land, low, from_w, from_e, from_n, from_s, *saved, *weights)
    recv = lax.ppermute(send, "core", ring(2, 1))
    (parts,) = call(
        merge, [((32, 3, 72, 128), BF16)], [HBM, VMEM], [pltpu.VMEM((3, 16, 72, C), F32), dma((6,))], vmem=MERGE_LIMIT
    )(keep, recv)
    parts = lax.all_to_all(parts, FIRST, 0, 0, tiled=True)
    (parts,) = call(total, [((4, 56, 128), F32)], [SMEM, VMEM], vmem=6 * MIB)(pos, parts)
    parts = lax.all_to_all(parts, SECOND, 0, 0, tiled=True)
    grads = call(finish, [((32, 72), F32)] * 3, [VMEM], vmem=2 * MIB)(parts)
    return tuple(g.T for g in grads)


def solution(mesh):
    fine = Mesh(mesh.devices.reshape((2,) * 8), LAT + LON)
    tile = P(LAT, LON, None)
    return jax.shard_map(
        step,
        mesh=fine,
        in_specs=(tile, tile, P(), P(), P(), tile, P(LAT, LON)),
        out_specs=(P(LON, LAT),) * 3,
        check_vma=False,
    )
```

```python
import jax
import jax.numpy as jnp
from jax import lax
from jax.experimental import pallas as pl
from jax.experimental.pallas import tpu as pltpu
from jax.sharding import Mesh, PartitionSpec as P

F32 = jnp.float32
BF16 = jnp.bfloat16
C = 256
H, W = 48, 24
LH, LW = 16, 8
WW = 32
LWW = 16
LAT = ("yh", "yl", "xh")
LON = ("zh", "zm", "zl", "xl", "core")
SCALE = 2.0 / (H * W * H * W)
NINTH = 1.0 / 9.0
PK = 240
MIB = 1024 * 1024
MAIN_LIMIT = 64 * MIB - 12_000_000
LON_LIMIT = 64 * MIB - 11_200_000
MERGE_LIMIT = 64 * MIB - 15_500_000
VMEM = pl.BlockSpec(memory_space=pltpu.VMEM)
SMEM = pl.BlockSpec(memory_space=pltpu.SMEM)
HBM = pl.BlockSpec(memory_space=pltpu.HBM)


def up_matrix():
    def weight(m, r, cell):
        side = jnp.where(cell == m, 2.0, jnp.where(cell == m + r - 1, 1.0, 0.0))
        return jnp.where(r == 1, jnp.where(cell == m, 3.0, 0.0), side)

    i = lax.broadcasted_iota(jnp.int32, (18, 1, 8 * LWW), 0)
    e = lax.broadcasted_iota(jnp.int32, (18, 1, 8 * LWW), 2) // LWW
    j = lax.broadcasted_iota(jnp.int32, (1, WW, 8 * LWW), 1) + 2
    f = lax.broadcasted_iota(jnp.int32, (1, WW, 8 * LWW), 2) % LWW
    both = weight(i // 3 + 1, i % 3, e) * weight(j // 3 + 1, j % 3, f)
    return both.reshape(18 * WW, 8 * LWW).astype(BF16)


def down_matrix():
    def weight(tap):
        return jnp.maximum(3 - jnp.abs(tap - 2), 0).astype(F32)

    m = lax.broadcasted_iota(jnp.int32, (8, 1, 26 * WW), 0)
    d = lax.broadcasted_iota(jnp.int32, (8, 1, 26 * WW), 2) // WW
    f = lax.broadcasted_iota(jnp.int32, (1, LWW, 26 * WW), 1) - 3
    j = lax.broadcasted_iota(jnp.int32, (1, LWW, 26 * WW), 2) % WW - 3
    both = weight(d - 3 * m) * jnp.where((f >= 0) & (f < LW), weight(j - 3 * f), 0.0)
    return both.reshape(8 * LWW, 26 * WW).astype(BF16)


def pack_lon(land_ref, hi_ref, tgt_ref, low_ref, west_ref, east_ref, edge_ref, hi_v, tgt_v, low_v, sem):
    copies = [
        pltpu.make_async_copy(src.at[:, pl.ds(start, 8), :], dst.at[side], sem.at[2 * n + side])
        for n, (src, dst) in enumerate(((hi_ref, hi_v), (tgt_ref, tgt_v)))
        for side, start in enumerate((0, 16))
    ]
    copies.append(pltpu.make_async_copy(low_ref, low_v, sem.at[4]))
    for side in range(2):
        copies.append(pltpu.make_async_copy(hi_ref.at[pl.ds(44 * side, 4)], edge_ref.at[side, 0:4], sem.at[5 + side]))
        copies.append(pltpu.make_async_copy(tgt_ref.at[pl.ds(46 * side, 2)], edge_ref.at[side, 4:6], sem.at[7 + side]))
    for copy in copies:
        copy.start()
    land = land_ref[0, 0]
    sub = lax.broadcasted_iota(jnp.int32, (H, 8, C), 1)
    row = lax.broadcasted_iota(jnp.int32, (H, 8, C), 0)
    lands = jnp.where(row % 2 == 0, (land // 32).astype(F32), (land % 32).astype(F32))
    for copy in copies:
        copy.wait()
    low = low_v[...].astype(F32)

    def rest(start):
        cells = jnp.stack([pltpu.roll(low, (7 - start - b) % 8, 1) for b in range(3)], axis=1)
        return jnp.where(sub == 6, lands, cells.reshape(H, 8, C))

    west = jnp.where(
        sub < 4, hi_v[0].astype(F32), jnp.where(sub < 6, pltpu.roll(tgt_v[0].astype(F32), 4, 1), rest(0))
    )
    east = jnp.where(
        sub < 4,
        pltpu.roll(hi_v[1].astype(F32), 4, 1),
        jnp.where(sub < 6, pltpu.roll(tgt_v[1].astype(F32), 6, 1), rest(5)),
    )
    west_ref[...] = west.astype(BF16)
    east_ref[...] = east.astype(BF16)
    for side in range(2):
        edge_ref[side, 6] = low_v[13 * side : 13 * side + 3].astype(F32).reshape(24, C).astype(BF16)


def widen_pixels(own, left, right):
    turned = [pltpu.roll(own[:, 8 * g : 8 * g + 8], 4, 1) for g in range(3)]
    parts = [left] + turned + [right]
    low_half = lax.broadcasted_iota(jnp.int32, left.shape, 1) < 4
    return jnp.concatenate([jnp.where(low_half, parts[g], parts[g + 1]) for g in range(4)], axis=1)


def widen_hi(own, wpk, epk):
    return widen_pixels(own, wpk, pltpu.roll(epk, 4, 1))


def widen_tgt(own, wpk, epk):
    return widen_pixels(own, pltpu.roll(wpk, 6, 1), epk)


def widen_low(own, wpk, epk):
    rows = own.shape[0]
    own = pltpu.roll(own, 3, 1)
    sub = lax.broadcasted_iota(jnp.int32, own.shape, 1)
    wpk = wpk.reshape(rows, 3, 8, C)
    epk = epk.reshape(rows, 3, 8, C)
    left, right = own, own
    for b in range(3):
        left = jnp.where(sub == b, pltpu.roll(wpk[:, b], b + 1, 1), left)
        right = jnp.where(sub == 3 + b, pltpu.roll(epk[:, b], b + 4, 1), right)
    return jnp.concatenate([left, right], axis=1)


def land_columns(left, own, right):
    col = lax.broadcasted_iota(jnp.int32, (WW, C), 0)
    weight = jnp.where(col < 4, left, jnp.where(col < 4 + W, own, right))
    return (weight * SCALE)[None]


def pack_lat(land_ref, own_ref, w_ref, e_ref, north_ref, south_ref):
    land = land_ref[0, 0]
    wpk = w_ref[0:2].astype(F32)
    epk = e_ref[0:2].astype(F32)
    area = lax.broadcasted_iota(jnp.int32, (3, LWW, C), 0)
    col = lax.broadcasted_iota(jnp.int32, (3, LWW, C), 1)

    def lands(part, own):
        left = wpk[part, 6:7, :][None]
        right = epk[part, 6:7, :][None]
        return jnp.where(area == 0, left, jnp.where(area == 1, own, right))

    high_part = lands(0, (land // 32).astype(F32))
    low_part = lands(1, (land % 32).astype(F32))
    for side, out_ref in enumerate((north_ref, south_ref)):
        def edge(ref, depth):
            start = (H - depth) * side
            return ref[start : start + depth].astype(F32)

        own = own_ref[side].astype(F32)
        hi = widen_hi(own[0:4], edge(w_ref, 4), edge(e_ref, 4))
        tgt = widen_tgt(own[4:6], edge(w_ref, 2), edge(e_ref, 2))
        low = widen_low(own[6].reshape(3, 8, C), edge(w_ref, 9), edge(e_ref, 9))
        low = jnp.where(col == 14, high_part, jnp.where(col == 15, low_part, low))
        out_ref[0:128] = hi.reshape(128, C).astype(BF16)
        out_ref[128:192] = tgt.reshape(64, C).astype(BF16)
        out_ref[192:240] = low.reshape(48, C).astype(BF16)


def put3(dst, start, v):
    rows = v.shape[0]
    dst[pl.ds(start, rows), 0:C] = pltpu.roll(v, 1, 0).astype(BF16)
    dst[pl.ds(start, rows), C : 2 * C] = v.astype(BF16)
    dst[pl.ds(start, rows), 2 * C : 3 * C] = pltpu.roll(v, rows - 1, 0).astype(BF16)


def window(src, start, rows, stride):
    return jnp.concatenate(
        [src[pl.ds(pl.multiple_of(start + d * stride, 16), rows), :] for d in range(3)], axis=1
    )


def own_columns(rows):
    col = lax.broadcasted_iota(jnp.int32, (rows // WW, WW, C), 1).reshape(rows, C)
    return (col >= 4) & (col < 4 + W)


def zero_at(flag, ref, start, rows):
    @pl.when(flag)
    def _():
        ref[start : start + rows, :] = jnp.zeros((rows, ref.shape[1]), ref.dtype)


def contract(x_ref, g_val, base, stride, rows, out):
    turned = g_val.T
    for d in range(3):
        out[d * 768 : (d + 1) * 768, :] = jnp.dot(
            turned, x_ref[base + d * stride : base + d * stride + rows, :], preferred_element_type=F32
        ).T


def block_start(t, half):
    return pl.multiple_of((t % 8 * 4 + t // 8 * 2 + half) * 72, 8)


def hand_out(g_ref, keep_hbm, sent_ref, send_hbm, core, keep_sem, send_sem):
    for t in range(16):
        pltpu.make_async_copy(g_ref.at[pl.ds(block_start(t, core), 72)], keep_hbm.at[t], keep_sem).start()

    for t in range(16):
        sent_ref[t] = g_ref[pl.ds(block_start(t, 1 - core), 72), :].astype(BF16)
    pltpu.make_async_copy(sent_ref, send_hbm, send_sem).start()


def inner(hi_hbm, tgt_hbm, w_ref, e_ref, kh_hbm, x3_hbm, ha_hbm, tgw_hbm, x3_ref, ha_ref, tgw_ref, hi_v, tgt_v, kh_ref, sem):
    fetch = [
        pltpu.make_async_copy(src, dst, sem.at[n])
        for n, (src, dst) in enumerate(((hi_hbm, hi_v), (kh_hbm, kh_ref), (tgt_hbm, tgt_v)))
    ]
    for copy in fetch:
        copy.start()
    leave = [
        pltpu.make_async_copy(src, dst, sem.at[3 + n])
        for n, (src, dst) in enumerate(((x3_ref, x3_hbm), (tgw_ref, tgw_hbm), (ha_ref, ha_hbm)))
    ]
    fetch[0].wait()

    def widen_rows(t, _):
        rows = pl.ds(pl.multiple_of(t * 8, 8), 8)
        wide = widen_hi(hi_v[rows].astype(F32), w_ref[rows].astype(F32), e_ref[rows].astype(F32))
        put3(x3_ref, pl.multiple_of(t * 256, 128), wide.reshape(256, C))
        return 0

    lax.fori_loop(0, 6, widen_rows, 0, unroll=True)
    leave[0].start()
    fetch[1].wait()
    fetch[2].wait()

    def widen_targets(t, _):
        rows = pl.ds(pl.multiple_of(t * 8, 8), 8)
        wide = widen_tgt(tgt_v[rows].astype(F32), w_ref[rows].astype(F32), e_ref[rows].astype(F32))
        tgw_ref[pl.ds(pl.multiple_of(t * 256, 128), 256), :] = wide.reshape(256, C).astype(BF16)
        return 0

    def conv(b, _):
        s = pl.multiple_of(b * 736, 32)
        ha_ref[pl.ds(s, 736), :] = jnp.maximum(
            jnp.dot(window(x3_ref, s, 736, WW), kh_ref[...], preferred_element_type=F32), 0.0
        ).astype(BF16)
        return 0

    lax.fori_loop(0, 6, widen_targets, 0, unroll=True)
    lax.fori_loop(0, 2, conv, 0, unroll=True)
    leave[1].start()
    leave[2].start()
    for copy in leave:
        copy.wait()


def main(
    land_ref, low_hbm, w_ref, e_ref, n_ref, s_ref, x3_hbm, ha_hbm, tgw_hbm, kh_hbm, kl_hbm, kj_hbm,
    keep_hbm, send_hbm,
    x3_ref, j3_ref, o3_ref, l3_ref, ha_ref, la_ref, og_ref, tg_ref, jg_ref, lg_ref, g_ref, sent_ref, up_ref,
    low_v, kh_ref, kl_ref, kj_ref, kt_ref, sem, keep_sem, send_sem,
):
    fetch = [
        pltpu.make_async_copy(src, dst, sem.at[n])
        for n, (src, dst) in enumerate(
            (
                (low_hbm, low_v),
                (kl_hbm, kl_ref),
                (kh_hbm, kh_ref),
                (x3_hbm, x3_ref.at[128:1664]),
                (ha_hbm, ha_ref.at[128:1600]),
                (kj_hbm, kj_ref),
                (tgw_hbm, tg_ref.at[64:1600]),
            )
        )
    ]
    for copy in fetch:
        copy.start()
    fetch_low, fetch_kl, fetch_kh, fetch_x3, fetch_ha, fetch_kj, fetch_tgt = fetch
    lat = lax.axis_index(LAT)
    core = lax.axis_index("core")
    first = lat == 0
    last = lat == 7
    up_ref[...] = up_matrix()

    put3(l3_ref, 0, n_ref[192:240, :].astype(F32))
    put3(l3_ref, 304, s_ref[192:240, :].astype(F32))
    put3(x3_ref, 0, n_ref[0:128, :].astype(F32))
    put3(x3_ref, 1664, s_ref[0:128, :].astype(F32))
    tg_ref[0:64, :] = n_ref[128:192, :]
    tg_ref[1600:1664, :] = s_ref[128:192, :]
    zero_at(first, l3_ref, 0, 48)
    zero_at(last, l3_ref, 304, 48)
    zero_at(first, x3_ref, 0, 128)
    zero_at(last, x3_ref, 1664, 128)

    def lands_of(ref):
        rows = ref[192:240, :].astype(F32)
        pairs = [rows[16 * n + 14 : 16 * n + 16] for n in range(3)]
        return land_columns(*[pair[0:1] * 32.0 + pair[1:2] for pair in pairs])

    top = lands_of(n_ref)
    bot = lands_of(s_ref)
    mid = land_columns(
        w_ref[0, 6:7, :].astype(F32) * 32.0 + w_ref[1, 6:7, :].astype(F32),
        land_ref[0, 0].astype(F32),
        e_ref[0, 6:7, :].astype(F32) * 32.0 + e_ref[1, 6:7, :].astype(F32),
    )
    fetch_low.wait()
    put3(
        l3_ref,
        48,
        widen_low(low_v[...].astype(F32), w_ref[...].astype(F32), e_ref[...].astype(F32)).reshape(256, C),
    )
    fetch_kl.wait()
    la_ref[...] = jnp.maximum(
        jnp.dot(window(l3_ref, 0, 320, LWW), kl_ref[...], preferred_element_type=F32), 0.0
    ).astype(BF16)
    zero_at(first, la_ref, 0, 32)
    zero_at(last, la_ref, 288, 32)
    fetch_kh.wait()
    fetch_x3.wait()
    fetch_ha.wait()
    edges = jnp.concatenate([window(x3_ref, 0, 128, WW), window(x3_ref, 1600, 128, WW)], axis=0)
    act = jnp.maximum(jnp.dot(edges, kh_ref[...], preferred_element_type=F32), 0.0).astype(BF16)
    ha_ref[0:128, :] = act[0:128]
    ha_ref[1600:1728, :] = act[128:256]

    def high(b, _):
        s = pl.multiple_of(b * 576, 64)
        cells = la_ref[pl.ds(pl.multiple_of(b * 96, 32), 128), :]
        lift = jnp.dot(up_ref[...], cells, preferred_element_type=F32) * NINTH
        put3(j3_ref, s, ha_ref[pl.ds(s, 576), :].astype(F32) + lift)
        return 0

    lax.fori_loop(0, 3, high, 0, unroll=True)
    zero_at(first, j3_ref, 0, 96)
    zero_at(last, j3_ref, 51 * WW, 96)
    fetch_kj.wait()
    fetch_tgt.wait()

    def join(b, _):
        s = pl.multiple_of(b * 832, 32)
        y = jnp.dot(window(j3_ref, s, 832, WW), kj_ref[...], preferred_element_type=F32)
        diff = (y - tg_ref[pl.ds(s, 832), :].astype(F32)).reshape(26, WW, C)
        row = lax.broadcasted_iota(jnp.int32, (26, WW, C), 0) + b * 26
        weight = jnp.where(row < 2, top, jnp.where(row >= 50, bot, mid))
        grad = (weight * diff).reshape(832, C)
        put3(o3_ref, s, grad)
        og_ref[pl.ds(s, 832), :] = jnp.where(own_columns(832), grad, 0.0).astype(BF16)
        return 0

    lax.fori_loop(0, 2, join, 0, unroll=True)
    zero_at(first, o3_ref, 0, 64)
    zero_at(last, o3_ref, 50 * WW, 64)
    contract(j3_ref, og_ref[64:1600, :], 64, WW, 1536, g_ref.at[2])
    hand_out(g_ref.at[2], keep_hbm.at[2], sent_ref.at[2], send_hbm.at[2], core, keep_sem.at[2], send_sem.at[2])
    for tap in range(9):
        kt_ref[(8 - tap) * C : (9 - tap) * C, :] = kj_ref[tap * C : (tap + 1) * C, :].T

    def back(b, _):
        s = pl.multiple_of(b * 800, 32)
        y = jnp.dot(window(o3_ref, s, 800, WW), kt_ref[...], preferred_element_type=F32)
        jg_ref[pl.ds(s, 800), :] = y.astype(BF16)
        on = ha_ref[pl.ds(pl.multiple_of(s + 64, 32), 800), :].astype(F32) > 0
        og_ref[pl.ds(s, 800), :] = jnp.where(own_columns(800) & on, y, 0.0).astype(BF16)
        return 0

    lax.fori_loop(0, 2, back, 0, unroll=True)
    zero_at(first, jg_ref, 0, 32)
    zero_at(last, jg_ref, 49 * WW, 32)
    contract(x3_ref, og_ref[32:1568, :], 96, WW, 1536, g_ref.at[0])
    hand_out(g_ref.at[0], keep_hbm.at[0], sent_ref.at[0], send_hbm.at[0], core, keep_sem.at[0], send_sem.at[0])
    down = down_matrix()
    for b in range(2):
        lifted = jnp.dot(down, jg_ref[b * 768 : b * 768 + 832, :], preferred_element_type=F32) * NINTH
        on = la_ref[32 + b * 128 : 160 + b * 128, :].astype(F32) > 0
        lg_ref[b * 128 : (b + 1) * 128, :] = jnp.where(on, lifted, 0.0).astype(BF16)
    contract(l3_ref, lg_ref[...], 32, LWW, 256, g_ref.at[1])
    hand_out(g_ref.at[1], keep_hbm.at[1], sent_ref.at[1], send_hbm.at[1], core, keep_sem.at[1], send_sem.at[1])
    for n in range(3):
        pltpu.make_async_copy(g_ref.at[n, 0:1152], keep_hbm.at[n], keep_sem.at[n]).wait()
        pltpu.make_async_copy(sent_ref.at[n], send_hbm.at[n], send_sem.at[n]).wait()


def merge(keep_hbm, recv_ref, out_ref, keep_ref, sem):
    copies = [
        pltpu.make_async_copy(keep_hbm.at[n, pl.ds(8 * xl, 8)], keep_ref.at[n, pl.ds(8 * xl, 8)], sem.at[2 * n + xl])
        for n in range(3)
        for xl in range(2)
    ]
    for copy in copies:
        copy.start()
    quarter = lax.broadcasted_iota(jnp.int32, (72, 128), 1) // 32
    for n in range(3):
        for xl in range(2):
            copies[2 * n + xl].wait()

            def one(p, _):
                for h in range(2):
                    lanes = slice(h * 128, (h + 1) * 128)
                    parts = []
                    for g in range(4):
                        at = xl * 8 + 2 * g + p
                        v = keep_ref[n, at, :, lanes] + recv_ref[n, at, :, lanes].astype(F32)
                        parts.append(pltpu.roll(v, 32 * g, 1) if g else v)
                    for q in range(4):
                        out = parts[(3 - q) % 4]
                        for s in range(3):
                            out = jnp.where(quarter == s, parts[(s - q) % 4], out)
                        out_ref[(h * 4 + q) * 4 + 2 * xl + p, n] = out.astype(BF16)
                return 0

            lax.fori_loop(0, 2, one, 0, unroll=True)


def total(in_ref, out_ref):
    quarter = lax.broadcasted_iota(jnp.int32, (56, 128), 1) // 32
    mine = lax.axis_index(LAT) % 4
    sums = []
    for n in range(3):
        acc = in_ref[0, n].astype(F32)
        for i in range(1, 32):
            acc = acc + in_ref[i, n].astype(F32)
        sums.append(acc)
    rows = jnp.concatenate(sums + [jnp.zeros((8, 128), F32)], axis=0)
    for at in range(4):
        out = None
        for s in range(4):
            shift = ((s - at) * 32) % 128
            part = rows[s * 56 : (s + 1) * 56]
            turned = pltpu.roll(part, shift, 1) if shift else part
            out = turned if out is None else jnp.where(quarter == s, turned, out)
        out_ref[(at + 4 - mine) % 4] = out


def finish(in_ref, a_ref, b_ref, c_ref):
    acc = in_ref[0].astype(F32)
    for i in range(1, 4):
        acc = acc + in_ref[i].astype(F32)
    rows = jnp.concatenate(
        [acc if s == 0 else pltpu.roll(acc, 128 - 32 * s, 1) for s in range(4)], axis=0
    )
    for g, ref in enumerate((a_ref, b_ref, c_ref)):
        ref[...] = rows[g * 72 : (g + 1) * 72].T[0:32]


def call(kernel, out, specs, scratch=(), outs=None, vmem=None):
    return pl.pallas_call(
        kernel,
        out_shape=tuple(jax.ShapeDtypeStruct(s, d) for s, d in out),
        in_specs=list(specs),
        out_specs=outs or tuple(VMEM for _ in out),
        scratch_shapes=list(scratch),
        compiler_params=pltpu.CompilerParams(vmem_limit_bytes=vmem) if vmem else None,
    )


def ring(count, step):
    return [(i, (i + step) % count) for i in range(count)]


FIRST = ("yh", "yl", "xh", "xl", "zl")
SECOND = ("zh", "zm")


def step(hi, low, kh, kl, kj, tgt, land):
    dma = pltpu.SemaphoreType.DMA
    west, east, edges = call(
        pack_lon,
        [((H, 8, C), BF16)] * 2 + [((2, 7, W, C), BF16)],
        [SMEM] + [HBM] * 3,
        [pltpu.VMEM((2, H, 8, C), BF16), pltpu.VMEM((2, H, 8, C), BF16), pltpu.VMEM((LH, LW, C), BF16), dma((9,))],
        vmem=LON_LIMIT,
    )(land, hi, tgt, low)
    from_e = lax.ppermute(west, LON, ring(32, -1))
    from_w = lax.ppermute(east, LON, ring(32, 1))
    north, south = call(pack_lat, [((PK, C), BF16)] * 2, [SMEM] + [VMEM] * 3, vmem=6 * MIB)(land, edges, from_w, from_e)
    from_s = lax.ppermute(north, LAT, ring(8, -1))
    from_n = lax.ppermute(south, LAT, ring(8, 1))
    weights = [k.reshape(9 * C, C) for k in (kh, kl, kj)]
    saved = call(
        inner,
        [((1536, 768), BF16), ((1472, C), BF16), ((1536, C), BF16)],
        [HBM] * 2 + [VMEM] * 2 + [HBM],
        [
            pltpu.VMEM((1536, 768), BF16),
            pltpu.VMEM((1472, C), BF16),
            pltpu.VMEM((1536, C), BF16),
            pltpu.VMEM((H, W, C), BF16),
            pltpu.VMEM((H, W, C), BF16),
            pltpu.VMEM((2304, C), BF16),
            dma((6,)),
        ],
        outs=(HBM,) * 3,
        vmem=MAIN_LIMIT,
    )(hi, tgt, from_w, from_e, weights[0])
    keep, send = call(
        main,
        [((3, 16, 72, C), F32), ((3, 16, 72, C), BF16)],
        [SMEM] + [HBM] + [VMEM] * 4 + [HBM] * 6,
        [
            pltpu.VMEM((1792, 768), BF16),
            pltpu.VMEM((1728, 768), BF16),
            pltpu.VMEM((1664, 768), BF16),
            pltpu.VMEM((352, 768), BF16),
            pltpu.VMEM((1728, C), BF16),
            pltpu.VMEM((320, C), BF16),
            pltpu.VMEM((1664, C), BF16),
            pltpu.VMEM((1664, C), BF16),
            pltpu.VMEM((1600, C), BF16),
            pltpu.VMEM((256, C), BF16),
            pltpu.VMEM((3, 2304, C), F32),
            pltpu.VMEM((3, 16, 72, C), BF16),
            pltpu.VMEM((576, 128), BF16),
            pltpu.VMEM((LH, LW, C), BF16),
            pltpu.VMEM((2304, C), BF16),
            pltpu.VMEM((2304, C), BF16),
            pltpu.VMEM((2304, C), BF16),
            pltpu.VMEM((2304, C), BF16),
            dma((7,)),
            dma((3,)),
            dma((3,)),
        ],
        outs=(HBM, HBM),
        vmem=MAIN_LIMIT,
    )(land, low, from_w, from_e, from_n, from_s, *saved, *weights)
    recv = lax.ppermute(send, "core", ring(2, 1))
    (parts,) = call(
        merge, [((32, 3, 72, 128), BF16)], [HBM, VMEM], [pltpu.VMEM((3, 16, 72, C), F32), dma((6,))], vmem=MERGE_LIMIT
    )(keep, recv)
    parts = lax.all_to_all(parts, FIRST, 0, 0, tiled=True)
    (parts,) = call(total, [((4, 56, 128), F32)], [VMEM], vmem=6 * MIB)(parts)
    parts = lax.all_to_all(parts, SECOND, 0, 0, tiled=True)
    grads = call(finish, [((32, 72), F32)] * 3, [VMEM], vmem=2 * MIB)(parts)
    return tuple(g.T for g in grads)


def solution(mesh):
    fine = Mesh(mesh.devices.reshape((2,) * 8), LAT + LON)
    tile = P(LAT, LON, None)
    return jax.shard_map(
        step,
        mesh=fine,
        in_specs=(tile, tile, P(), P(), P(), tile, P(LAT, LON)),
        out_specs=(P(LON, LAT),) * 3,
        check_vma=False,
    )
```
